256 devices in a mesh: row: 16 (over x_hi, z), col: 16 (over y, x_lo, core).
Axes of the slice: x: 4 (x_hi: 2, x_lo: 2; x = x_hi * 2 + x_lo), y: 4, z: 8, core: 2. Of those that a mesh axis runs over, the one named last changes fastest.
Arguments:
- objective: float32 [256, 32768], P('row', 'col'), may hold values from -6 to 6
- center: bfloat16 [256, 32768], P('row', 'col'), may hold values from -5 to 5
- radius: bfloat16 [256, 32768], P('row', 'col'), may hold values from 0.049804688 to 1
- lower_gap: bfloat16 [3, 256, 32768], P(None, 'row', 'col'), may hold values from 0.19921875 to 3
- upper_gap: bfloat16 [3, 256, 32768], P(None, 'row', 'col'), may hold values from 0.19921875 to 3
- kernels: float32 [4, 3, 3, 64, 64], replicated, may hold values from -0.25 to 0.25
- biases: float32 [4, 64], replicated, may hold values from -3 to 3
- step_sizes: float32 [3], replicated, may hold values from 0.2 to 1
Outputs:
- bounds: float32 [3], replicated
- final_duals: float32 [3, 256, 32768], P(None, 'row', 'col')
- final_multipliers: float32 [3, 256, 32768], P(None, 'row', 'col')
The draws below stay inside these ranges and needn't reach their ends.
All inputs are finite; a program needn't handle non-finite values.
Results may differ from the reference program's by a relative error of at most 0.0003.
Values sent between devices are 32-bit elements; how exact they have to be, the bound alone decides.
A program may use at most 128 MiB of HBM per device.

```python
import math
import jax
import jax.numpy as jnp
from jax import lax

CH = 64
LAYERS = 4
ITERS = 3
H = 256
W = 512
WC = 32768


def steps_of(rng, extent, split, low, top_value):
    def one(dim, blocks):
        steps = jax.random.uniform(jax.random.fold_in(jax.random.fold_in(rng, 6), dim), (blocks,), jnp.float32, low / len(split), top_value / len(split))
        return jnp.repeat(jnp.exp(steps), extent[dim] // blocks).reshape((-1,) + (1,) * (len(extent) - dim - 1))

    level = one(*split[0])
    for cut in split[1:]:
        level = level * one(*cut)
    return level


def noise(rng, extent, deviation, bound, cuts=(), dtype=jnp.bfloat16):
    gain = steps_of(rng, extent, cuts, -0.22, 0.18) if cuts else 1.0
    entries = jax.random.normal(rng, extent, jnp.float32) * deviation * gain
    return jnp.minimum(jnp.maximum(entries, -bound), bound).astype(dtype)


def setup_inputs(seed: int = 0) -> dict:
    key_of = jax.random.split(jax.random.key(seed), 9)
    objective = noise(key_of[0], (H, WC), 1.0, 6.0, ((0, 16), (1, 16)), jnp.float32)
    center = noise(key_of[1], (H, WC), 1.0, 5.0, ((0, 16), (1, 16)))
    radius = jnp.clip(jnp.exp(math.log(1.0) - 2.9996462 * jax.random.uniform(key_of[2], (H, WC), jnp.float32) ** steps_of(key_of[2], (H, WC), ((0, 16), (1, 16)), -0.2, 0.2)), 0.049804688, 1.0).astype(jnp.bfloat16)
    lower_gap = jnp.clip(jnp.exp(math.log(3.0) - 2.7119641 * jax.random.uniform(key_of[3], (LAYERS - 1, H, WC), jnp.float32) ** steps_of(key_of[3], (LAYERS - 1, H, WC), ((1, 16), (2, 16)), -0.2, 0.2)), 0.19921875, 3.0).astype(jnp.bfloat16)
    upper_gap = jnp.clip(jnp.exp(math.log(3.0) - 2.7119641 * jax.random.uniform(key_of[4], (LAYERS - 1, H, WC), jnp.float32) ** steps_of(key_of[4], (LAYERS - 1, H, WC), ((1, 16), (2, 16)), -0.2, 0.2)), 0.19921875, 3.0).astype(jnp.bfloat16)
    kernels = noise(key_of[5], (LAYERS, 3, 3, CH, CH), (9 * CH) ** -0.5, 0.25, (), jnp.float32)
    biases = noise(key_of[6], (LAYERS, CH), 0.5, 3.0, (), jnp.float32)
    step_sizes = jnp.clip(jnp.exp(jax.random.uniform(key_of[7], (ITERS,), jnp.float32, math.log(0.2), math.log(1.0))), 0.2, 1.0)
    return dict(objective=objective, center=center, radius=radius, lower_gap=lower_gap, upper_gap=upper_gap, kernels=kernels, biases=biases, step_sizes=step_sizes)


TEMP = 0.5
EPS = 1e-06

def soft_value(coef, low, high):
    return coef * low - TEMP * jax.nn.softplus(coef * (low - high) / TEMP)

def soft_point(coef, low, high):
    return low + (high - low) * jax.nn.sigmoid(coef * (low - high) / TEMP)

def flipped(kernel):
    return jnp.transpose(kernel[::-1, ::-1], (0, 1, 3, 2))

def conv_same(maps, kernel):
    result = lax.conv_general_dilated(maps[None], kernel, (1, 1), 'SAME', dimension_numbers=('NHWC', 'HWIO', 'NHWC'), precision=lax.Precision.HIGHEST)
    return result[0]

def reference(objective, center, radius, lower_gap, upper_gap, kernels, biases, step_sizes):
    depth = LAYERS - 1
    target = objective.reshape(H, W, CH)
    middle = center.astype(jnp.float32).reshape(H, W, CH)
    half = radius.astype(jnp.float32).reshape(H, W, CH)
    below = lower_gap.astype(jnp.float32).reshape(depth, H, W, CH)
    above = upper_gap.astype(jnp.float32).reshape(depth, H, W, CH)
    zero_map = jnp.zeros((H, W, CH), jnp.float32)
    lows = [middle - half] + [zero_map] * depth
    highs = [middle + half] + [above[j] for j in range(depth)]
    target_back = conv_same(target, flipped(kernels[LAYERS - 1]))
    fixed_part = jnp.sum(target * biases[LAYERS - 1])
    duals = [zero_map] * depth
    multipliers = [zero_map] * depth
    total_cells = H * W * CH
    bounds = []
    for step in range(ITERS):
        value = fixed_part
        points = []
        for layer in range(LAYERS):
            if layer < depth:
                coef = -conv_same(duals[layer], flipped(kernels[layer]))
            else:
                coef = target_back
            if layer > 0:
                coef = coef + multipliers[layer - 1]
            value = value + jnp.sum(soft_value(coef, lows[layer], highs[layer]))
            points.append(soft_point(coef, lows[layer], highs[layer]))
        slope_duals = []
        slope_mults = []
        squares = jnp.zeros((), jnp.float32)
        for j in range(depth):
            pos_coef = duals[j] - multipliers[j]
            neg_coef = -duals[j]
            value = value + jnp.sum(soft_value(pos_coef, zero_map, above[j]))
            value = value + jnp.sum(soft_value(neg_coef, zero_map, below[j]))
            value = value - jnp.sum(duals[j] * biases[j])
            positive = soft_point(pos_coef, zero_map, above[j])
            negative = soft_point(neg_coef, zero_map, below[j])
            slope_dual = positive - negative - conv_same(points[j], kernels[j]) - biases[j]
            slope_mult = points[j + 1] - positive
            squares = squares + jnp.sum(slope_dual * slope_dual) + jnp.sum(slope_mult * slope_mult)
            slope_duals.append(slope_dual)
            slope_mults.append(slope_mult)
        scale = step_sizes[step] / jnp.sqrt(squares / (2 * depth * total_cells) + EPS)
        duals = [duals[j] + scale * slope_duals[j] for j in range(depth)]
        multipliers = [multipliers[j] + scale * slope_mults[j] for j in range(depth)]
        bounds.append(value / total_cells)
    final_duals = jnp.stack(duals).reshape(depth, H, W * CH)
    final_multipliers = jnp.stack(multipliers).reshape(depth, H, W * CH)
    return (jnp.stack(bounds), final_duals, final_multipliers)
```

```python
import jax
import jax.numpy as jnp
from jax import lax
from jax.experimental import pallas as pl
from jax.experimental.pallas import tpu as pltpu
from jax.sharding import PartitionSpec as P

CH = 64
LAYERS = 4
ITERS = 3
DEPTH = LAYERS - 1
EPS = 1e-06
MESH = pl.DeviceIdType.MESH
F32 = jnp.float32
BF16 = jnp.bfloat16

ROWS = 16
PAIRS = 16
EXT = 24
EPAIRS = 18
WIDE = 32
PLANES = 8
MID, HALF, H1, H2, OBJ, H3, Q1, Q2, Q3 = range(9)
UP, DOWN, LEFT, RIGHT = range(4)
SIDES = ((-1, 0), (1, 0), (0, -1), (0, 1), (-1, -1), (-1, 1), (1, -1), (1, 1))


def at(start, size):
    return pl.ds(pl.multiple_of(start, 8), size)


def inner(which, pair):
    return at((which * PAIRS + pair) * ROWS, ROWS)


def ext(which, pair):
    return at((which * EPAIRS + pair) * EXT, EXT)


def ext_inner(which, pair):
    return pl.ds((which * EPAIRS + pair + 1) * EXT + 1, ROWS)


def softplus(z):
    return jnp.maximum(z, 0.0) + jnp.log1p(jnp.exp(-jnp.abs(z)))


def split(v):
    hi = v.astype(BF16)
    return hi, (v - hi.astype(F32)).astype(BF16)


def body(total_cells, n_row, n_col, obj_h, cen_h, rad_h, low_h, upp_h, ker_h, bia_h, steps,
         bounds_ref, lam_out, mu_out,
         obj_v, cen_v, rad_v, low_v, upp_v, ker_v, bia_v,
         base, wide_in, lam, mu, lam_x, mu_x, dl, dmu, dmu_x, trans, upd, g_x, x_x, p_x, pn, tb, conv_out,
         d_w, y_s, lhs_i, lhs_x, wts,
         rows_s0, cols_s0, diag_s0, rows_r0, cols_r0, diag_r0,
         rows_s, cols_s, diag_s, rows_r, cols_r, diag_r,
         pay_a, buf_a, pay_b, buf_b,
         load_sem, halo_send, halo_recv, a_send, a_recv, b_send, b_recv):
    row = lax.axis_index("row")
    col = lax.axis_index("col")
    x_hi = row // PLANES
    z = row % PLANES
    n_plane = (n_row // PLANES) * n_col
    place = x_hi * n_col + col

    def plane_device(slot):
        return ((slot // n_col) * PLANES + z, slot % n_col)

    def side_device(side):
        return ((row + side[0] + n_row) % n_row, (col + side[1] + n_col) % n_col)

    loads = []
    for n, (src, dst) in enumerate(((cen_h, cen_v), (rad_h, rad_v), (upp_h, upp_v), (obj_h, obj_v),
                                    (ker_h, ker_v), (low_h, low_v), (bia_h, bia_v))):
        copy = pltpu.make_async_copy(src, dst, load_sem.at[n])
        copy.start()
        loads.append(copy)

    barrier = pltpu.get_barrier_semaphore()
    greeted = 0
    for d in range(1, n_plane):
        pl.semaphore_signal(barrier, inc=1, device_id=plane_device((place + d) % n_plane), device_id_type=MESH)
        greeted += 1
    for d in range(1, PLANES):
        pl.semaphore_signal(barrier, inc=1, device_id=(x_hi * PLANES + (z + d) % PLANES, col), device_id_type=MESH)
        greeted += 1
    for side in SIDES:
        if side[0] != 0:
            pl.semaphore_signal(barrier, inc=1, device_id=side_device(side), device_id_type=MESH)
            greeted += 1

    zero_tile = jnp.zeros((8, 128), F32)

    def halo_start(n, src_ref, maps, deep, bufs):
        rows_src, cols_src, diag_src, rows_dst, cols_dst, diag_dst = bufs
        for m in range(maps):
            first = m * PAIRS * ROWS
            for r in range(deep):
                rows_src[UP, m, r] = src_ref[pl.ds(first + r, PAIRS, stride=ROWS), :]
                rows_src[DOWN, m, r] = src_ref[pl.ds(first + ROWS - deep + r, PAIRS, stride=ROWS), :]
            cols_src[0, m] = src_ref[first : first + ROWS, :]
            cols_src[1, m] = src_ref[first + (PAIRS - 1) * ROWS : first + PAIRS * ROWS, :]
            last = first + (PAIRS - 1) * ROWS
            diag_src[0, m] = src_ref[first : first + deep, :]
            diag_src[1, m] = src_ref[last : last + deep, :]
            diag_src[2, m] = src_ref[first + ROWS - deep : first + ROWS, :]
            diag_src[3, m] = src_ref[last + ROWS - deep : last + ROWS, :]
        copies = []
        for s in (4, 5, 6, 7, 0, 1, 2, 3):
            if s < 2:
                src, dst = rows_src.at[s], rows_dst.at[s]
            elif s < 4:
                src, dst = cols_src.at[s - 2], cols_dst.at[s - 2]
            else:
                src, dst = diag_src.at[s - 4], diag_dst.at[s - 4]
            copy = pltpu.make_async_remote_copy(
                src_ref=src, dst_ref=dst, send_sem=halo_send.at[n, s], recv_sem=halo_recv.at[n, s],
                device_id=side_device(SIDES[s]), device_id_type=MESH)
            copy.start()
            copies.append(copy)
        return copies

    no_above = row == 0
    no_below = row == n_row - 1
    no_left = col == 0
    no_right = col == n_col - 1

    def halo_place(dst_ref, maps, deep, tall, top, bufs):
        _, _, _, rows_dst, cols_dst, diag_dst = bufs

        def cut(gone, v):
            return jnp.where(gone, 0.0, v)

        for m in range(maps):
            first = m * EPAIRS * tall
            last = first + (EPAIRS - 1) * tall
            for r in range(deep):
                dst_ref[pl.ds(first + tall + top + ROWS + r, PAIRS, stride=tall), :] = cut(
                    no_below, rows_dst[0, m, r])
                dst_ref[pl.ds(first + tall + top - deep + r, PAIRS, stride=tall), :] = cut(
                    no_above, rows_dst[1, m, r])
            dst_ref[last + top : last + top + ROWS, :] = cut(no_right, cols_dst[0, m])
            dst_ref[first + top : first + top + ROWS, :] = cut(no_left, cols_dst[1, m])
            dst_ref[last + top + ROWS : last + top + ROWS + deep, :] = cut(
                jnp.logical_or(no_below, no_right), diag_dst[0, m])
            dst_ref[first + top + ROWS : first + top + ROWS + deep, :] = cut(
                jnp.logical_or(no_below, no_left), diag_dst[1, m])
            dst_ref[last + top - deep : last + top, :] = cut(
                jnp.logical_or(no_above, no_right), diag_dst[2, m])
            dst_ref[first + top - deep : first + top, :] = cut(
                jnp.logical_or(no_above, no_left), diag_dst[3, m])

    sends = []

    def sum_start(n, first_row, second_row):
        pay_a[n, 0:1] = first_row
        pay_a[n, 1:2] = second_row
        buf_a[n, place, 0:1] = first_row
        buf_a[n, place, 1:2] = second_row
        for d in range(1, n_plane):
            pltpu.make_async_remote_copy(
                src_ref=pay_a.at[n], dst_ref=buf_a.at[n, place], send_sem=a_send.at[n], recv_sem=a_recv.at[n],
                device_id=plane_device((place + d) % n_plane), device_id_type=MESH).start()

    def whole(buf, n, count, send, recv):
        part = buf.at[n, 0:count]
        return pltpu.make_async_remote_copy(
            src_ref=part, dst_ref=part, send_sem=send.at[n], recv_sem=recv.at[n],
            device_id=side_device((0, 1)), device_id_type=MESH)

    def sum_middle(n):
        whole(buf_a, n, n_plane - 1, a_send, a_recv).wait_recv()
        part = jnp.sum(buf_a[n], axis=0)
        pay_b[n] = part
        buf_b[n, z] = part
        for d in range(1, PLANES):
            pltpu.make_async_remote_copy(
                src_ref=pay_b.at[n], dst_ref=buf_b.at[n, z], send_sem=b_send.at[n], recv_sem=b_recv.at[n],
                device_id=(x_hi * PLANES + (z + d) % PLANES, col), device_id_type=MESH).start()

    def sum_end(n):
        whole(buf_b, n, PLANES - 1, b_send, b_recv).wait_recv()
        return jnp.sum(buf_b[n], axis=0)

    lane = lax.broadcasted_iota(jnp.int32, (EXT, 128), 1) < CH
    lane_w = lax.broadcasted_iota(jnp.int32, (WIDE, 128), 1) < CH

    def windows(src_ref, which, slot):
        def step(t, carry):
            a = pltpu.roll(src_ref[ext(which, t), :], CH, 1)
            b = pltpu.roll(src_ref[ext(which, t + 1), :], CH, 1)
            y_s[at((slot * EPAIRS + t) * EXT, EXT), :] = jnp.where(lane, a, b)
            for dh in range(3):
                hi, lo = split(y_s[pl.ds((slot * EPAIRS + t) * EXT + dh, ROWS), :])
                lhs_i[slot, 0, dh, pl.ds(pl.multiple_of(t * ROWS, ROWS), ROWS), :] = hi
                lhs_i[slot, 1, dh, pl.ds(pl.multiple_of(t * ROWS, ROWS), ROWS), :] = lo
            return carry
        lax.fori_loop(0, PAIRS + 1, step, 0)

    def conv(slot, weight):
        size = PAIRS * ROWS
        halves = []
        for part in range(2):
            tiles = []
            for dh in range(3):
                tiles.append(lhs_i[slot, part, dh, 0:size, :])
                tiles.append(lhs_i[slot, part, dh, ROWS : size + ROWS, :])
            halves.append(jnp.concatenate(tiles, axis=1))
        out = jnp.dot(jnp.concatenate(halves, axis=0), wts[weight], preferred_element_type=F32)
        total = (out[size:, 128:] + out[size:, :128]) + out[:size, 128:] + out[:size, :128]
        conv_out[at(slot * size, size), :] = total

    def windows_wide(m):
        first = m * EPAIRS * WIDE
        ybase = 0

        def form(t, left, right):
            y_s[at(ybase + t * WIDE, WIDE), :] = jnp.where(lane_w, left, right)

        def turned(p):
            return pltpu.roll(d_w[at(first + p * WIDE, WIDE), :], CH, 1)

        none = jnp.zeros((WIDE, 128), F32)
        form(0, none, turned(0))
        form(EPAIRS, turned(EPAIRS - 1), none)

        def step(t, carry):
            form(t, turned(t - 1), turned(t))
            return carry
        lax.fori_loop(1, EPAIRS, step, 0)

        def cast(t, carry):
            for dh in range(3):
                ys = [y_s[pl.ds(ybase + (2 * t + i) * WIDE + dh, EXT), :] for i in range(3)]
                for half in range(2):
                    hi, lo = split(jnp.concatenate([ys[half], ys[half + 1]], axis=0))
                    rows = pl.ds(pl.multiple_of(t * 2 * EXT, 16), 2 * EXT)
                    lhs_x[0, rows, (dh * 2 + half) * 128 : (dh * 2 + half + 1) * 128] = hi
                    lhs_x[1, rows, (dh * 2 + half) * 128 : (dh * 2 + half + 1) * 128] = lo
            return carry
        lax.fori_loop(0, EPAIRS // 2, cast, 0)

    def conv_wide(m):
        size = EPAIRS * EXT
        for part in range(2):
            out = jnp.dot(lhs_x[part], wts[3 + m], preferred_element_type=F32)
            total = out[:, 128:] + out[:, :128]
            if part == 0:
                upd[at(m * size, size), :] = total
            else:
                upd[at(m * size, size), :] += total

    for n in range(4):
        loads[n].wait()

    def fill(j, carry):
        lanes = pl.ds(pl.multiple_of(j * 128, 128), 128)
        c = cen_v[:, lanes].astype(F32)
        r = rad_v[:, lanes].astype(F32)
        lo, hi = c - r, c + r
        vals = {MID: 0.5 * (hi + lo), HALF: 0.5 * (hi - lo), OBJ: obj_v[:, lanes]}
        for m, name in enumerate((H1, H2, H3)):
            vals[name] = 0.5 * upp_v[m, :, lanes].astype(F32)
        for name, v in vals.items():
            base[inner(name, j), :] = v
            if name <= OBJ:
                wide_in[at((name * EPAIRS + j + 1) * EXT, 8), :] = zero_tile
                wide_in[at((name * EPAIRS + j + 1) * EXT + 16, 8), :] = zero_tile
                wide_in[ext_inner(name, j), :] = v
        return carry
    lax.fori_loop(0, PAIRS, fill, 0)
    for m in range(5):
        for e in (0, EPAIRS - 1):
            wide_in[ext(m, e), :] = jnp.zeros((EXT, 128), F32)

    pl.semaphore_wait(barrier, greeted)
    bufs0 = (rows_s0, cols_s0, diag_s0, rows_r0, cols_r0, diag_r0)
    first_copies = halo_start(0, base, 5, 1, bufs0)
    sends += first_copies

    for n in range(4, 7):
        loads[n].wait()

    def fill_low(j, carry):
        lanes = pl.ds(pl.multiple_of(j * 128, 128), 128)
        for m, name in enumerate((Q1, Q2, Q3)):
            base[inner(name, j), :] = 0.5 * low_v[m, :, lanes].astype(F32)
        return carry
    lax.fori_loop(0, PAIRS, fill_low, 0)

    bias = jnp.concatenate([bia_v[...], bia_v[...]], axis=1)
    none64 = jnp.zeros((CH, CH), F32)

    def put_weight(slot, dh, block):
        hi, lo = split(block)
        wts[slot, dh * 256 : (dh + 1) * 256, 0:128] = hi
        wts[slot, dh * 256 : (dh + 1) * 256, 128:256] = lo

    def build(k, carry):
        for dh in range(3):
            taps = [ker_v[k, 2 - dh, dw] for dw in range(3)]
            one = jnp.concatenate([jnp.concatenate([taps[2], taps[1]], axis=1),
                                   jnp.concatenate([none64, taps[2]], axis=1)], axis=0)
            two = jnp.concatenate([jnp.concatenate([taps[0], none64], axis=1),
                                   jnp.concatenate([taps[1], taps[0]], axis=1)], axis=0)
            put_weight(3 + k, dh, jnp.concatenate([one.T, two.T], axis=0))
        return carry
    lax.fori_loop(0, LAYERS, build, 0)

    def build_forward(k, carry):
        for dh in range(3):
            taps = [ker_v[k, dh, dw] for dw in range(3)]
            put_weight(k, dh, jnp.concatenate(
                [jnp.concatenate(taps + [none64], axis=0), jnp.concatenate([none64] + taps, axis=0)], axis=1))
        return carry
    lax.fori_loop(0, DEPTH, build_forward, 0)

    def clear(t, carry):
        d_w[at(t * WIDE, WIDE), :] = jnp.zeros((WIDE, 128), F32)
        return carry
    lax.fori_loop(0, DEPTH * EPAIRS, clear, 0)

    for copy in first_copies:
        copy.wait_recv()
    halo_place(wide_in, 5, 1, EXT, 1, bufs0)

    def value_terms(i, j):
        q = -0.5
        total = base[inner(OBJ, j), :] * bias[DEPTH : DEPTH + 1]
        mid, half = base[inner(MID, j), :], base[inner(HALF, j), :]
        hs = [base[inner(n, j), :] for n in (H1, H2, H3)]
        qs = [base[inner(n, j), :] for n in (Q1, Q2, Q3)]
        t3 = tb[inner(0, j), :]
        if i == 0:
            total += q * softplus(-4.0 * hs[2] * t3)
            return total
        g0 = g_x[ext_inner(0, j), :]
        total += g0 * (mid - half) + q * softplus(-4.0 * half * g0)
        lams = [lam_x[ext_inner(0, j), :], lam_x[ext_inner(1, j), :], lam[inner(0, j), :]]
        mus = [mu_x[ext_inner(0, j), :], mu_x[ext_inner(1, j), :], mu[inner(0, j), :]]
        for m in range(DEPTH):
            g = g_x[ext_inner(m + 1, j), :] if m < 2 else mus[2] + t3
            total += q * softplus(-4.0 * hs[m] * g)
            total += q * softplus(-4.0 * hs[m] * (lams[m] - mus[m]))
            total += q * softplus(4.0 * qs[m] * lams[m])
            total -= lams[m] * bias[m : m + 1]
        return total

    def value_row(i):
        def step(j, acc):
            return acc + value_terms(i, j)
        acc = lax.fori_loop(0, PAIRS, step, jnp.zeros((ROWS, 128), F32))
        out = jnp.sum(acc, axis=0, keepdims=True)
        if i == 0:
            out = out - (0.5 * 0.6931471805599453 * 9 * ROWS * PAIRS)
        return out

    scale = None
    value_prev = jnp.zeros((1, 128), F32)
    totals = []
    for i in range(ITERS):
        if i == 0:
            def start_x(e, carry):
                xs = [wide_in[ext(MID, e), :], wide_in[ext(H1, e), :], wide_in[ext(H2, e), :]]
                for k in range(DEPTH):
                    x_x[ext(k, e), :] = xs[k]
                for m in range(2):
                    p_x[ext(m, e), :] = xs[m + 1]
                    dmu_x[ext(m, e), :] = x_x[ext(m + 1, e), :] - p_x[ext(m, e), :]
                return carry
            lax.fori_loop(0, EPAIRS, start_x, 0)
            windows(wide_in, OBJ, 3)
            conv(3, 3 + DEPTH)

            def start_inner(j, carry):
                t3 = conv_out[inner(3, j), :]
                tb[inner(0, j), :] = t3
                hs = [base[inner(n, j), :] for n in (H1, H2, H3)]
                qs = [base[inner(n, j), :] for n in (Q1, Q2, Q3)]
                dmu[inner(0, j), :] = (hs[2] - hs[2] * jnp.tanh(2.0 * hs[2] * t3)) - hs[2]
                for m in range(DEPTH):
                    pn[inner(m, j), :] = hs[m] - qs[m] - bias[m : m + 1]
                return carry
            lax.fori_loop(0, PAIRS, start_inner, 0)
        else:
            first = i == 1

            def step_x(e, carry):
                halfs = [wide_in[ext(n, e), :] for n in (HALF, H1, H2)]
                mids = [wide_in[ext(MID, e), :], halfs[1], halfs[2]]
                xs = []
                mus = []
                for m in range(2):
                    new_mu = scale * dmu_x[ext(m, e), :]
                    new_lam = scale * d_w[pl.ds((m * EPAIRS + e) * WIDE + 1, EXT), :]
                    if not first:
                        new_mu = mu_x[ext(m, e), :] + new_mu
                        new_lam = lam_x[ext(m, e), :] + new_lam
                    mu_x[ext(m, e), :] = new_mu
                    lam_x[ext(m, e), :] = new_lam
                    mus.append((new_mu, new_lam))
                for k in range(DEPTH):
                    t = scale * upd[ext(k, e), :]
                    if not first:
                        t = trans[ext(k, e), :] + t
                    trans[ext(k, e), :] = t
                    g = -t if k == 0 else mus[k - 1][0] - t
                    g_x[ext(k, e), :] = g
                    x = mids[k] - halfs[k] * jnp.tanh(2.0 * halfs[k] * g)
                    x_x[ext(k, e), :] = x
                    xs.append(x)
                for m in range(2):
                    h = halfs[m + 1]
                    p = h - h * jnp.tanh(2.0 * h * (mus[m][1] - mus[m][0]))
                    p_x[ext(m, e), :] = p
                    dmu_x[ext(m, e), :] = xs[m + 1] - p
                return carry
            lax.fori_loop(0, EPAIRS, step_x, 0)

            def step_inner(j, carry):
                hs2 = base[inner(H3, j), :]
                qs = [base[inner(n, j), :] for n in (Q1, Q2, Q3)]
                new_mu = scale * dmu[inner(0, j), :]
                new_lam = scale * dl[inner(2, j), :]
                if not first:
                    new_mu = mu[inner(0, j), :] + new_mu
                    new_lam = lam[inner(0, j), :] + new_lam
                mu[inner(0, j), :] = new_mu
                lam[inner(0, j), :] = new_lam
                lams = [lam_x[ext_inner(0, j), :], lam_x[ext_inner(1, j), :], new_lam]
                p3 = hs2 - hs2 * jnp.tanh(2.0 * hs2 * (new_lam - new_mu))
                ps = [p_x[ext_inner(0, j), :], p_x[ext_inner(1, j), :], p3]
                g3 = new_mu + tb[inner(0, j), :]
                dmu[inner(0, j), :] = (hs2 - hs2 * jnp.tanh(2.0 * hs2 * g3)) - p3
                for m in range(DEPTH):
                    n = qs[m] + qs[m] * jnp.tanh(2.0 * qs[m] * lams[m])
                    pn[inner(m, j), :] = ps[m] - n - bias[m : m + 1]
                return carry
            lax.fori_loop(0, PAIRS, step_inner, 0)

        for k in range(DEPTH):
            windows(x_x, k, k)
            conv(k, k)

        def step_slope(j, acc):
            for m in range(DEPTH):
                v = pn[inner(m, j), :] - conv_out[inner(m, j), :]
                dl[inner(m, j), :] = v
                d_w[pl.ds((m * EPAIRS + j + 1) * WIDE + 2, ROWS), :] = v
                acc = acc + v * v
            for m in range(2):
                v = dmu_x[ext_inner(m, j), :]
                acc = acc + v * v
            v = dmu[inner(0, j), :]
            return acc + v * v
        acc = lax.fori_loop(0, PAIRS, step_slope, jnp.zeros((ROWS, 128), F32))
        sum_start(i, jnp.sum(acc, axis=0, keepdims=True), value_prev)

        copies = []
        if i < ITERS - 1:
            bufs = tuple(ref.at[i] for ref in (rows_s, cols_s, diag_s, rows_r, cols_r, diag_r))
            copies = halo_start(1 + i, dl, DEPTH, 2, bufs)
            sends += copies
        value_prev = value_row(i)
        sum_middle(i)
        if i < ITERS - 1:
            for copy in copies:
                copy.wait_recv()
            halo_place(d_w, DEPTH, 2, WIDE, 2, bufs)
            for m in range(DEPTH):
                windows_wide(m)
                conv_wide(m)
        else:
            sum_start(ITERS, jnp.zeros((1, 128), F32), value_prev)
        both = sum_end(i)
        squares = jnp.sum(both[0:1], axis=1, keepdims=True)
        scale = steps[i] / jnp.sqrt(squares / (2 * DEPTH * total_cells) + EPS)
        scale = jnp.broadcast_to(scale, (1, 128))
        totals.append(both)

    def finish(j, carry):
        lanes = pl.ds(pl.multiple_of(j * 128, 128), 128)
        for m in range(2):
            lam_out[m, :, lanes] = lam_x[ext_inner(m, j), :] + scale * dl[inner(m, j), :]
            mu_out[m, :, lanes] = mu_x[ext_inner(m, j), :] + scale * dmu_x[ext_inner(m, j), :]
        lam_out[2, :, lanes] = lam[inner(0, j), :] + scale * dl[inner(2, j), :]
        mu_out[2, :, lanes] = mu[inner(0, j), :] + scale * dmu[inner(0, j), :]
        return carry
    lax.fori_loop(0, PAIRS, finish, 0)
    sum_middle(ITERS)
    totals.append(sum_end(ITERS))
    for i in range(ITERS):
        bounds_ref[i] = jnp.sum(totals[i + 1][1:2]) / total_cells

    for copy in sends:
        copy.wait_send()
    for n in range(ITERS + 1):
        whole(buf_a, n, n_plane - 1, a_send, a_recv).wait_send()
        whole(buf_b, n, PLANES - 1, b_send, b_recv).wait_send()


def solution(mesh):
    n_row, n_col = mesh.shape["row"], mesh.shape["col"]
    n_plane = (n_row // PLANES) * n_col
    total_cells = n_row * n_col * ROWS * PAIRS * 128

    def vm(*shape, dtype=F32):
        return pltpu.VMEM(shape, dtype)

    inner_rows = PAIRS * ROWS
    ext_rows = EPAIRS * EXT
    lanes = PAIRS * 128
    any_spec = pl.BlockSpec(memory_space=pl.ANY)

    def kernel(*refs):
        body(float(total_cells), n_row, n_col, *refs)

    def shards(*args):
        call = pl.pallas_call(
            kernel,
            out_shape=(jax.ShapeDtypeStruct((ITERS,), F32),
                       jax.ShapeDtypeStruct((DEPTH, ROWS, lanes), F32),
                       jax.ShapeDtypeStruct((DEPTH, ROWS, lanes), F32)),
            in_specs=[any_spec] * 7 + [pl.BlockSpec(memory_space=pltpu.SMEM)],
            out_specs=(pl.BlockSpec(memory_space=pltpu.SMEM),
                       pl.BlockSpec(memory_space=pltpu.VMEM), pl.BlockSpec(memory_space=pltpu.VMEM)),
            scratch_shapes=[
                vm(ROWS, lanes), vm(ROWS, lanes, dtype=BF16), vm(ROWS, lanes, dtype=BF16),
                vm(DEPTH, ROWS, lanes, dtype=BF16), vm(DEPTH, ROWS, lanes, dtype=BF16),
                vm(LAYERS, 3, 3, CH, CH), vm(LAYERS, CH),
                vm(9 * inner_rows, 128), vm(5 * ext_rows, 128),
                vm(inner_rows, 128), vm(inner_rows, 128),
                vm(2 * ext_rows, 128), vm(2 * ext_rows, 128),
                vm(3 * inner_rows, 128), vm(inner_rows, 128), vm(2 * ext_rows, 128),
                vm(3 * ext_rows, 128), vm(3 * ext_rows, 128),
                vm(3 * ext_rows, 128), vm(3 * ext_rows, 128), vm(2 * ext_rows, 128),
                vm(3 * inner_rows, 128), vm(inner_rows, 128), vm(4 * inner_rows, 128),
                vm(3 * EPAIRS * WIDE, 128), vm(4 * ext_rows, 128),
                vm(4, 2, 3, inner_rows + ROWS, 128, dtype=BF16), vm(2, ext_rows, 768, dtype=BF16),
                vm(7, 768, 256, dtype=BF16),
                vm(2, 5, 1, PAIRS, 128), vm(2, 5, ROWS, 128), vm(4, 5, 1, 128),
                vm(2, 5, 1, PAIRS, 128), vm(2, 5, ROWS, 128), vm(4, 5, 1, 128),
                vm(2, 2, 3, 2, PAIRS, 128), vm(2, 2, 3, ROWS, 128), vm(2, 4, 3, 2, 128),
                vm(2, 2, 3, 2, PAIRS, 128), vm(2, 2, 3, ROWS, 128), vm(2, 4, 3, 2, 128),
                vm(ITERS + 1, 2, 128), vm(ITERS + 1, n_plane, 2, 128),
                vm(ITERS + 1, 2, 128), vm(ITERS + 1, PLANES, 2, 128),
                pltpu.SemaphoreType.DMA((7,)),
                pltpu.SemaphoreType.DMA((3, 8)), pltpu.SemaphoreType.DMA((3, 8)),
                pltpu.SemaphoreType.DMA((ITERS + 1,)), pltpu.SemaphoreType.DMA((ITERS + 1,)),
                pltpu.SemaphoreType.DMA((ITERS + 1,)), pltpu.SemaphoreType.DMA((ITERS + 1,)),
            ],
            compiler_params=pltpu.CompilerParams(
                collective_id=0, has_side_effects=True, vmem_limit_bytes=56 * 1024 * 1024),
            name="ascent",
        )
        return call(*args)

    placed = (P("row", "col"), P("row", "col"), P("row", "col"), P(None, "row", "col"), P(None, "row", "col"),
              P(), P(), P())
    return jax.shard_map(
        shards, mesh=mesh, in_specs=placed,
        out_specs=(P(), P(None, "row", "col"), P(None, "row", "col")), check_vma=False)
```

```python
import jax
import jax.numpy as jnp
from jax import lax
from jax.experimental import pallas as pl
from jax.experimental.pallas import tpu as pltpu
from jax.sharding import PartitionSpec as P

CH = 64
LAYERS = 4
ITERS = 3
DEPTH = LAYERS - 1
EPS = 1e-06
MESH = pl.DeviceIdType.MESH
F32 = jnp.float32
BF16 = jnp.bfloat16

ROWS = 16
PAIRS = 16
EXT = 24
EPAIRS = 18
WIDE = 32
PLANES = 8
MID, HALF, H1, H2, OBJ, H3, Q1, Q2, Q3 = range(9)
UP, DOWN, LEFT, RIGHT = range(4)
SIDES = ((-1, 0), (1, 0), (0, -1), (0, 1), (-1, -1), (-1, 1), (1, -1), (1, 1))


def at(start, size):
    return pl.ds(pl.multiple_of(start, 8), size)


def inner(which, pair):
    return at((which * PAIRS + pair) * ROWS, ROWS)


def ext(which, pair):
    return at((which * EPAIRS + pair) * EXT, EXT)


def ext_inner(which, pair):
    return pl.ds((which * EPAIRS + pair + 1) * EXT + 1, ROWS)


def softplus(z):
    return jnp.maximum(z, 0.0) + jnp.log1p(jnp.exp(-jnp.abs(z)))


def split(v):
    hi = v.astype(BF16)
    return hi, (v - hi.astype(F32)).astype(BF16)


def body(total_cells, n_row, n_col, obj_h, cen_h, rad_h, low_h, upp_h, ker_h, bia_h, steps,
         bounds_ref, lam_out, mu_out,
         obj_v, cen_v, rad_v, low_v, upp_v, ker_v, bia_v,
         base, wide_in, lam, mu, lam_x, mu_x, dl, dmu, dmu_x, trans, upd, g_x, p_x, pn, tb,
         d_w, y_s, y_w, lhs_i, lhs_x, wts,
         rows_s0, cols_s0, diag_s0, rows_r0, cols_r0, diag_r0,
         rows_s, cols_s, diag_s, rows_r, cols_r, diag_r,
         pay_a, buf_a, pay_b, buf_b,
         load_sem, halo_send, halo_recv, a_send, a_recv, b_send, b_recv):
    row = lax.axis_index("row")
    col = lax.axis_index("col")
    x_hi = row // PLANES
    z = row % PLANES
    n_plane = (n_row // PLANES) * n_col
    place = x_hi * n_col + col

    def plane_device(d):
        return (row ^ ((d // n_col) * PLANES), col ^ (d % n_col))

    def line_device(d):
        return (row ^ d, col)

    ring = [[place_ for place_ in (at_, (at_ + 1) % size, (at_ + size - 1) % size)]
            for at_, size in ((row, n_row), (col, n_col))]

    def side_device(side):
        return (ring[0][side[0]], ring[1][side[1]])

    loads = []
    for n, (src, dst) in enumerate(((cen_h, cen_v), (rad_h, rad_v), (upp_h, upp_v), (obj_h, obj_v),
                                    (ker_h, ker_v), (low_h, low_v), (bia_h, bia_v))):
        copy = pltpu.make_async_copy(src, dst, load_sem.at[n])
        copy.start()
        loads.append(copy)

    barrier = pltpu.get_barrier_semaphore()
    greeted = 0
    for d in range(1, n_plane):
        pl.semaphore_signal(barrier, inc=1, device_id=plane_device(d), device_id_type=MESH)
        greeted += 1
    for d in range(1, PLANES):
        pl.semaphore_signal(barrier, inc=1, device_id=line_device(d), device_id_type=MESH)
        greeted += 1
    for side in SIDES:
        if side[0] != 0:
            pl.semaphore_signal(barrier, inc=1, device_id=side_device(side), device_id_type=MESH)
            greeted += 1

    zero_tile = jnp.zeros((8, 128), F32)

    def halo_start(n, src_ref, maps, deep, bufs):
        rows_src, cols_src, diag_src, rows_dst, cols_dst, diag_dst = bufs
        for m in range(maps):
            first = m * PAIRS * ROWS
            for r in range(deep):
                rows_src[UP, m, r] = src_ref[pl.ds(first + r, PAIRS, stride=ROWS), :]
                rows_src[DOWN, m, r] = src_ref[pl.ds(first + ROWS - deep + r, PAIRS, stride=ROWS), :]
            cols_src[0, m] = src_ref[first : first + ROWS, :]
            cols_src[1, m] = src_ref[first + (PAIRS - 1) * ROWS : first + PAIRS * ROWS, :]
            last = first + (PAIRS - 1) * ROWS
            diag_src[0, m] = src_ref[first : first + deep, :]
            diag_src[1, m] = src_ref[last : last + deep, :]
            diag_src[2, m] = src_ref[first + ROWS - deep : first + ROWS, :]
            diag_src[3, m] = src_ref[last + ROWS - deep : last + ROWS, :]
        copies = []
        for s in (4, 5, 6, 7, 0, 1, 2, 3):
            if s < 2:
                src, dst = rows_src.at[s], rows_dst.at[s]
            elif s < 4:
                src, dst = cols_src.at[s - 2], cols_dst.at[s - 2]
            else:
                src, dst = diag_src.at[s - 4], diag_dst.at[s - 4]
            copy = pltpu.make_async_remote_copy(
                src_ref=src, dst_ref=dst, send_sem=halo_send.at[n, s], recv_sem=halo_recv.at[n, s],
                device_id=side_device(SIDES[s]), device_id_type=MESH)
            copy.start()
            copies.append(copy)
        return copies

    no_above = row == 0
    no_below = row == n_row - 1
    no_left = col == 0
    no_right = col == n_col - 1

    def halo_place(dst_ref, maps, deep, tall, top, pairs, bufs):
        _, _, _, rows_dst, cols_dst, diag_dst = bufs

        def cut(gone, v):
            return jnp.where(gone, 0.0, v)

        for m in range(maps):
            first = m * pairs * tall
            last = first + (EPAIRS - 1) * tall
            for r in range(deep):
                dst_ref[pl.ds(first + tall + top + ROWS + r, PAIRS, stride=tall), :] = cut(
                    no_below, rows_dst[0, m, r])
                dst_ref[pl.ds(first + tall + top - deep + r, PAIRS, stride=tall), :] = cut(
                    no_above, rows_dst[1, m, r])
            dst_ref[last + top : last + top + ROWS, :] = cut(no_right, cols_dst[0, m])
            dst_ref[first + top : first + top + ROWS, :] = cut(no_left, cols_dst[1, m])
            dst_ref[last + top + ROWS : last + top + ROWS + deep, :] = cut(
                jnp.logical_or(no_below, no_right), diag_dst[0, m])
            dst_ref[first + top + ROWS : first + top + ROWS + deep, :] = cut(
                jnp.logical_or(no_below, no_left), diag_dst[1, m])
            dst_ref[last + top - deep : last + top, :] = cut(
                jnp.logical_or(no_above, no_right), diag_dst[2, m])
            dst_ref[first + top - deep : first + top, :] = cut(
                jnp.logical_or(no_above, no_left), diag_dst[3, m])

    sends = []

    def sum_start(n, first_row, second_row):
        pay_a[n, 0:1] = first_row
        pay_a[n, 1:2] = second_row
        buf_a[n, place, 0:1] = first_row
        buf_a[n, place, 1:2] = second_row
        for d in range(1, n_plane):
            pltpu.make_async_remote_copy(
                src_ref=pay_a.at[n], dst_ref=buf_a.at[n, place], send_sem=a_send.at[n], recv_sem=a_recv.at[n],
                device_id=plane_device(d), device_id_type=MESH).start()

    def whole(buf, n, count, send, recv):
        part = buf.at[n, 0:count]
        return pltpu.make_async_remote_copy(
            src_ref=part, dst_ref=part, send_sem=send.at[n], recv_sem=recv.at[n],
            device_id=side_device((0, 1)), device_id_type=MESH)

    def sum_middle(n):
        whole(buf_a, n, n_plane - 1, a_send, a_recv).wait_recv()
        part = jnp.sum(buf_a[n], axis=0)
        pay_b[n] = part
        buf_b[n, z] = part
        for d in range(1, PLANES):
            pltpu.make_async_remote_copy(
                src_ref=pay_b.at[n], dst_ref=buf_b.at[n, z], send_sem=b_send.at[n], recv_sem=b_recv.at[n],
                device_id=line_device(d), device_id_type=MESH).start()

    def sum_end(n):
        whole(buf_b, n, PLANES - 1, b_send, b_recv).wait_recv()
        return jnp.sum(buf_b[n], axis=0)

    lane = lax.broadcasted_iota(jnp.int32, (EXT, 128), 1) < CH
    lane_w = lax.broadcasted_iota(jnp.int32, (WIDE, 128), 1) < CH

    def turn(x):
        return pltpu.roll(x, CH, 1)

    def window(k, u, e, before, now):
        y = y_s[u * LAYERS + k]
        y[...] = jnp.where(lane, before, now)
        for dh in range(3):
            hi, lo = split(y[dh : dh + ROWS, :])
            rows = pl.ds(pl.multiple_of(e * ROWS, ROWS), ROWS)
            lhs_i[k, 0, dh, rows, :] = hi
            lhs_i[k, 1, dh, rows, :] = lo

    def conv(slot, weight):
        size = PAIRS * ROWS
        halves = []
        for part in range(2):
            tiles = []
            for dh in range(3):
                tiles.append(lhs_i[slot, part, dh, ROWS : size + ROWS, :])
                tiles.append(lhs_i[slot, part, dh, 2 * ROWS : size + 2 * ROWS, :])
            halves.append(jnp.concatenate(tiles, axis=1))
        high = jnp.dot(halves[0], wts[weight], preferred_element_type=F32)
        low = jnp.dot(halves[1], wts[weight, :, 0:128], preferred_element_type=F32)
        return (low + high[:, 128:]) + high[:, :128]

    def windows_wide():
        def wide(m, p):
            return turn(d_w[at((m * (EPAIRS + 1) + p) * WIDE, WIDE), :])

        none = jnp.zeros((WIDE, 128), F32)
        start = []
        for m in range(DEPTH):
            r = wide(m, 0)
            start += [r, jnp.where(lane_w, none, r)]

        def step(t, carry):
            out = []
            for m in range(DEPTH):
                r0, ya = carry[2 * m], carry[2 * m + 1]
                r1, r2 = wide(m, 2 * t + 1), wide(m, 2 * t + 2)
                yb = jnp.where(lane_w, r0, r1)
                yc = jnp.where(lane_w, r1, r2)
                for i, y in enumerate((ya, yb, yc)):
                    y_w[m * 3 + i][...] = y
                for dh in range(3):
                    ys = [y_w[m * 3 + i][dh : dh + EXT, :] for i in range(3)]
                    for half in range(2):
                        hi, lo = split(jnp.concatenate([ys[half], ys[half + 1]], axis=0))
                        rows = pl.ds(pl.multiple_of(t * 2 * EXT, 16), 2 * EXT)
                        lhs_x[m, 0, rows, (dh * 2 + half) * 128 : (dh * 2 + half + 1) * 128] = hi
                        lhs_x[m, 1, rows, (dh * 2 + half) * 128 : (dh * 2 + half + 1) * 128] = lo
                out += [r2, yc]
            return tuple(out)
        lax.fori_loop(0, EPAIRS // 2, step, tuple(start))

    def conv_wide(m):
        size = EPAIRS * EXT
        high = jnp.dot(lhs_x[m, 0], wts[3 + m], preferred_element_type=F32)
        low = jnp.dot(lhs_x[m, 1], wts[3 + m, :, 0:128], preferred_element_type=F32)
        upd[at(m * size, size), :] = (low + high[:, 128:]) + high[:, :128]

    for n in range(4):
        loads[n].wait()

    def fill(j, carry):
        lanes = pl.ds(pl.multiple_of(j * 128, 128), 128)
        c = cen_v[:, lanes].astype(F32)
        r = rad_v[:, lanes].astype(F32)
        lo, hi = c - r, c + r
        vals = {MID: 0.5 * (hi + lo), HALF: 0.5 * (hi - lo), OBJ: obj_v[:, lanes]}
        for m, name in enumerate((H1, H2, H3)):
            vals[name] = 0.5 * upp_v[m, :, lanes].astype(F32)
        for name, v in vals.items():
            base[inner(name, j), :] = v
            if name <= OBJ:
                wide_in[at((name * EPAIRS + j + 1) * EXT, 8), :] = zero_tile
                wide_in[at((name * EPAIRS + j + 1) * EXT + 16, 8), :] = zero_tile
                wide_in[ext_inner(name, j), :] = v
        return carry
    lax.fori_loop(0, PAIRS, fill, 0)
    for m in range(5):
        for e in (0, EPAIRS - 1):
            wide_in[ext(m, e), :] = jnp.zeros((EXT, 128), F32)

    pl.semaphore_wait(barrier, greeted)
    bufs0 = (rows_s0, cols_s0, diag_s0, rows_r0, cols_r0, diag_r0)
    first_copies = halo_start(0, base, 5, 1, bufs0)
    sends += first_copies

    for n in range(4, 7):
        loads[n].wait()

    def fill_low(j, carry):
        lanes = pl.ds(pl.multiple_of(j * 128, 128), 128)
        for m, name in enumerate((Q1, Q2, Q3)):
            base[inner(name, j), :] = 0.5 * low_v[m, :, lanes].astype(F32)
        return carry
    lax.fori_loop(0, PAIRS, fill_low, 0)

    bias = jnp.concatenate([bia_v[...], bia_v[...]], axis=1)
    none64 = jnp.zeros((CH, CH), F32)

    def put_weight(slot, dh, block):
        hi, lo = split(block)
        wts[slot, dh * 256 : (dh + 1) * 256, 0:128] = hi
        wts[slot, dh * 256 : (dh + 1) * 256, 128:256] = lo

    def build(k, carry):
        for dh in range(3):
            taps = [ker_v[k, 2 - dh, dw] for dw in range(3)]
            one = jnp.concatenate([jnp.concatenate([taps[2], taps[1]], axis=1),
                                   jnp.concatenate([none64, taps[2]], axis=1)], axis=0)
            two = jnp.concatenate([jnp.concatenate([taps[0], none64], axis=1),
                                   jnp.concatenate([taps[1], taps[0]], axis=1)], axis=0)
            put_weight(3 + k, dh, jnp.concatenate([one.T, two.T], axis=0))
        return carry
    lax.fori_loop(0, LAYERS, build, 0)

    def build_forward(k, carry):
        for dh in range(3):
            taps = [ker_v[k, dh, dw] for dw in range(3)]
            put_weight(k, dh, jnp.concatenate(
                [jnp.concatenate(taps + [none64], axis=0), jnp.concatenate([none64] + taps, axis=0)], axis=1))
        return carry
    lax.fori_loop(0, DEPTH, build_forward, 0)

    def clear(t, carry):
        d_w[at(t * WIDE, WIDE), :] = jnp.zeros((WIDE, 128), F32)
        return carry
    lax.fori_loop(0, DEPTH * (EPAIRS + 1), clear, 0)

    for copy in first_copies:
        copy.wait_recv()
    halo_place(wide_in, 5, 1, EXT, 1, EPAIRS, bufs0)

    def value_terms(i, j):
        q = -0.5
        total = base[inner(OBJ, j), :] * bias[DEPTH : DEPTH + 1]
        mid, half = base[inner(MID, j), :], base[inner(HALF, j), :]
        hs = [base[inner(n, j), :] for n in (H1, H2, H3)]
        qs = [base[inner(n, j), :] for n in (Q1, Q2, Q3)]
        t3 = tb[inner(0, j), :]
        if i == 0:
            total += q * softplus(-4.0 * hs[2] * t3)
            return total
        g0 = g_x[ext_inner(0, j), :]
        total += g0 * (mid - half) + q * softplus(-4.0 * half * g0)
        lams = [lam_x[ext_inner(0, j), :], lam_x[ext_inner(1, j), :], lam[inner(0, j), :]]
        mus = [mu_x[ext_inner(0, j), :], mu_x[ext_inner(1, j), :], mu[inner(0, j), :]]
        for m in range(DEPTH):
            g = g_x[ext_inner(m + 1, j), :] if m < 2 else mus[2] + t3
            total += q * softplus(-4.0 * hs[m] * g)
            total += q * softplus(-4.0 * hs[m] * (lams[m] - mus[m]))
            total += q * softplus(4.0 * qs[m] * lams[m])
            total -= lams[m] * bias[m : m + 1]
        return total

    def value_row(i):
        def step(j, acc):
            return acc + value_terms(i, j)
        acc = lax.fori_loop(0, PAIRS, step, jnp.zeros((ROWS, 128), F32))
        out = jnp.sum(acc, axis=0, keepdims=True)
        if i == 0:
            out = out - (0.5 * 0.6931471805599453 * 9 * ROWS * PAIRS)
        return out

    scale = None
    value_prev = jnp.zeros((1, 128), F32)
    totals = []
    for i in range(ITERS):
        first = i == 1

        def step_x(g, carry):
            before = list(carry)
            for u in range(3):
                e = 3 * g + u
                if i == 0:
                    xs = [wide_in[ext(n, e), :] for n in (MID, H1, H2)]
                    for m in range(2):
                        p_x[ext(m, e), :] = xs[m + 1]
                        dmu_x[ext(m, e), :] = xs[m + 1] - p_x[ext(m, e), :]
                    xs.append(wide_in[ext(OBJ, e), :])
                else:
                    halfs = [wide_in[ext(n, e), :] for n in (HALF, H1, H2)]
                    mids = [wide_in[ext(MID, e), :], halfs[1], halfs[2]]
                    xs = []
                    mus = []
                    for m in range(2):
                        new_mu = scale * dmu_x[ext(m, e), :]
                        new_lam = scale * d_w[pl.ds((m * (EPAIRS + 1) + e) * WIDE + 1, EXT), :]
                        if not first:
                            new_mu = mu_x[ext(m, e), :] + new_mu
                            new_lam = lam_x[ext(m, e), :] + new_lam
                        mu_x[ext(m, e), :] = new_mu
                        lam_x[ext(m, e), :] = new_lam
                        mus.append((new_mu, new_lam))
                    for k in range(DEPTH):
                        t = scale * upd[ext(k, e), :]
                        if not first:
                            t = trans[ext(k, e), :] + t
                        trans[ext(k, e), :] = t
                        coef = -t if k == 0 else mus[k - 1][0] - t
                        g_x[ext(k, e), :] = coef
                        xs.append(mids[k] - halfs[k] * jnp.tanh(2.0 * halfs[k] * coef))
                    for m in range(2):
                        h = halfs[m + 1]
                        p = h - h * jnp.tanh(2.0 * h * (mus[m][1] - mus[m][0]))
                        p_x[ext(m, e), :] = p
                        dmu_x[ext(m, e), :] = xs[m + 1] - p
                for k, x in enumerate(xs):
                    now = turn(x)
                    window(k, u, e, before[k], now)
                    before[k] = now
            return tuple(before)
        maps = LAYERS if i == 0 else DEPTH
        lax.fori_loop(0, EPAIRS // 3, step_x, tuple(jnp.zeros((EXT, 128), F32) for _ in range(maps)))

        acc = jnp.zeros((ROWS, 128), F32)
        if i == 0:
            back = conv(DEPTH, 3 + DEPTH)
            for j in range(PAIRS):
                tb[inner(0, j), :] = back[j * ROWS : (j + 1) * ROWS]
        for m in (2, 0, 1):
            rest = []
            for j in range(PAIRS):
                h = base[inner(H1 + m if m < 2 else H3, j), :]
                q = base[inner(Q1 + m, j), :]
                if m == 2:
                    t3 = tb[inner(0, j), :]
                    if i == 0:
                        p, v_lam = h, None
                    else:
                        new_mu = scale * dmu[inner(0, j), :]
                        v_lam = scale * dl[inner(2, j), :]
                        if not first:
                            new_mu = mu[inner(0, j), :] + new_mu
                            v_lam = lam[inner(0, j), :] + v_lam
                        mu[inner(0, j), :] = new_mu
                        lam[inner(0, j), :] = v_lam
                        p = h - h * jnp.tanh(2.0 * h * (v_lam - new_mu))
                        t3 = new_mu + t3
                    v = (h - h * jnp.tanh(2.0 * h * t3)) - p
                    dmu[inner(0, j), :] = v
                else:
                    p = p_x[ext_inner(m, j), :]
                    v_lam = None if i == 0 else lam_x[ext_inner(m, j), :]
                    v = dmu_x[ext_inner(m, j), :]
                acc = acc + v * v
                n = q if i == 0 else q + q * jnp.tanh(2.0 * q * v_lam)
                pn[inner(m, j), :] = p - n - bias[m : m + 1]
            image = conv(m, m)
            for j in range(PAIRS):
                v = pn[inner(m, j), :] - image[j * ROWS : (j + 1) * ROWS]
                dl[inner(m, j), :] = v
                d_w[pl.ds((m * (EPAIRS + 1) + j + 1) * WIDE + 2, ROWS), :] = v
                acc = acc + v * v
        sum_start(i, jnp.sum(acc, axis=0, keepdims=True), value_prev)

        copies = []
        if i < ITERS - 1:
            bufs = tuple(ref.at[i] for ref in (rows_s, cols_s, diag_s, rows_r, cols_r, diag_r))
            copies = halo_start(1 + i, dl, DEPTH, 2, bufs)
            sends += copies
        value_prev = value_row(i)
        sum_middle(i)
        if i < ITERS - 1:
            for copy in copies:
                copy.wait_recv()
            halo_place(d_w, DEPTH, 2, WIDE, 2, EPAIRS + 1, bufs)
            windows_wide()
            for m in range(DEPTH):
                conv_wide(m)
        else:
            sum_start(ITERS, jnp.zeros((1, 128), F32), value_prev)
        both = sum_end(i)
        squares = jnp.sum(both[0:1], axis=1, keepdims=True)
        scale = steps[i] / jnp.sqrt(squares / (2 * DEPTH * total_cells) + EPS)
        scale = jnp.broadcast_to(scale, (1, 128))
        totals.append(both)

    def finish(j, carry):
        lanes = pl.ds(pl.multiple_of(j * 128, 128), 128)
        for m in range(2):
            lam_out[m, :, lanes] = lam_x[ext_inner(m, j), :] + scale * dl[inner(m, j), :]
            mu_out[m, :, lanes] = mu_x[ext_inner(m, j), :] + scale * dmu_x[ext_inner(m, j), :]
        lam_out[2, :, lanes] = lam[inner(0, j), :] + scale * dl[inner(2, j), :]
        mu_out[2, :, lanes] = mu[inner(0, j), :] + scale * dmu[inner(0, j), :]
        return carry
    lax.fori_loop(0, PAIRS, finish, 0)
    sum_middle(ITERS)
    totals.append(sum_end(ITERS))
    for i in range(ITERS):
        bounds_ref[i] = jnp.sum(totals[i + 1][1:2]) / total_cells

    for copy in sends:
        copy.wait_send()
    for n in range(ITERS + 1):
        whole(buf_a, n, n_plane - 1, a_send, a_recv).wait_send()
        whole(buf_b, n, PLANES - 1, b_send, b_recv).wait_send()


def solution(mesh):
    n_row, n_col = mesh.shape["row"], mesh.shape["col"]
    n_plane = (n_row // PLANES) * n_col
    total_cells = n_row * n_col * ROWS * PAIRS * 128

    def vm(*shape, dtype=F32):
        return pltpu.VMEM(shape, dtype)

    inner_rows = PAIRS * ROWS
    ext_rows = EPAIRS * EXT
    lanes = PAIRS * 128
    any_spec = pl.BlockSpec(memory_space=pl.ANY)

    def kernel(*refs):
        body(float(total_cells), n_row, n_col, *refs)

    def shards(*args):
        call = pl.pallas_call(
            kernel,
            out_shape=(jax.ShapeDtypeStruct((ITERS,), F32),
                       jax.ShapeDtypeStruct((DEPTH, ROWS, lanes), F32),
                       jax.ShapeDtypeStruct((DEPTH, ROWS, lanes), F32)),
            in_specs=[any_spec] * 7 + [pl.BlockSpec(memory_space=pltpu.SMEM)],
            out_specs=(pl.BlockSpec(memory_space=pltpu.SMEM),
                       pl.BlockSpec(memory_space=pltpu.VMEM), pl.BlockSpec(memory_space=pltpu.VMEM)),
            scratch_shapes=[
                vm(ROWS, lanes), vm(ROWS, lanes, dtype=BF16), vm(ROWS, lanes, dtype=BF16),
                vm(DEPTH, ROWS, lanes, dtype=BF16), vm(DEPTH, ROWS, lanes, dtype=BF16),
                vm(LAYERS, 3, 3, CH, CH), vm(LAYERS, CH),
                vm(9 * inner_rows, 128), vm(5 * ext_rows, 128),
                vm(inner_rows, 128), vm(inner_rows, 128),
                vm(2 * ext_rows, 128), vm(2 * ext_rows, 128),
                vm(3 * inner_rows, 128), vm(inner_rows, 128), vm(2 * ext_rows, 128),
                vm(3 * ext_rows, 128), vm(3 * ext_rows, 128),
                vm(3 * ext_rows, 128), vm(2 * ext_rows, 128),
                vm(3 * inner_rows, 128), vm(inner_rows, 128),
                vm(3 * (EPAIRS + 1) * WIDE, 128),
                [vm(EXT, 128)] * 12, [vm(WIDE, 128)] * 9,
                vm(4, 2, 3, inner_rows + 2 * ROWS, 128, dtype=BF16), vm(3, 2, ext_rows, 768, dtype=BF16),
                vm(7, 768, 256, dtype=BF16),
                vm(2, 5, 1, PAIRS, 128), vm(2, 5, ROWS, 128), vm(4, 5, 1, 128),
                vm(2, 5, 1, PAIRS, 128), vm(2, 5, ROWS, 128), vm(4, 5, 1, 128),
                vm(2, 2, 3, 2, PAIRS, 128), vm(2, 2, 3, ROWS, 128), vm(2, 4, 3, 2, 128),
                vm(2, 2, 3, 2, PAIRS, 128), vm(2, 2, 3, ROWS, 128), vm(2, 4, 3, 2, 128),
                vm(ITERS + 1, 2, 128), vm(ITERS + 1, n_plane, 2, 128),
                vm(ITERS + 1, 2, 128), vm(ITERS + 1, PLANES, 2, 128),
                pltpu.SemaphoreType.DMA((7,)),
                pltpu.SemaphoreType.DMA((3, 8)), pltpu.SemaphoreType.DMA((3, 8)),
                pltpu.SemaphoreType.DMA((ITERS + 1,)), pltpu.SemaphoreType.DMA((ITERS + 1,)),
                pltpu.SemaphoreType.DMA((ITERS + 1,)), pltpu.SemaphoreType.DMA((ITERS + 1,)),
            ],
            compiler_params=pltpu.CompilerParams(
                collective_id=0, has_side_effects=True, vmem_limit_bytes=56 * 1024 * 1024),
            name="ascent",
        )
        return call(*args)

    placed = (P("row", "col"), P("row", "col"), P("row", "col"), P(None, "row", "col"), P(None, "row", "col"),
              P(), P(), P())
    return jax.shard_map(
        shards, mesh=mesh, in_specs=placed,
        out_specs=(P(), P(None, "row", "col"), P(None, "row", "col")), check_vma=False)
```

```python
import jax
import jax.numpy as jnp
from jax import lax
from jax.experimental import pallas as pl
from jax.experimental.pallas import tpu as pltpu
from jax.sharding import PartitionSpec as P

CH = 64
LAYERS = 4
ITERS = 3
DEPTH = LAYERS - 1
EPS = 1e-06
MESH = pl.DeviceIdType.MESH
F32 = jnp.float32
BF16 = jnp.bfloat16

ROWS = 16
PAIRS = 16
EXT = 24
EPAIRS = 18
WIDE = 32
PLANES = 8
MID, HALF, H1, H2, OBJ, H3, Q1, Q2, Q3 = range(9)
UP, DOWN, LEFT, RIGHT = range(4)
SIDES = ((-1, 0), (1, 0), (0, -1), (0, 1), (-1, -1), (-1, 1), (1, -1), (1, 1))


def at(start, size):
    return pl.ds(pl.multiple_of(start, 8), size)


def inner(which, pair):
    return at((which * PAIRS + pair) * ROWS, ROWS)


def ext(which, pair):
    return at((which * EPAIRS + pair) * EXT, EXT)


def ext_inner(which, pair):
    return pl.ds((which * EPAIRS + pair + 1) * EXT + 1, ROWS)


def softplus(z):
    return jnp.maximum(z, 0.0) + jnp.log1p(jnp.exp(-jnp.abs(z)))


def split(v):
    hi = v.astype(BF16)
    return hi, (v - hi.astype(F32)).astype(BF16)


def body(total_cells, n_row, n_col, obj_h, cen_h, rad_h, low_h, upp_h, ker_h, bia_h, steps,
         bounds_ref, lam_out, mu_out,
         obj_v, cen_v, rad_v, low_v, upp_v, ker_v, bia_v,
         base, wide_in, lam, mu, lam_x, mu_x, dl, dmu, dmu_x, trans, upd, g_x, p_x, pn, tb,
         d_w, y_s, y_w, lhs_i, lhs_x, wts,
         rows_s0, cols_s0, diag_s0, rows_r0, cols_r0, diag_r0,
         rows_s, cols_s, diag_s, rows_r, cols_r, diag_r,
         pay_a, buf_a, pay_b, buf_b,
         load_sem, halo_send, halo_recv, a_send, a_recv, b_send, b_recv):
    row = lax.axis_index("row")
    col = lax.axis_index("col")
    x_hi = row // PLANES
    z = row % PLANES
    n_plane = (n_row // PLANES) * n_col
    place = x_hi * n_col + col

    def plane_device(d):
        return (row ^ ((d // n_col) * PLANES), col ^ (d % n_col))

    def line_device(d):
        return (row ^ d, col)

    ring = [[place_ for place_ in (at_, (at_ + 1) % size, (at_ + size - 1) % size)]
            for at_, size in ((row, n_row), (col, n_col))]

    def side_device(side):
        return (ring[0][side[0]], ring[1][side[1]])

    loads = []
    for n, (src, dst) in enumerate(((cen_h, cen_v), (rad_h, rad_v), (upp_h, upp_v), (obj_h, obj_v),
                                    (ker_h, ker_v), (low_h, low_v), (bia_h, bia_v))):
        copy = pltpu.make_async_copy(src, dst, load_sem.at[n])
        copy.start()
        loads.append(copy)

    barrier = pltpu.get_barrier_semaphore()
    greeted = 0
    for d in range(1, n_plane):
        pl.semaphore_signal(barrier, inc=1, device_id=plane_device(d), device_id_type=MESH)
        greeted += 1
    for d in range(1, PLANES):
        pl.semaphore_signal(barrier, inc=1, device_id=line_device(d), device_id_type=MESH)
        greeted += 1
    for side in SIDES:
        if side[0] != 0:
            pl.semaphore_signal(barrier, inc=1, device_id=side_device(side), device_id_type=MESH)
            greeted += 1

    zero_tile = jnp.zeros((8, 128), F32)

    def halo_start(n, src_ref, maps, deep, bufs):
        rows_src, cols_src, diag_src, rows_dst, cols_dst, diag_dst = bufs
        for m in range(maps):
            first = m * PAIRS * ROWS
            for r in range(deep):
                rows_src[UP, m, r] = src_ref[pl.ds(first + r, PAIRS, stride=ROWS), :]
                rows_src[DOWN, m, r] = src_ref[pl.ds(first + ROWS - deep + r, PAIRS, stride=ROWS), :]
            cols_src[0, m] = src_ref[first : first + ROWS, :]
            cols_src[1, m] = src_ref[first + (PAIRS - 1) * ROWS : first + PAIRS * ROWS, :]
            last = first + (PAIRS - 1) * ROWS
            diag_src[0, m] = src_ref[first : first + deep, :]
            diag_src[1, m] = src_ref[last : last + deep, :]
            diag_src[2, m] = src_ref[first + ROWS - deep : first + ROWS, :]
            diag_src[3, m] = src_ref[last + ROWS - deep : last + ROWS, :]
        copies = []
        for s in (4, 5, 6, 7, 0, 1, 2, 3):
            if s < 2:
                src, dst = rows_src.at[s], rows_dst.at[s]
            elif s < 4:
                src, dst = cols_src.at[s - 2], cols_dst.at[s - 2]
            else:
                src, dst = diag_src.at[s - 4], diag_dst.at[s - 4]
            copy = pltpu.make_async_remote_copy(
                src_ref=src, dst_ref=dst, send_sem=halo_send.at[n, s], recv_sem=halo_recv.at[n, s],
                device_id=side_device(SIDES[s]), device_id_type=MESH)
            copy.start()
            copies.append(copy)
        return copies

    no_above = row == 0
    no_below = row == n_row - 1
    no_left = col == 0
    no_right = col == n_col - 1

    def halo_place(dst_ref, maps, deep, tall, top, pairs, bufs):
        _, _, _, rows_dst, cols_dst, diag_dst = bufs

        def cut(gone, v):
            return jnp.where(gone, 0.0, v)

        for m in range(maps):
            first = m * pairs * tall
            last = first + (EPAIRS - 1) * tall
            for r in range(deep):
                dst_ref[pl.ds(first + tall + top + ROWS + r, PAIRS, stride=tall), :] = cut(
                    no_below, rows_dst[0, m, r])
                dst_ref[pl.ds(first + tall + top - deep + r, PAIRS, stride=tall), :] = cut(
                    no_above, rows_dst[1, m, r])
            dst_ref[last + top : last + top + ROWS, :] = cut(no_right, cols_dst[0, m])
            dst_ref[first + top : first + top + ROWS, :] = cut(no_left, cols_dst[1, m])
            dst_ref[last + top + ROWS : last + top + ROWS + deep, :] = cut(
                jnp.logical_or(no_below, no_right), diag_dst[0, m])
            dst_ref[first + top + ROWS : first + top + ROWS + deep, :] = cut(
                jnp.logical_or(no_below, no_left), diag_dst[1, m])
            dst_ref[last + top - deep : last + top, :] = cut(
                jnp.logical_or(no_above, no_right), diag_dst[2, m])
            dst_ref[first + top - deep : first + top, :] = cut(
                jnp.logical_or(no_above, no_left), diag_dst[3, m])

    sends = []

    def sum_start(n, first_row, second_row):
        pay_a[n, 0:1] = first_row
        pay_a[n, 1:2] = second_row
        buf_a[n, place, 0:1] = first_row
        buf_a[n, place, 1:2] = second_row
        for d in range(1, n_plane):
            pltpu.make_async_remote_copy(
                src_ref=pay_a.at[n], dst_ref=buf_a.at[n, place], send_sem=a_send.at[n], recv_sem=a_recv.at[n],
                device_id=plane_device(d), device_id_type=MESH).start()

    def whole(buf, n, count, send, recv):
        part = buf.at[n, 0:count]
        return pltpu.make_async_remote_copy(
            src_ref=part, dst_ref=part, send_sem=send.at[n], recv_sem=recv.at[n],
            device_id=side_device((0, 1)), device_id_type=MESH)

    def sum_middle(n):
        whole(buf_a, n, n_plane - 1, a_send, a_recv).wait_recv()
        part = jnp.sum(buf_a[n], axis=0)
        pay_b[n] = part
        buf_b[n, z] = part
        for d in range(1, PLANES):
            pltpu.make_async_remote_copy(
                src_ref=pay_b.at[n], dst_ref=buf_b.at[n, z], send_sem=b_send.at[n], recv_sem=b_recv.at[n],
                device_id=line_device(d), device_id_type=MESH).start()

    def sum_end(n):
        whole(buf_b, n, PLANES - 1, b_send, b_recv).wait_recv()
        return jnp.sum(buf_b[n], axis=0)

    lane = lax.broadcasted_iota(jnp.int32, (EXT, 128), 1) < CH
    lane_w = lax.broadcasted_iota(jnp.int32, (WIDE, 128), 1) < CH

    def turn(x):
        return pltpu.roll(x, CH, 1)

    def window(k, u, e, before, now):
        y = y_s[u * LAYERS + k]
        y[...] = jnp.where(lane, before, now)
        for dh in range(3):
            hi, lo = split(y[dh : dh + ROWS, :])
            rows = pl.ds(pl.multiple_of(e * ROWS, ROWS), ROWS)
            lhs_i[k, 0, dh, rows, :] = hi
            lhs_i[k, 1, dh, rows, :] = lo

    def conv(slot, weight):
        size = PAIRS * ROWS
        halves = []
        for part in range(2):
            tiles = []
            for dh in range(3):
                tiles.append(lhs_i[slot, part, dh, ROWS : size + ROWS, :])
                tiles.append(lhs_i[slot, part, dh, 2 * ROWS : size + 2 * ROWS, :])
            halves.append(jnp.concatenate(tiles, axis=1))
        high = jnp.dot(halves[0], wts[weight], preferred_element_type=F32)
        low = jnp.dot(halves[1], wts[weight, :, 0:128], preferred_element_type=F32)
        return (low + high[:, 128:]) + high[:, :128]

    def windows_wide():
        def wide(m, p):
            return turn(d_w[at((m * (EPAIRS + 1) + p) * WIDE, WIDE), :])

        none = jnp.zeros((WIDE, 128), F32)
        start = []
        for m in range(DEPTH):
            r = wide(m, 0)
            start += [r, jnp.where(lane_w, none, r)]

        def step(t, carry):
            out = []
            for m in range(DEPTH):
                r0, ya = carry[2 * m], carry[2 * m + 1]
                r1, r2 = wide(m, 2 * t + 1), wide(m, 2 * t + 2)
                yb = jnp.where(lane_w, r0, r1)
                yc = jnp.where(lane_w, r1, r2)
                for i, y in enumerate((ya, yb, yc)):
                    y_w[m * 3 + i][...] = y
                for dh in range(3):
                    ys = [y_w[m * 3 + i][dh : dh + EXT, :] for i in range(3)]
                    for half in range(2):
                        hi, lo = split(jnp.concatenate([ys[half], ys[half + 1]], axis=0))
                        rows = pl.ds(pl.multiple_of(t * 2 * EXT, 16), 2 * EXT)
                        lhs_x[m, 0, rows, (dh * 2 + half) * 128 : (dh * 2 + half + 1) * 128] = hi
                        lhs_x[m, 1, rows, (dh * 2 + half) * 128 : (dh * 2 + half + 1) * 128] = lo
                out += [r2, yc]
            return tuple(out)
        lax.fori_loop(0, EPAIRS // 2, step, tuple(start))

    def conv_wide(m):
        size = EPAIRS * EXT
        high = jnp.dot(lhs_x[m, 0], wts[3 + m], preferred_element_type=F32)
        low = jnp.dot(lhs_x[m, 1], wts[3 + m, :, 0:128], preferred_element_type=F32)
        upd[at(m * size, size), :] = (low + high[:, 128:]) + high[:, :128]

    for n in range(4):
        loads[n].wait()

    def fill(j, carry):
        lanes = pl.ds(pl.multiple_of(j * 128, 128), 128)
        c = cen_v[:, lanes].astype(F32)
        r = rad_v[:, lanes].astype(F32)
        lo, hi = c - r, c + r
        vals = {MID: 0.5 * (hi + lo), HALF: 0.5 * (hi - lo), OBJ: obj_v[:, lanes]}
        for m, name in enumerate((H1, H2, H3)):
            vals[name] = 0.5 * upp_v[m, :, lanes].astype(F32)
        for name, v in vals.items():
            base[inner(name, j), :] = v
            if name <= OBJ:
                wide_in[at((name * EPAIRS + j + 1) * EXT, 8), :] = zero_tile
                wide_in[at((name * EPAIRS + j + 1) * EXT + 16, 8), :] = zero_tile
                wide_in[ext_inner(name, j), :] = v
        return carry
    lax.fori_loop(0, PAIRS, fill, 0)
    for m in range(5):
        for e in (0, EPAIRS - 1):
            wide_in[ext(m, e), :] = jnp.zeros((EXT, 128), F32)

    pl.semaphore_wait(barrier, greeted)
    bufs0 = (rows_s0, cols_s0, diag_s0, rows_r0, cols_r0, diag_r0)
    first_copies = halo_start(0, base, 5, 1, bufs0)
    sends += first_copies

    for n in range(4, 7):
        loads[n].wait()

    def fill_low(j, carry):
        lanes = pl.ds(pl.multiple_of(j * 128, 128), 128)
        for m, name in enumerate((Q1, Q2, Q3)):
            base[inner(name, j), :] = 0.5 * low_v[m, :, lanes].astype(F32)
        return carry
    lax.fori_loop(0, PAIRS, fill_low, 0)

    bias = jnp.concatenate([bia_v[...], bia_v[...]], axis=1)
    none64 = jnp.zeros((CH, CH), F32)

    def put_weight(slot, dh, block):
        hi, lo = split(block)
        wts[slot, dh * 256 : (dh + 1) * 256, 0:128] = hi
        wts[slot, dh * 256 : (dh + 1) * 256, 128:256] = lo

    def build(k, carry):
        for dh in range(3):
            taps = [ker_v[k, 2 - dh, dw] for dw in range(3)]
            one = jnp.concatenate([jnp.concatenate([taps[2], taps[1]], axis=1),
                                   jnp.concatenate([none64, taps[2]], axis=1)], axis=0)
            two = jnp.concatenate([jnp.concatenate([taps[0], none64], axis=1),
                                   jnp.concatenate([taps[1], taps[0]], axis=1)], axis=0)
            put_weight(3 + k, dh, jnp.concatenate([one.T, two.T], axis=0))
        return carry
    lax.fori_loop(0, LAYERS, build, 0)

    def build_forward(k, carry):
        for dh in range(3):
            taps = [ker_v[k, dh, dw] for dw in range(3)]
            put_weight(k, dh, jnp.concatenate(
                [jnp.concatenate(taps + [none64], axis=0), jnp.concatenate([none64] + taps, axis=0)], axis=1))
        return carry
    lax.fori_loop(0, DEPTH, build_forward, 0)

    def clear(t, carry):
        d_w[at(t * WIDE, WIDE), :] = jnp.zeros((WIDE, 128), F32)
        return carry
    lax.fori_loop(0, DEPTH * (EPAIRS + 1), clear, 0)

    for copy in first_copies:
        copy.wait_recv()
    halo_place(wide_in, 5, 1, EXT, 1, EPAIRS, bufs0)

    def value_terms(i, j):
        q = -0.5
        total = base[inner(OBJ, j), :] * bias[DEPTH : DEPTH + 1]
        mid, half = base[inner(MID, j), :], base[inner(HALF, j), :]
        hs = [base[inner(n, j), :] for n in (H1, H2, H3)]
        qs = [base[inner(n, j), :] for n in (Q1, Q2, Q3)]
        t3 = tb[inner(0, j), :]
        if i == 0:
            total += q * softplus(-4.0 * hs[2] * t3)
            return total
        g0 = g_x[ext_inner(0, j), :]
        total += g0 * (mid - half) + q * softplus(-4.0 * half * g0)
        lams = [lam_x[ext_inner(0, j), :], lam_x[ext_inner(1, j), :], lam[inner(0, j), :]]
        mus = [mu_x[ext_inner(0, j), :], mu_x[ext_inner(1, j), :], mu[inner(0, j), :]]
        for m in range(DEPTH):
            g = g_x[ext_inner(m + 1, j), :] if m < 2 else mus[2] + t3
            total += q * softplus(-4.0 * hs[m] * g)
            total += q * softplus(-4.0 * hs[m] * (lams[m] - mus[m]))
            total += q * softplus(4.0 * qs[m] * lams[m])
            total -= lams[m] * bias[m : m + 1]
        return total

    def value_row(i):
        def step(j, acc):
            return acc + value_terms(i, j)
        acc = lax.fori_loop(0, PAIRS, step, jnp.zeros((ROWS, 128), F32))
        out = jnp.sum(acc, axis=0, keepdims=True)
        if i == 0:
            out = out - (0.5 * 0.6931471805599453 * 9 * ROWS * PAIRS)
        return out

    scale = None
    value_prev = jnp.zeros((1, 128), F32)
    totals = []
    for i in range(ITERS):
        first = i == 1

        def step_x(g, carry):
            before = list(carry)
            for u in range(3):
                e = 3 * g + u
                if i == 0:
                    xs = [wide_in[ext(n, e), :] for n in (MID, H1, H2)]
                    for m in range(2):
                        p_x[ext(m, e), :] = xs[m + 1]
                        dmu_x[ext(m, e), :] = xs[m + 1] - p_x[ext(m, e), :]
                    xs.append(wide_in[ext(OBJ, e), :])
                else:
                    halfs = [wide_in[ext(n, e), :] for n in (HALF, H1, H2)]
                    mids = [wide_in[ext(MID, e), :], halfs[1], halfs[2]]
                    xs = []
                    mus = []
                    for m in range(2):
                        new_mu = scale * dmu_x[ext(m, e), :]
                        new_lam = scale * d_w[pl.ds((m * (EPAIRS + 1) + e) * WIDE + 1, EXT), :]
                        if not first:
                            new_mu = mu_x[ext(m, e), :] + new_mu
                            new_lam = lam_x[ext(m, e), :] + new_lam
                        mu_x[ext(m, e), :] = new_mu
                        lam_x[ext(m, e), :] = new_lam
                        mus.append((new_mu, new_lam))
                    for k in range(DEPTH):
                        t = scale * upd[ext(k, e), :]
                        if not first:
                            t = trans[ext(k, e), :] + t
                        trans[ext(k, e), :] = t
                        coef = -t if k == 0 else mus[k - 1][0] - t
                        g_x[ext(k, e), :] = coef
                        xs.append(mids[k] - halfs[k] * jnp.tanh(2.0 * halfs[k] * coef))
                    for m in range(2):
                        h = halfs[m + 1]
                        p = h - h * jnp.tanh(2.0 * h * (mus[m][1] - mus[m][0]))
                        p_x[ext(m, e), :] = p
                        dmu_x[ext(m, e), :] = xs[m + 1] - p
                for k, x in enumerate(xs):
                    now = turn(x)
                    window(k, u, e, before[k], now)
                    before[k] = now
            return tuple(before)
        maps = LAYERS if i == 0 else DEPTH
        lax.fori_loop(0, EPAIRS // 3, step_x, tuple(jnp.zeros((EXT, 128), F32) for _ in range(maps)))

        acc = jnp.zeros((ROWS, 128), F32)
        if i == 0:
            back = conv(DEPTH, 3 + DEPTH)
            for j in range(PAIRS):
                tb[inner(0, j), :] = back[j * ROWS : (j + 1) * ROWS]
        for m in (2, 0, 1):
            rest = []
            for j in range(PAIRS):
                h = base[inner(H1 + m if m < 2 else H3, j), :]
                q = base[inner(Q1 + m, j), :]
                if m == 2:
                    t3 = tb[inner(0, j), :]
                    if i == 0:
                        p, v_lam = h, None
                    else:
                        new_mu = scale * dmu[inner(0, j), :]
                        v_lam = scale * dl[inner(2, j), :]
                        if not first:
                            new_mu = mu[inner(0, j), :] + new_mu
                            v_lam = lam[inner(0, j), :] + v_lam
                        mu[inner(0, j), :] = new_mu
                        lam[inner(0, j), :] = v_lam
                        p = h - h * jnp.tanh(2.0 * h * (v_lam - new_mu))
                        t3 = new_mu + t3
                    v = (h - h * jnp.tanh(2.0 * h * t3)) - p
                    dmu[inner(0, j), :] = v
                else:
                    p = p_x[ext_inner(m, j), :]
                    v_lam = None if i == 0 else lam_x[ext_inner(m, j), :]
                    v = dmu_x[ext_inner(m, j), :]
                acc = acc + v * v
                n = q if i == 0 else q + q * jnp.tanh(2.0 * q * v_lam)
                pn[inner(m, j), :] = p - n - bias[m : m + 1]
            image = conv(m, m)
            for j in range(PAIRS):
                v = pn[inner(m, j), :] - image[j * ROWS : (j + 1) * ROWS]
                dl[inner(m, j), :] = v
                d_w[pl.ds((m * (EPAIRS + 1) + j + 1) * WIDE + 2, ROWS), :] = v
                acc = acc + v * v
        sum_start(i, jnp.sum(acc, axis=0, keepdims=True), value_prev)

        copies = []
        if i < ITERS - 1:
            bufs = tuple(ref.at[i] for ref in (rows_s, cols_s, diag_s, rows_r, cols_r, diag_r))
            copies = halo_start(1 + i, dl, DEPTH, 2, bufs)
            sends += copies
        value_prev = value_row(i)
        if i == ITERS - 1:
            sum_start(ITERS, jnp.zeros((1, 128), F32), value_prev)
        sum_middle(i)
        if i < ITERS - 1:
            for copy in copies:
                copy.wait_recv()
            halo_place(d_w, DEPTH, 2, WIDE, 2, EPAIRS + 1, bufs)
            windows_wide()
            for m in range(DEPTH):
                conv_wide(m)
        else:
            sum_middle(ITERS)
        both = sum_end(i)
        squares = jnp.sum(both[0:1], axis=1, keepdims=True)
        scale = steps[i] / jnp.sqrt(squares / (2 * DEPTH * total_cells) + EPS)
        scale = jnp.broadcast_to(scale, (1, 128))
        totals.append(both)

    def finish(j, carry):
        lanes = pl.ds(pl.multiple_of(j * 128, 128), 128)
        for m in range(2):
            lam_out[m, :, lanes] = lam_x[ext_inner(m, j), :] + scale * dl[inner(m, j), :]
            mu_out[m, :, lanes] = mu_x[ext_inner(m, j), :] + scale * dmu_x[ext_inner(m, j), :]
        lam_out[2, :, lanes] = lam[inner(0, j), :] + scale * dl[inner(2, j), :]
        mu_out[2, :, lanes] = mu[inner(0, j), :] + scale * dmu[inner(0, j), :]
        return carry
    lax.fori_loop(0, PAIRS, finish, 0)
    totals.append(sum_end(ITERS))
    for i in range(ITERS):
        mean = jnp.sum(totals[i + 1][1:2], axis=1, keepdims=True) / total_cells
        bounds_ref[i : i + 1, :] = jnp.broadcast_to(mean, (1, 128))

    for copy in sends:
        copy.wait_send()
    for n in range(ITERS + 1):
        whole(buf_a, n, n_plane - 1, a_send, a_recv).wait_send()
        whole(buf_b, n, PLANES - 1, b_send, b_recv).wait_send()


def store(bounds_v, lam_v, mu_v, bounds_out, lam_out, mu_out, sem):
    copies = [pltpu.make_async_copy(lam_v, lam_out, sem.at[0]), pltpu.make_async_copy(mu_v, mu_out, sem.at[1])]
    for copy in copies:
        copy.start()
    for i in range(ITERS):
        bounds_out[i] = bounds_v[i, 0]
    for copy in copies:
        copy.wait()


def solution(mesh):
    n_row, n_col = mesh.shape["row"], mesh.shape["col"]
    n_plane = (n_row // PLANES) * n_col
    total_cells = n_row * n_col * ROWS * PAIRS * 128

    def vm(*shape, dtype=F32):
        return pltpu.VMEM(shape, dtype)

    inner_rows = PAIRS * ROWS
    ext_rows = EPAIRS * EXT
    lanes = PAIRS * 128
    hbm_spec = pl.BlockSpec(memory_space=pltpu.HBM)
    vmem_spec = pl.BlockSpec(memory_space=pltpu.VMEM)

    def kernel(*refs):
        body(float(total_cells), n_row, n_col, *refs)

    def shards(*args):
        call = pl.pallas_call(
            kernel,
            out_shape=(pltpu.VMEM((8, 128), F32),
                       pltpu.VMEM((DEPTH, ROWS, lanes), F32),
                       pltpu.VMEM((DEPTH, ROWS, lanes), F32)),
            in_specs=[hbm_spec] * 7 + [pl.BlockSpec(memory_space=pltpu.SMEM)],
            out_specs=(pl.BlockSpec(memory_space=pltpu.VMEM),
                       pl.BlockSpec(memory_space=pltpu.VMEM), pl.BlockSpec(memory_space=pltpu.VMEM)),
            scratch_shapes=[
                vm(ROWS, lanes), vm(ROWS, lanes, dtype=BF16), vm(ROWS, lanes, dtype=BF16),
                vm(DEPTH, ROWS, lanes, dtype=BF16), vm(DEPTH, ROWS, lanes, dtype=BF16),
                vm(LAYERS, 3, 3, CH, CH), vm(LAYERS, CH),
                vm(9 * inner_rows, 128), vm(5 * ext_rows, 128),
                vm(inner_rows, 128), vm(inner_rows, 128),
                vm(2 * ext_rows, 128), vm(2 * ext_rows, 128),
                vm(3 * inner_rows, 128), vm(inner_rows, 128), vm(2 * ext_rows, 128),
                vm(3 * ext_rows, 128), vm(3 * ext_rows, 128),
                vm(3 * ext_rows, 128), vm(2 * ext_rows, 128),
                vm(3 * inner_rows, 128), vm(inner_rows, 128),
                vm(3 * (EPAIRS + 1) * WIDE, 128),
                [vm(EXT, 128)] * 12, [vm(WIDE, 128)] * 9,
                vm(4, 2, 3, inner_rows + 2 * ROWS, 128, dtype=BF16), vm(3, 2, ext_rows, 768, dtype=BF16),
                vm(7, 768, 256, dtype=BF16),
                vm(2, 5, 1, PAIRS, 128), vm(2, 5, ROWS, 128), vm(4, 5, 1, 128),
                vm(2, 5, 1, PAIRS, 128), vm(2, 5, ROWS, 128), vm(4, 5, 1, 128),
                vm(2, 2, 3, 2, PAIRS, 128), vm(2, 2, 3, ROWS, 128), vm(2, 4, 3, 2, 128),
                vm(2, 2, 3, 2, PAIRS, 128), vm(2, 2, 3, ROWS, 128), vm(2, 4, 3, 2, 128),
                vm(ITERS + 1, 2, 128), vm(ITERS + 1, n_plane, 2, 128),
                vm(ITERS + 1, 2, 128), vm(ITERS + 1, PLANES, 2, 128),
                pltpu.SemaphoreType.DMA((7,)),
                pltpu.SemaphoreType.DMA((3, 8)), pltpu.SemaphoreType.DMA((3, 8)),
                pltpu.SemaphoreType.DMA((ITERS + 1,)), pltpu.SemaphoreType.DMA((ITERS + 1,)),
                pltpu.SemaphoreType.DMA((ITERS + 1,)), pltpu.SemaphoreType.DMA((ITERS + 1,)),
            ],
            compiler_params=pltpu.CompilerParams(
                collective_id=0, has_side_effects=True, vmem_limit_bytes=56 * 1024 * 1024),
            name="ascent",
        )
        results = call(*args)
        return pl.pallas_call(
            store,
            out_shape=(jax.ShapeDtypeStruct((ITERS,), F32),
                       jax.ShapeDtypeStruct((DEPTH, ROWS, lanes), F32),
                       jax.ShapeDtypeStruct((DEPTH, ROWS, lanes), F32)),
            in_specs=[vmem_spec] * 3,
            out_specs=(pl.BlockSpec(memory_space=pltpu.SMEM), hbm_spec, hbm_spec),
            scratch_shapes=[pltpu.SemaphoreType.DMA((2,))],
            compiler_params=pltpu.CompilerParams(vmem_limit_bytes=1024 * 1024),
            name="store",
        )(*results)

    placed = (P("row", "col"), P("row", "col"), P("row", "col"), P(None, "row", "col"), P(None, "row", "col"),
              P(), P(), P())
    return jax.shard_map(
        shards, mesh=mesh, in_specs=placed,
        out_specs=(P(), P(None, "row", "col"), P(None, "row", "col")), check_vma=False)
```

```python
import jax
import jax.numpy as jnp
from jax import lax
from jax.experimental import pallas as pl
from jax.experimental.pallas import tpu as pltpu
from jax.sharding import PartitionSpec as P

CH = 64
LAYERS = 4
ITERS = 3
DEPTH = LAYERS - 1
EPS = 1e-06
MESH = pl.DeviceIdType.MESH
F32 = jnp.float32
BF16 = jnp.bfloat16

ROWS = 16
PAIRS = 16
EXT = 24
EPAIRS = 18
WIDE = 32
PLANES = 8
MID, HALF, H1, H2, OBJ, H3, Q1, Q2, Q3 = range(9)
UP, DOWN, LEFT, RIGHT = range(4)
SIDES = ((-1, 0), (1, 0), (0, -1), (0, 1), (-1, -1), (-1, 1), (1, -1), (1, 1))


def at(start, size):
    return pl.ds(pl.multiple_of(start, 8), size)


def inner(which, pair):
    return at((which * PAIRS + pair) * ROWS, ROWS)


def ext(which, pair):
    return at((which * EPAIRS + pair) * EXT, EXT)


def ext_inner(which, pair):
    return pl.ds((which * EPAIRS + pair + 1) * EXT + 1, ROWS)


def split(v):
    hi = v.astype(BF16)
    return hi, (v - hi.astype(F32)).astype(BF16)


def body(total_cells, n_row, n_col, obj_h, cen_h, rad_h, low_h, upp_h, ker_h, bia_h, steps,
         bounds_ref, lam_out, mu_out,
         obj_v, cen_v, rad_v, low_v, upp_v, ker_v, bia_v,
         base, wide_in, lam, mu, lam_x, mu_x, dl, dmu, dmu_x, trans, upd, p_x, pn, tb,
         d_w, y_s, y_w, lhs_i, lhs_x, wts,
         rows_s0, cols_s0, diag_s0, rows_r0, cols_r0, diag_r0,
         rows_s, cols_s, diag_s, rows_r, cols_r, diag_r,
         pay, buf_plane, buf_line, buf_pair, buf_chip,
         load_sem, halo_send, halo_recv, sum_send, sum_recv):
    row = lax.axis_index("row")
    col = lax.axis_index("col")
    x_hi = row // PLANES
    z = row % PLANES
    place = x_hi * n_col + col

    ring = [[place_ for place_ in (at_, (at_ + 1) % size, (at_ + size - 1) % size)]
            for at_, size in ((row, n_row), (col, n_col))]

    def side_device(side):
        return (ring[0][side[0]], ring[1][side[1]])

    loads = []
    sends = []
    for n, (src, dst) in enumerate(((cen_h, cen_v), (rad_h, rad_v), (upp_h, upp_v), (obj_h, obj_v),
                                    (ker_h, ker_v), (low_h, low_v), (bia_h, bia_v))):
        copy = pltpu.make_async_copy(src, dst, load_sem.at[n])
        copy.start()
        loads.append(copy)

    barrier = pltpu.get_barrier_semaphore()
    greeted = 0
    for a in range(0, n_row, PLANES):
        for b in range(n_col):
            if a or b:
                pl.semaphore_signal(barrier, inc=1, device_id=(row ^ a if a else row, col ^ b if b else col),
                                    device_id_type=MESH)
                greeted += 1
    for a in range(1, PLANES):
        pl.semaphore_signal(barrier, inc=1, device_id=(row ^ a, col), device_id_type=MESH)
        greeted += 1
    for side in SIDES:
        if side[0] != 0:
            pl.semaphore_signal(barrier, inc=1, device_id=side_device(side), device_id_type=MESH)
            greeted += 1

    zero_tile = jnp.zeros((8, 128), F32)

    def halo_start(n, src_ref, maps, deep, bufs):
        rows_src, cols_src, diag_src, rows_dst, cols_dst, diag_dst = bufs
        for m in range(maps):
            first = m * PAIRS * ROWS
            for r in range(deep):
                rows_src[UP, m, r] = src_ref[pl.ds(first + r, PAIRS, stride=ROWS), :]
                rows_src[DOWN, m, r] = src_ref[pl.ds(first + ROWS - deep + r, PAIRS, stride=ROWS), :]
            cols_src[0, m] = src_ref[first : first + ROWS, :]
            cols_src[1, m] = src_ref[first + (PAIRS - 1) * ROWS : first + PAIRS * ROWS, :]
            last = first + (PAIRS - 1) * ROWS
            diag_src[0, m] = src_ref[first : first + deep, :]
            diag_src[1, m] = src_ref[last : last + deep, :]
            diag_src[2, m] = src_ref[first + ROWS - deep : first + ROWS, :]
            diag_src[3, m] = src_ref[last + ROWS - deep : last + ROWS, :]
        copies = []
        for s in (4, 5, 6, 7, 0, 1, 2, 3):
            if s < 2:
                src, dst = rows_src.at[s], rows_dst.at[s]
            elif s < 4:
                src, dst = cols_src.at[s - 2], cols_dst.at[s - 2]
            else:
                src, dst = diag_src.at[s - 4], diag_dst.at[s - 4]
            copy = pltpu.make_async_remote_copy(
                src_ref=src, dst_ref=dst, send_sem=halo_send.at[n, s], recv_sem=halo_recv.at[n, s],
                device_id=side_device(SIDES[s]), device_id_type=MESH)
            copy.start()
            copies.append(copy)
        return copies

    no_above = row == 0
    no_below = row == n_row - 1
    no_left = col == 0
    no_right = col == n_col - 1

    def halo_place(dst_ref, maps, deep, tall, top, pairs, bufs):
        _, _, _, rows_dst, cols_dst, diag_dst = bufs

        def cut(gone, v):
            return jnp.where(gone, 0.0, v)

        for m in range(maps):
            first = m * pairs * tall
            last = first + (EPAIRS - 1) * tall
            for r in range(deep):
                dst_ref[pl.ds(first + tall + top + ROWS + r, PAIRS, stride=tall), :] = cut(
                    no_below, rows_dst[0, m, r])
                dst_ref[pl.ds(first + tall + top - deep + r, PAIRS, stride=tall), :] = cut(
                    no_above, rows_dst[1, m, r])
            dst_ref[last + top : last + top + ROWS, :] = cut(no_right, cols_dst[0, m])
            dst_ref[first + top : first + top + ROWS, :] = cut(no_left, cols_dst[1, m])
            dst_ref[last + top + ROWS : last + top + ROWS + deep, :] = cut(
                jnp.logical_or(no_below, no_right), diag_dst[0, m])
            dst_ref[first + top + ROWS : first + top + ROWS + deep, :] = cut(
                jnp.logical_or(no_below, no_left), diag_dst[1, m])
            dst_ref[last + top - deep : last + top, :] = cut(
                jnp.logical_or(no_above, no_right), diag_dst[2, m])
            dst_ref[first + top - deep : first + top, :] = cut(
                jnp.logical_or(no_above, no_left), diag_dst[3, m])

    def far(d):
        lines, across = d
        z_, y_ = lines % PLANES, across // 4
        return -(min(z_, PLANES - z_) + 2 * (lines // PLANES) + min(y_, 4 - y_) + (across % 4) // 2)

    def order(row_steps, col_steps):
        steps = [(a, b) for a in row_steps for b in col_steps if a or b]
        return sorted(steps, key=far)

    pair_steps = order((0,), (0, 1))
    chip_steps = order(range(n_row), range(0, n_col, 2))
    plane_steps = order(range(0, n_row, PLANES), range(n_col))
    line_steps = order(range(PLANES), (0,))
    chip = row * (n_col // 2) + col // 2

    def stages(n):
        if n == 0:
            return ((plane_steps, buf_plane, place), (line_steps, buf_line, z))
        return ((pair_steps, buf_pair.at[n - 1], col % 2), (chip_steps, buf_chip.at[n - 1], chip))

    def exchange(n, stage, part):
        steps, buf, slot = stages(n)[stage]
        pay[n, stage] = part
        buf[slot] = part
        for a, b in steps:
            pltpu.make_async_remote_copy(
                src_ref=pay.at[n, stage], dst_ref=buf.at[slot],
                send_sem=sum_send.at[n, stage], recv_sem=sum_recv.at[n, stage],
                device_id=(row ^ a if a else row, col ^ b if b else col), device_id_type=MESH).start()

    def whole(n, stage):
        steps, buf, _ = stages(n)[stage]
        part = buf.at[0 : len(steps)]
        return pltpu.make_async_remote_copy(
            src_ref=part, dst_ref=part, send_sem=sum_send.at[n, stage], recv_sem=sum_recv.at[n, stage],
            device_id=side_device((0, 1)), device_id_type=MESH)

    def collect(n, stage):
        whole(n, stage).wait_recv()
        return jnp.sum(stages(n)[stage][1][...], axis=0)

    low_half = lax.broadcasted_iota(jnp.int32, (1, 128), 1) < CH

    def fold(v):
        return v + pltpu.roll(v, CH, 1)

    def sum_start(n, first_row, second_row):
        exchange(n, 0, jnp.where(low_half, fold(first_row), fold(second_row)))

    def sum_middle(n):
        exchange(n, 1, collect(n, 0))

    def sum_end(n):
        return collect(n, 1)

    lane = lax.broadcasted_iota(jnp.int32, (EXT, 128), 1) < CH
    lane_w = lax.broadcasted_iota(jnp.int32, (WIDE, 128), 1) < CH

    def turn(x):
        return pltpu.roll(x, CH, 1)

    def window(k, u, e, before, now):
        y = y_s[u * LAYERS + k]
        y[...] = jnp.where(lane, before, now)
        for dh in range(3):
            hi, lo = split(y[dh : dh + ROWS, :])
            rows = pl.ds(pl.multiple_of(e * ROWS, ROWS), ROWS)
            lhs_i[k, 0, dh, rows, :] = hi
            lhs_i[k, 1, dh, rows, :] = lo

    def conv(slot, weight):
        size = PAIRS * ROWS
        halves = []
        for part in range(2):
            tiles = []
            for dh in range(3):
                tiles.append(lhs_i[slot, part, dh, ROWS : size + ROWS, :])
                tiles.append(lhs_i[slot, part, dh, 2 * ROWS : size + 2 * ROWS, :])
            halves.append(jnp.concatenate(tiles, axis=1))
        high = jnp.dot(halves[0], wts[weight], preferred_element_type=F32)
        low = jnp.dot(halves[1], wts[weight, :, 0:128], preferred_element_type=F32)
        return (low + high[:, 128:]) + high[:, :128]

    def windows_wide():
        def wide(m, p):
            return turn(d_w[at((m * (EPAIRS + 1) + p) * WIDE, WIDE), :])

        none = jnp.zeros((WIDE, 128), F32)
        start = []
        for m in range(DEPTH):
            r = wide(m, 0)
            start += [r, jnp.where(lane_w, none, r)]

        def step(t, carry):
            out = []
            for m in range(DEPTH):
                r0, ya = carry[2 * m], carry[2 * m + 1]
                r1, r2 = wide(m, 2 * t + 1), wide(m, 2 * t + 2)
                yb = jnp.where(lane_w, r0, r1)
                yc = jnp.where(lane_w, r1, r2)
                for i, y in enumerate((ya, yb, yc)):
                    y_w[m * 3 + i][...] = y
                for dh in range(3):
                    ys = [y_w[m * 3 + i][dh : dh + EXT, :] for i in range(3)]
                    for half in range(2):
                        hi, lo = split(jnp.concatenate([ys[half], ys[half + 1]], axis=0))
                        rows = pl.ds(pl.multiple_of(t * 2 * EXT, 16), 2 * EXT)
                        lhs_x[m, 0, rows, (dh * 2 + half) * 128 : (dh * 2 + half + 1) * 128] = hi
                        lhs_x[m, 1, rows, (dh * 2 + half) * 128 : (dh * 2 + half + 1) * 128] = lo
                out += [r2, yc]
            return tuple(out)
        lax.fori_loop(0, EPAIRS // 2, step, tuple(start))

    def conv_wide(m):
        size = EPAIRS * EXT
        high = jnp.dot(lhs_x[m, 0], wts[3 + m], preferred_element_type=F32)
        low = jnp.dot(lhs_x[m, 1], wts[3 + m, :, 0:128], preferred_element_type=F32)
        upd[at(m * size, size), :] = (low + high[:, 128:]) + high[:, :128]

    for n in range(4):
        loads[n].wait()

    def fill(j, carry):
        lanes = pl.ds(pl.multiple_of(j * 128, 128), 128)
        c = cen_v[:, lanes].astype(F32)
        r = rad_v[:, lanes].astype(F32)
        lo, hi = c - r, c + r
        vals = {MID: 0.5 * (hi + lo), HALF: 0.5 * (hi - lo), OBJ: obj_v[:, lanes]}
        for m, name in enumerate((H1, H2, H3)):
            vals[name] = 0.5 * upp_v[m, :, lanes].astype(F32)
        for name, v in vals.items():
            base[inner(name, j), :] = v
            if name <= OBJ:
                wide_in[at((name * EPAIRS + j + 1) * EXT, 8), :] = zero_tile
                wide_in[at((name * EPAIRS + j + 1) * EXT + 16, 8), :] = zero_tile
                wide_in[ext_inner(name, j), :] = v
        return carry
    lax.fori_loop(0, PAIRS, fill, 0)
    for m in range(5):
        for e in (0, EPAIRS - 1):
            wide_in[ext(m, e), :] = jnp.zeros((EXT, 128), F32)

    pl.semaphore_wait(barrier, greeted)
    bufs0 = (rows_s0, cols_s0, diag_s0, rows_r0, cols_r0, diag_r0)
    first_copies = halo_start(0, base, 5, 1, bufs0)
    sends += first_copies

    for n in range(4, 7):
        loads[n].wait()

    def fill_low(j, carry):
        lanes = pl.ds(pl.multiple_of(j * 128, 128), 128)
        for m, name in enumerate((Q1, Q2, Q3)):
            base[inner(name, j), :] = 0.5 * low_v[m, :, lanes].astype(F32)
        return carry
    lax.fori_loop(0, PAIRS, fill_low, 0)

    bias = jnp.concatenate([bia_v[...], bia_v[...]], axis=1)
    none64 = jnp.zeros((CH, CH), F32)

    def put_weight(slot, dh, block):
        hi, lo = split(block)
        wts[slot, dh * 256 : (dh + 1) * 256, 0:128] = hi
        wts[slot, dh * 256 : (dh + 1) * 256, 128:256] = lo

    def build(k, carry):
        for dh in range(3):
            taps = [ker_v[k, 2 - dh, dw] for dw in range(3)]
            one = jnp.concatenate([jnp.concatenate([taps[2], taps[1]], axis=1),
                                   jnp.concatenate([none64, taps[2]], axis=1)], axis=0)
            two = jnp.concatenate([jnp.concatenate([taps[0], none64], axis=1),
                                   jnp.concatenate([taps[1], taps[0]], axis=1)], axis=0)
            put_weight(3 + k, dh, jnp.concatenate([one.T, two.T], axis=0))
        return carry
    lax.fori_loop(0, LAYERS, build, 0)

    def build_forward(k, carry):
        for dh in range(3):
            taps = [ker_v[k, dh, dw] for dw in range(3)]
            put_weight(k, dh, jnp.concatenate(
                [jnp.concatenate(taps + [none64], axis=0), jnp.concatenate([none64] + taps, axis=0)], axis=1))
        return carry
    lax.fori_loop(0, DEPTH, build_forward, 0)

    def clear(t, carry):
        d_w[at(t * WIDE, WIDE), :] = jnp.zeros((WIDE, 128), F32)
        return carry
    lax.fori_loop(0, DEPTH * (EPAIRS + 1), clear, 0)

    for copy in first_copies:
        copy.wait_recv()
    halo_place(wide_in, 5, 1, EXT, 1, EPAIRS, bufs0)

    def value_terms(i, j):
        total = base[inner(OBJ, j), :] * bias[DEPTH : DEPTH + 1]
        hs = [base[inner(n, j), :] for n in (H1, H2, H3)]
        t3 = tb[inner(0, j), :]
        args = []
        if i == 0:
            args.append(-4.0 * hs[2] * t3)
        else:
            mid, half = base[inner(MID, j), :], base[inner(HALF, j), :]
            qs = [base[inner(n, j), :] for n in (Q1, Q2, Q3)]
            g0 = -trans[ext_inner(0, j), :]
            total += g0 * (mid - half)
            args.append(-4.0 * half * g0)
            lams = [lam_x[ext_inner(0, j), :], lam_x[ext_inner(1, j), :], lam[inner(0, j), :]]
            mus = [mu_x[ext_inner(0, j), :], mu_x[ext_inner(1, j), :], mu[inner(0, j), :]]
            for m in range(DEPTH):
                g = mus[m] - trans[ext_inner(m + 1, j), :] if m < 2 else mus[2] + t3
                h4 = -4.0 * hs[m]
                args += [h4 * g, h4 * (lams[m] - mus[m]), 4.0 * qs[m] * lams[m]]
                total -= lams[m] * bias[m : m + 1]
        product = 1.0 + jnp.exp(-jnp.abs(args[0]))
        positive = jnp.maximum(args[0], 0.0)
        for arg in args[1:]:
            product = product * (1.0 + jnp.exp(-jnp.abs(arg)))
            positive = positive + jnp.maximum(arg, 0.0)
        return total - 0.5 * (positive + jnp.log(product))

    def value_row(i):
        def step(j, acc):
            return acc + value_terms(i, j)
        acc = lax.fori_loop(0, PAIRS, step, jnp.zeros((ROWS, 128), F32))
        out = jnp.sum(acc, axis=0, keepdims=True)
        if i == 0:
            out = out - (0.5 * 0.6931471805599453 * 9 * ROWS * PAIRS)
        return out

    scale = None
    value_prev = jnp.zeros((1, 128), F32)
    totals = []
    for i in range(ITERS):
        first = i == 1

        def step_x(g, carry):
            before = list(carry)
            for u in range(3):
                e = 3 * g + u
                if i == 0:
                    xs = [wide_in[ext(n, e), :] for n in (MID, H1, H2)]
                    for m in range(2):
                        p_x[ext(m, e), :] = xs[m + 1]
                        dmu_x[ext(m, e), :] = xs[m + 1] - p_x[ext(m, e), :]
                    xs.append(wide_in[ext(OBJ, e), :])
                else:
                    halfs = [wide_in[ext(n, e), :] for n in (HALF, H1, H2)]
                    mids = [wide_in[ext(MID, e), :], halfs[1], halfs[2]]
                    xs = []
                    mus = []
                    for m in range(2):
                        new_mu = scale * dmu_x[ext(m, e), :]
                        new_lam = scale * d_w[pl.ds((m * (EPAIRS + 1) + e) * WIDE + 1, EXT), :]
                        if not first:
                            new_mu = mu_x[ext(m, e), :] + new_mu
                            new_lam = lam_x[ext(m, e), :] + new_lam
                        mu_x[ext(m, e), :] = new_mu
                        lam_x[ext(m, e), :] = new_lam
                        mus.append((new_mu, new_lam))
                    for k in range(DEPTH):
                        t = scale * upd[ext(k, e), :]
                        if not first:
                            t = trans[ext(k, e), :] + t
                        trans[ext(k, e), :] = t
                        coef = -t if k == 0 else mus[k - 1][0] - t
                        xs.append(mids[k] - halfs[k] * jnp.tanh(2.0 * halfs[k] * coef))
                    for m in range(2):
                        h = halfs[m + 1]
                        p = h - h * jnp.tanh(2.0 * h * (mus[m][1] - mus[m][0]))
                        p_x[ext(m, e), :] = p
                        dmu_x[ext(m, e), :] = xs[m + 1] - p
                for k, x in enumerate(xs):
                    now = turn(x)
                    window(k, u, e, before[k], now)
                    before[k] = now
            return tuple(before)
        maps = LAYERS if i == 0 else DEPTH
        lax.fori_loop(0, EPAIRS // 3, step_x, tuple(jnp.zeros((EXT, 128), F32) for _ in range(maps)))

        acc = jnp.zeros((ROWS, 128), F32)
        if i == 0:
            back = conv(DEPTH, 3 + DEPTH)
            for j in range(PAIRS):
                tb[inner(0, j), :] = back[j * ROWS : (j + 1) * ROWS]
        for m in (2, 0, 1):
            rest = []
            for j in range(PAIRS):
                h = base[inner(H1 + m if m < 2 else H3, j), :]
                q = base[inner(Q1 + m, j), :]
                if m == 2:
                    t3 = tb[inner(0, j), :]
                    if i == 0:
                        p, v_lam = h, None
                    else:
                        new_mu = scale * dmu[inner(0, j), :]
                        v_lam = scale * dl[inner(2, j), :]
                        if not first:
                            new_mu = mu[inner(0, j), :] + new_mu
                            v_lam = lam[inner(0, j), :] + v_lam
                        mu[inner(0, j), :] = new_mu
                        lam[inner(0, j), :] = v_lam
                        p = h - h * jnp.tanh(2.0 * h * (v_lam - new_mu))
                        t3 = new_mu + t3
                    v = (h - h * jnp.tanh(2.0 * h * t3)) - p
                    dmu[inner(0, j), :] = v
                else:
                    p = p_x[ext_inner(m, j), :]
                    v_lam = None if i == 0 else lam_x[ext_inner(m, j), :]
                    v = dmu_x[ext_inner(m, j), :]
                acc = acc + v * v
                n = q if i == 0 else q + q * jnp.tanh(2.0 * q * v_lam)
                pn[inner(m, j), :] = p - n - bias[m : m + 1]
            image = conv(m, m)
            for j in range(PAIRS):
                v = pn[inner(m, j), :] - image[j * ROWS : (j + 1) * ROWS]
                dl[inner(m, j), :] = v
                d_w[pl.ds((m * (EPAIRS + 1) + j + 1) * WIDE + 2, ROWS), :] = v
                acc = acc + v * v
        sum_start(i, jnp.sum(acc, axis=0, keepdims=True), value_prev)

        copies = []
        if i < ITERS - 1:
            bufs = tuple(ref.at[i] for ref in (rows_s, cols_s, diag_s, rows_r, cols_r, diag_r))
            copies = halo_start(1 + i, dl, DEPTH, 2, bufs)
            sends += copies
        value_prev = value_row(i)
        if i == ITERS - 1:
            sum_start(ITERS, jnp.zeros((1, 128), F32), value_prev)
        sum_middle(i)
        if i < ITERS - 1:
            for copy in copies:
                copy.wait_recv()
            halo_place(d_w, DEPTH, 2, WIDE, 2, EPAIRS + 1, bufs)
            windows_wide()
            for m in range(DEPTH):
                conv_wide(m)
        else:
            sum_middle(ITERS)
        both = sum_end(i)
        squares = jnp.sum(jnp.where(low_half, both, 0.0), axis=1, keepdims=True)
        scale = steps[i] / jnp.sqrt(squares / (2 * DEPTH * total_cells) + EPS)
        scale = jnp.broadcast_to(scale, (1, 128))
        totals.append(both)

    def finish(j, carry):
        lanes = pl.ds(pl.multiple_of(j * 128, 128), 128)
        for m in range(2):
            lam_out[m, :, lanes] = lam_x[ext_inner(m, j), :] + scale * dl[inner(m, j), :]
            mu_out[m, :, lanes] = mu_x[ext_inner(m, j), :] + scale * dmu_x[ext_inner(m, j), :]
        lam_out[2, :, lanes] = lam[inner(0, j), :] + scale * dl[inner(2, j), :]
        mu_out[2, :, lanes] = mu[inner(0, j), :] + scale * dmu[inner(0, j), :]
        return carry
    lax.fori_loop(0, PAIRS, finish, 0)
    totals.append(sum_end(ITERS))
    for i in range(ITERS):
        mean = jnp.sum(jnp.where(low_half, 0.0, totals[i + 1]), axis=1, keepdims=True) / total_cells
        bounds_ref[i : i + 1, :] = jnp.broadcast_to(mean, (1, 128))

    for copy in sends:
        copy.wait_send()
    for n in range(ITERS + 1):
        for stage in range(2):
            whole(n, stage).wait_send()


def store(bounds_v, lam_v, mu_v, bounds_out, lam_out, mu_out, sem):
    copies = [pltpu.make_async_copy(lam_v, lam_out, sem.at[0]), pltpu.make_async_copy(mu_v, mu_out, sem.at[1])]
    for copy in copies:
        copy.start()
    for i in range(ITERS):
        bounds_out[i] = bounds_v[i, 0]
    for copy in copies:
        copy.wait()


def solution(mesh):
    n_row, n_col = mesh.shape["row"], mesh.shape["col"]
    n_plane = (n_row // PLANES) * n_col
    total_cells = n_row * n_col * ROWS * PAIRS * 128

    def vm(*shape, dtype=F32):
        return pltpu.VMEM(shape, dtype)

    inner_rows = PAIRS * ROWS
    ext_rows = EPAIRS * EXT
    lanes = PAIRS * 128
    hbm_spec = pl.BlockSpec(memory_space=pltpu.HBM)
    vmem_spec = pl.BlockSpec(memory_space=pltpu.VMEM)

    def kernel(*refs):
        body(float(total_cells), n_row, n_col, *refs)

    def shards(*args):
        call = pl.pallas_call(
            kernel,
            out_shape=(pltpu.VMEM((8, 128), F32),
                       pltpu.VMEM((DEPTH, ROWS, lanes), F32),
                       pltpu.VMEM((DEPTH, ROWS, lanes), F32)),
            in_specs=[hbm_spec] * 7 + [pl.BlockSpec(memory_space=pltpu.SMEM)],
            out_specs=(pl.BlockSpec(memory_space=pltpu.VMEM),
                       pl.BlockSpec(memory_space=pltpu.VMEM), pl.BlockSpec(memory_space=pltpu.VMEM)),
            scratch_shapes=[
                vm(ROWS, lanes), vm(ROWS, lanes, dtype=BF16), vm(ROWS, lanes, dtype=BF16),
                vm(DEPTH, ROWS, lanes, dtype=BF16), vm(DEPTH, ROWS, lanes, dtype=BF16),
                vm(LAYERS, 3, 3, CH, CH), vm(LAYERS, CH),
                vm(9 * inner_rows, 128), vm(5 * ext_rows, 128),
                vm(inner_rows, 128), vm(inner_rows, 128),
                vm(2 * ext_rows, 128), vm(2 * ext_rows, 128),
                vm(3 * inner_rows, 128), vm(inner_rows, 128), vm(2 * ext_rows, 128),
                vm(3 * ext_rows, 128), vm(3 * ext_rows, 128),
                vm(2 * ext_rows, 128),
                vm(3 * inner_rows, 128), vm(inner_rows, 128),
                vm(3 * (EPAIRS + 1) * WIDE, 128),
                [vm(EXT, 128)] * 12, [vm(WIDE, 128)] * 9,
                vm(4, 2, 3, inner_rows + 2 * ROWS, 128, dtype=BF16), vm(3, 2, ext_rows, 768, dtype=BF16),
                vm(7, 768, 256, dtype=BF16),
                vm(2, 5, 1, PAIRS, 128), vm(2, 5, ROWS, 128), vm(4, 5, 1, 128),
                vm(2, 5, 1, PAIRS, 128), vm(2, 5, ROWS, 128), vm(4, 5, 1, 128),
                vm(2, 2, 3, 2, PAIRS, 128), vm(2, 2, 3, ROWS, 128), vm(2, 4, 3, 2, 128),
                vm(2, 2, 3, 2, PAIRS, 128), vm(2, 2, 3, ROWS, 128), vm(2, 4, 3, 2, 128),
                vm(ITERS + 1, 2, 1, 128), vm(n_plane, 1, 128), vm(PLANES, 1, 128),
                vm(ITERS, 2, 1, 128), vm(ITERS, n_row * n_col // 2, 1, 128),
                pltpu.SemaphoreType.DMA((7,)),
                pltpu.SemaphoreType.DMA((3, 8)), pltpu.SemaphoreType.DMA((3, 8)),
                pltpu.SemaphoreType.DMA((ITERS + 1, 2)), pltpu.SemaphoreType.DMA((ITERS + 1, 2)),
            ],
            compiler_params=pltpu.CompilerParams(
                collective_id=0, has_side_effects=True, vmem_limit_bytes=56 * 1024 * 1024),
            name="ascent",
        )
        results = call(*args)
        return pl.pallas_call(
            store,
            out_shape=(jax.ShapeDtypeStruct((ITERS,), F32),
                       jax.ShapeDtypeStruct((DEPTH, ROWS, lanes), F32),
                       jax.ShapeDtypeStruct((DEPTH, ROWS, lanes), F32)),
            in_specs=[vmem_spec] * 3,
            out_specs=(pl.BlockSpec(memory_space=pltpu.SMEM), hbm_spec, hbm_spec),
            scratch_shapes=[pltpu.SemaphoreType.DMA((2,))],
            compiler_params=pltpu.CompilerParams(vmem_limit_bytes=1024 * 1024),
            name="store",
        )(*results)

    placed = (P("row", "col"), P("row", "col"), P("row", "col"), P(None, "row", "col"), P(None, "row", "col"),
              P(), P(), P())
    return jax.shard_map(
        shards, mesh=mesh, in_specs=placed,
        out_specs=(P(), P(None, "row", "col"), P(None, "row", "col")), check_vma=False)
```

```python
import jax
import jax.numpy as jnp
from jax import lax
from jax.experimental import pallas as pl
from jax.experimental.pallas import tpu as pltpu
from jax.sharding import PartitionSpec as P

CH = 64
LAYERS = 4
ITERS = 3
DEPTH = LAYERS - 1
EPS = 1e-06
MESH = pl.DeviceIdType.MESH
F32 = jnp.float32
BF16 = jnp.bfloat16

ROWS = 16
PAIRS = 16
EXT = 24
EPAIRS = 18
WIDE = 32
PLANES = 8
MID, HALF, H1, H2, OBJ, H3, Q1, Q2, Q3 = range(9)
UP, DOWN, LEFT, RIGHT = range(4)
SIDES = ((-1, 0), (1, 0), (0, -1), (0, 1), (-1, -1), (-1, 1), (1, -1), (1, 1))


def at(start, size):
    return pl.ds(pl.multiple_of(start, 8), size)


def inner(which, pair):
    return at((which * PAIRS + pair) * ROWS, ROWS)


def ext(which, pair):
    return at((which * EPAIRS + pair) * EXT, EXT)


def ext_inner(which, pair):
    return pl.ds((which * EPAIRS + pair + 1) * EXT + 1, ROWS)


def split(v):
    hi = v.astype(BF16)
    return hi, (v - hi.astype(F32)).astype(BF16)


def body(total_cells, n_row, n_col, obj_h, cen_h, rad_h, low_h, upp_h, ker_h, bia_h, steps,
         bounds_ref, lam_out, mu_out,
         obj_v, cen_v, rad_v, low_v, upp_v, ker_v, bia_v,
         base, wide_in, lam, mu, lam_x, mu_x, dl, dmu, dmu_x, trans, upd, p_x, pn, tb,
         d_w, y_s, y_w, lhs_i, lhs_x, wts,
         rows_s0, cols_s0, diag_s0, rows_r0, cols_r0, diag_r0,
         rows_s, cols_s, diag_s, rows_r, cols_r, diag_r,
         pay, buf_plane, buf_line, buf_pair, buf_chip,
         load_sem, halo_send, halo_recv, sum_send, sum_recv):
    row = lax.axis_index("row")
    col = lax.axis_index("col")
    x_hi = row // PLANES
    z = row % PLANES
    place = x_hi * n_col + col

    ring = [[place_ for place_ in (at_, (at_ + 1) % size, (at_ + size - 1) % size)]
            for at_, size in ((row, n_row), (col, n_col))]

    def side_device(side):
        return (ring[0][side[0]], ring[1][side[1]])

    loads = []
    sends = []
    for n, (src, dst) in enumerate(((cen_h, cen_v), (rad_h, rad_v), (upp_h, upp_v), (obj_h, obj_v),
                                    (ker_h, ker_v), (low_h, low_v), (bia_h, bia_v))):
        copy = pltpu.make_async_copy(src, dst, load_sem.at[n])
        copy.start()
        loads.append(copy)

    barrier = pltpu.get_barrier_semaphore()
    greeted = 0
    for a in range(0, n_row, PLANES):
        for b in range(n_col):
            if a or b:
                pl.semaphore_signal(barrier, inc=1, device_id=(row ^ a if a else row, col ^ b if b else col),
                                    device_id_type=MESH)
                greeted += 1
    for a in range(1, PLANES):
        pl.semaphore_signal(barrier, inc=1, device_id=(row ^ a, col), device_id_type=MESH)
        greeted += 1
    for side in SIDES:
        if side[0] != 0:
            pl.semaphore_signal(barrier, inc=1, device_id=side_device(side), device_id_type=MESH)
            greeted += 1

    zero_tile = jnp.zeros((8, 128), F32)

    def halo_start(n, src_ref, maps, deep, bufs):
        rows_src, cols_src, diag_src, rows_dst, cols_dst, diag_dst = bufs
        for m in range(maps):
            first = m * PAIRS * ROWS
            for r in range(deep):
                rows_src[UP, m, r] = src_ref[pl.ds(first + r, PAIRS, stride=ROWS), :]
                rows_src[DOWN, m, r] = src_ref[pl.ds(first + ROWS - deep + r, PAIRS, stride=ROWS), :]
            cols_src[0, m] = src_ref[first : first + ROWS, :]
            cols_src[1, m] = src_ref[first + (PAIRS - 1) * ROWS : first + PAIRS * ROWS, :]
            last = first + (PAIRS - 1) * ROWS
            diag_src[0, m] = src_ref[first : first + deep, :]
            diag_src[1, m] = src_ref[last : last + deep, :]
            diag_src[2, m] = src_ref[first + ROWS - deep : first + ROWS, :]
            diag_src[3, m] = src_ref[last + ROWS - deep : last + ROWS, :]
        copies = []
        for s in (4, 5, 6, 7, 0, 1, 2, 3):
            if s < 2:
                src, dst = rows_src.at[s], rows_dst.at[s]
            elif s < 4:
                src, dst = cols_src.at[s - 2], cols_dst.at[s - 2]
            else:
                src, dst = diag_src.at[s - 4], diag_dst.at[s - 4]
            copy = pltpu.make_async_remote_copy(
                src_ref=src, dst_ref=dst, send_sem=halo_send.at[n, s], recv_sem=halo_recv.at[n, s],
                device_id=side_device(SIDES[s]), device_id_type=MESH)
            copy.start()
            copies.append(copy)
        return copies

    no_above = row == 0
    no_below = row == n_row - 1
    no_left = col == 0
    no_right = col == n_col - 1

    def halo_place(dst_ref, maps, deep, tall, top, pairs, bufs):
        _, _, _, rows_dst, cols_dst, diag_dst = bufs

        def cut(gone, v):
            return jnp.where(gone, 0.0, v)

        for m in range(maps):
            first = m * pairs * tall
            last = first + (EPAIRS - 1) * tall
            for r in range(deep):
                dst_ref[pl.ds(first + tall + top + ROWS + r, PAIRS, stride=tall), :] = cut(
                    no_below, rows_dst[0, m, r])
                dst_ref[pl.ds(first + tall + top - deep + r, PAIRS, stride=tall), :] = cut(
                    no_above, rows_dst[1, m, r])
            dst_ref[last + top : last + top + ROWS, :] = cut(no_right, cols_dst[0, m])
            dst_ref[first + top : first + top + ROWS, :] = cut(no_left, cols_dst[1, m])
            dst_ref[last + top + ROWS : last + top + ROWS + deep, :] = cut(
                jnp.logical_or(no_below, no_right), diag_dst[0, m])
            dst_ref[first + top + ROWS : first + top + ROWS + deep, :] = cut(
                jnp.logical_or(no_below, no_left), diag_dst[1, m])
            dst_ref[last + top - deep : last + top, :] = cut(
                jnp.logical_or(no_above, no_right), diag_dst[2, m])
            dst_ref[first + top - deep : first + top, :] = cut(
                jnp.logical_or(no_above, no_left), diag_dst[3, m])

    def far(d):
        lines, across = d
        z_, y_ = lines % PLANES, across // 4
        return -(min(z_, PLANES - z_) + 2 * (lines // PLANES) + min(y_, 4 - y_) + (across % 4) // 2)

    def order(row_steps, col_steps):
        steps = [(a, b) for a in row_steps for b in col_steps if a or b]
        return sorted(steps, key=far)

    pair_steps = order((0,), (0, 1))
    chip_steps = order(range(n_row), range(0, n_col, 2))
    plane_steps = order(range(0, n_row, PLANES), range(n_col))
    line_steps = order(range(PLANES), (0,))
    chip = row * (n_col // 2) + col // 2

    def stages(n):
        if n == 0:
            return ((plane_steps, buf_plane, place), (line_steps, buf_line, z))
        return ((pair_steps, buf_pair.at[n - 1], col % 2), (chip_steps, buf_chip.at[n - 1], chip))

    def exchange(n, stage, part):
        steps, buf, slot = stages(n)[stage]
        pay[n, stage] = part
        buf[slot] = part
        for a, b in steps:
            pltpu.make_async_remote_copy(
                src_ref=pay.at[n, stage], dst_ref=buf.at[slot],
                send_sem=sum_send.at[n, stage], recv_sem=sum_recv.at[n, stage],
                device_id=(row ^ a if a else row, col ^ b if b else col), device_id_type=MESH).start()

    def whole(n, stage):
        steps, buf, _ = stages(n)[stage]
        part = buf.at[0 : len(steps)]
        return pltpu.make_async_remote_copy(
            src_ref=part, dst_ref=part, send_sem=sum_send.at[n, stage], recv_sem=sum_recv.at[n, stage],
            device_id=side_device((0, 1)), device_id_type=MESH)

    def collect(n, stage):
        whole(n, stage).wait_recv()
        return jnp.sum(stages(n)[stage][1][...], axis=0)

    low_half = lax.broadcasted_iota(jnp.int32, (1, 128), 1) < CH

    def fold(v):
        return v + pltpu.roll(v, CH, 1)

    def sum_start(n, first_row, second_row):
        exchange(n, 0, jnp.where(low_half, fold(first_row), fold(second_row)))

    def sum_middle(n):
        exchange(n, 1, collect(n, 0))

    def sum_end(n):
        return collect(n, 1)

    lane = lax.broadcasted_iota(jnp.int32, (EXT, 128), 1) < CH
    lane_w = lax.broadcasted_iota(jnp.int32, (WIDE, 128), 1) < CH

    def turn(x):
        return pltpu.roll(x, CH, 1)

    def window(k, u, e, before, now):
        y = y_s[u * LAYERS + k]
        y[...] = jnp.where(lane, before, now)
        for dh in range(3):
            hi, lo = split(y[dh : dh + ROWS, :])
            rows = pl.ds(pl.multiple_of(e * ROWS, ROWS), ROWS)
            lhs_i[k, 0, dh, rows, :] = hi
            lhs_i[k, 1, dh, rows, :] = lo

    def conv(slot, weight):
        size = PAIRS * ROWS
        halves = []
        for part in range(2):
            tiles = []
            for dh in range(3):
                tiles.append(lhs_i[slot, part, dh, ROWS : size + ROWS, :])
                tiles.append(lhs_i[slot, part, dh, 2 * ROWS : size + 2 * ROWS, :])
            halves.append(jnp.concatenate(tiles, axis=1))
        return product(halves[0], halves[1], weight)

    def product(hi, lo, weight):
        high = jnp.dot(hi, wts[weight], preferred_element_type=F32)
        low = jnp.dot(lo, wts[weight, :, 0:128], preferred_element_type=F32)
        return (low + high[:, 128:]) + high[:, :128]

    def rim(which, weight, scratch):
        lane_r = lane[0:ROWS]
        none = jnp.zeros((ROWS, 128), F32)
        start = which * EPAIRS * EXT
        sides = []
        for s in (0, ROWS + 1):
            x = [turn(wide_in[pl.ds(start + k * EXT + s, PAIRS, stride=EXT), :]) for k in range(3)]
            sides.append([jnp.where(lane_r, x[0], x[1]), jnp.where(lane_r, x[1], x[2])])
        left = jnp.where(lane_r, turn(wide_in[pl.ds(start + 1, ROWS), :]), none)
        right = jnp.where(lane_r, none, turn(wide_in[pl.ds(start + (EPAIRS - 1) * EXT + 1, ROWS), :]))
        for y, v in zip(scratch, (left, right)):
            y[0:8, :] = zero_tile
            y[16:24, :] = zero_tile
            y[1 : ROWS + 1, :] = v
        blocks = [sides[0] + [none] * 4, [none] * 4 + sides[1], [], []]
        for dh in range(3):
            blocks[2] += [scratch[0][dh : dh + ROWS, :], none]
            blocks[3] += [none, scratch[1][dh : dh + ROWS, :]]
        parts = [split(jnp.concatenate([b[k] for b in blocks], axis=0)) for k in range(6)]
        return product(jnp.concatenate([p[0] for p in parts], axis=1),
                       jnp.concatenate([p[1] for p in parts], axis=1), weight)

    def add_rim(dst, first, v):
        for at_, stride, k in ((0, ROWS, 0), (ROWS - 1, ROWS, 1)):
            rows = pl.ds(first + at_, PAIRS, stride=stride)
            dst[rows, :] = dst[rows, :] + v[k * ROWS : (k + 1) * ROWS]
        for pair, k in ((0, 2), (PAIRS - 1, 3)):
            rows = pl.ds(first + pair * ROWS, ROWS)
            dst[rows, :] = dst[rows, :] + v[k * ROWS : (k + 1) * ROWS]

    def windows_wide():
        def wide(m, p):
            return turn(d_w[at((m * (EPAIRS + 1) + p) * WIDE, WIDE), :])

        none = jnp.zeros((WIDE, 128), F32)
        start = []
        for m in range(DEPTH):
            r = wide(m, 0)
            start += [r, jnp.where(lane_w, none, r)]

        def step(t, carry):
            out = []
            for m in range(DEPTH):
                r0, ya = carry[2 * m], carry[2 * m + 1]
                r1, r2 = wide(m, 2 * t + 1), wide(m, 2 * t + 2)
                yb = jnp.where(lane_w, r0, r1)
                yc = jnp.where(lane_w, r1, r2)
                for i, y in enumerate((ya, yb, yc)):
                    y_w[m * 3 + i][...] = y
                for dh in range(3):
                    ys = [y_w[m * 3 + i][dh : dh + EXT, :] for i in range(3)]
                    for half in range(2):
                        hi, lo = split(jnp.concatenate([ys[half], ys[half + 1]], axis=0))
                        rows = pl.ds(pl.multiple_of(t * 2 * EXT, 16), 2 * EXT)
                        lhs_x[m, 0, rows, (dh * 2 + half) * 128 : (dh * 2 + half + 1) * 128] = hi
                        lhs_x[m, 1, rows, (dh * 2 + half) * 128 : (dh * 2 + half + 1) * 128] = lo
                out += [r2, yc]
            return tuple(out)
        lax.fori_loop(0, EPAIRS // 2, step, tuple(start))

    def conv_wide(m):
        size = EPAIRS * EXT
        high = jnp.dot(lhs_x[m, 0], wts[3 + m], preferred_element_type=F32)
        low = jnp.dot(lhs_x[m, 1], wts[3 + m, :, 0:128], preferred_element_type=F32)
        upd[at(m * size, size), :] = (low + high[:, 128:]) + high[:, :128]

    for n in range(4):
        loads[n].wait()

    def fill(j, carry):
        lanes = pl.ds(pl.multiple_of(j * 128, 128), 128)
        c = cen_v[:, lanes].astype(F32)
        r = rad_v[:, lanes].astype(F32)
        lo, hi = c - r, c + r
        vals = {MID: 0.5 * (hi + lo), HALF: 0.5 * (hi - lo), OBJ: obj_v[:, lanes]}
        for m, name in enumerate((H1, H2, H3)):
            vals[name] = 0.5 * upp_v[m, :, lanes].astype(F32)
        for name, v in vals.items():
            base[inner(name, j), :] = v
            if name <= OBJ:
                wide_in[at((name * EPAIRS + j + 1) * EXT, 8), :] = zero_tile
                wide_in[at((name * EPAIRS + j + 1) * EXT + 16, 8), :] = zero_tile
                wide_in[ext_inner(name, j), :] = v
        return carry
    lax.fori_loop(0, PAIRS, fill, 0)
    for m in range(5):
        for e in (0, EPAIRS - 1):
            wide_in[ext(m, e), :] = jnp.zeros((EXT, 128), F32)

    pl.semaphore_wait(barrier, greeted)
    bufs0 = (rows_s0, cols_s0, diag_s0, rows_r0, cols_r0, diag_r0)
    first_copies = halo_start(0, base, 5, 1, bufs0)
    sends += first_copies

    for n in range(4, 7):
        loads[n].wait()

    def fill_low(j, carry):
        lanes = pl.ds(pl.multiple_of(j * 128, 128), 128)
        for m, name in enumerate((Q1, Q2, Q3)):
            base[inner(name, j), :] = 0.5 * low_v[m, :, lanes].astype(F32)
        return carry
    lax.fori_loop(0, PAIRS, fill_low, 0)

    bias = jnp.concatenate([bia_v[...], bia_v[...]], axis=1)
    none64 = jnp.zeros((CH, CH), F32)

    def put_weight(slot, dh, block):
        hi, lo = split(block)
        wts[slot, dh * 256 : (dh + 1) * 256, 0:128] = hi
        wts[slot, dh * 256 : (dh + 1) * 256, 128:256] = lo

    def build(k, carry):
        for dh in range(3):
            taps = [ker_v[k, 2 - dh, dw] for dw in range(3)]
            one = jnp.concatenate([jnp.concatenate([taps[2], taps[1]], axis=1),
                                   jnp.concatenate([none64, taps[2]], axis=1)], axis=0)
            two = jnp.concatenate([jnp.concatenate([taps[0], none64], axis=1),
                                   jnp.concatenate([taps[1], taps[0]], axis=1)], axis=0)
            put_weight(3 + k, dh, jnp.concatenate([one.T, two.T], axis=0))
        return carry
    lax.fori_loop(0, LAYERS, build, 0)

    def build_forward(k, carry):
        for dh in range(3):
            taps = [ker_v[k, dh, dw] for dw in range(3)]
            put_weight(k, dh, jnp.concatenate(
                [jnp.concatenate(taps + [none64], axis=0), jnp.concatenate([none64] + taps, axis=0)], axis=1))
        return carry
    lax.fori_loop(0, DEPTH, build_forward, 0)

    def clear(t, carry):
        d_w[at(t * WIDE, WIDE), :] = jnp.zeros((WIDE, 128), F32)
        return carry
    lax.fori_loop(0, DEPTH * (EPAIRS + 1), clear, 0)

    def value_terms(i, j):
        total = base[inner(OBJ, j), :] * bias[DEPTH : DEPTH + 1]
        hs = [base[inner(n, j), :] for n in (H1, H2, H3)]
        t3 = tb[inner(0, j), :]
        args = []
        if i == 0:
            args.append(-4.0 * hs[2] * t3)
        else:
            mid, half = base[inner(MID, j), :], base[inner(HALF, j), :]
            qs = [base[inner(n, j), :] for n in (Q1, Q2, Q3)]
            g0 = -trans[ext_inner(0, j), :]
            total += g0 * (mid - half)
            args.append(-4.0 * half * g0)
            lams = [lam_x[ext_inner(0, j), :], lam_x[ext_inner(1, j), :], lam[inner(0, j), :]]
            mus = [mu_x[ext_inner(0, j), :], mu_x[ext_inner(1, j), :], mu[inner(0, j), :]]
            for m in range(DEPTH):
                g = mus[m] - trans[ext_inner(m + 1, j), :] if m < 2 else mus[2] + t3
                h4 = -4.0 * hs[m]
                args += [h4 * g, h4 * (lams[m] - mus[m]), 4.0 * qs[m] * lams[m]]
                total -= lams[m] * bias[m : m + 1]
        product = 1.0 + jnp.exp(-jnp.abs(args[0]))
        positive = jnp.maximum(args[0], 0.0)
        for arg in args[1:]:
            product = product * (1.0 + jnp.exp(-jnp.abs(arg)))
            positive = positive + jnp.maximum(arg, 0.0)
        return total - 0.5 * (positive + jnp.log(product))

    def value_row(i):
        def step(j, acc):
            return acc + value_terms(i, j)
        acc = lax.fori_loop(0, PAIRS, step, jnp.zeros((ROWS, 128), F32))
        out = jnp.sum(acc, axis=0, keepdims=True)
        if i == 0:
            out = out - (0.5 * 0.6931471805599453 * 9 * ROWS * PAIRS)
        return out

    scale = None
    value_prev = jnp.zeros((1, 128), F32)
    totals = []
    for i in range(ITERS):
        first = i == 1

        def step_x(g, carry):
            before = list(carry)
            for u in range(3):
                e = 3 * g + u
                if i == 0:
                    xs = [wide_in[ext(n, e), :] for n in (MID, H1, H2)]
                    for m in range(2):
                        p_x[ext(m, e), :] = xs[m + 1]
                        dmu_x[ext(m, e), :] = xs[m + 1] - p_x[ext(m, e), :]
                    xs.append(wide_in[ext(OBJ, e), :])
                else:
                    halfs = [wide_in[ext(n, e), :] for n in (HALF, H1, H2)]
                    mids = [wide_in[ext(MID, e), :], halfs[1], halfs[2]]
                    xs = []
                    mus = []
                    for m in range(2):
                        new_mu = scale * dmu_x[ext(m, e), :]
                        new_lam = scale * d_w[pl.ds((m * (EPAIRS + 1) + e) * WIDE + 1, EXT), :]
                        if not first:
                            new_mu = mu_x[ext(m, e), :] + new_mu
                            new_lam = lam_x[ext(m, e), :] + new_lam
                        mu_x[ext(m, e), :] = new_mu
                        lam_x[ext(m, e), :] = new_lam
                        mus.append((new_mu, new_lam))
                    for k in range(DEPTH):
                        t = scale * upd[ext(k, e), :]
                        if not first:
                            t = trans[ext(k, e), :] + t
                        trans[ext(k, e), :] = t
                        coef = -t if k == 0 else mus[k - 1][0] - t
                        xs.append(mids[k] - halfs[k] * jnp.tanh(2.0 * halfs[k] * coef))
                    for m in range(2):
                        h = halfs[m + 1]
                        p = h - h * jnp.tanh(2.0 * h * (mus[m][1] - mus[m][0]))
                        p_x[ext(m, e), :] = p
                        dmu_x[ext(m, e), :] = xs[m + 1] - p
                for k, x in enumerate(xs):
                    now = turn(x)
                    window(k, u, e, before[k], now)
                    before[k] = now
            return tuple(before)
        maps = LAYERS if i == 0 else DEPTH
        lax.fori_loop(0, EPAIRS // 3, step_x, tuple(jnp.zeros((EXT, 128), F32) for _ in range(maps)))

        acc = jnp.zeros((ROWS, 128), F32)
        if i == 0:
            for m in range(DEPTH):
                image = conv(m, m)
                for j in range(PAIRS):
                    dl[inner(m, j), :] = image[j * ROWS : (j + 1) * ROWS]
            image = conv(DEPTH, 3 + DEPTH)
            for j in range(PAIRS):
                tb[inner(0, j), :] = image[j * ROWS : (j + 1) * ROWS]
            for copy in first_copies:
                copy.wait_recv()
            halo_place(wide_in, 5, 1, EXT, 1, EPAIRS, bufs0)
            add_rim(tb, 0, rim(OBJ, 3 + DEPTH, y_s[0:2]))
            for m in range(DEPTH):
                add_rim(dl, m * PAIRS * ROWS, rim((MID, H1, H2)[m], m, y_s[2 * m + 2 : 2 * m + 4]))
            for j in range(PAIRS):
                for m in range(DEPTH):
                    h = base[inner(H1 + m if m < 2 else H3, j), :]
                    p = h if m == 2 else p_x[ext_inner(m, j), :]
                    if m == 2:
                        v = (h - h * jnp.tanh(2.0 * h * tb[inner(0, j), :])) - p
                        dmu[inner(0, j), :] = v
                    else:
                        v = dmu_x[ext_inner(m, j), :]
                    acc = acc + v * v
                    v = (p - base[inner(Q1 + m, j), :] - bias[m : m + 1]) - dl[inner(m, j), :]
                    dl[inner(m, j), :] = v
                    d_w[pl.ds((m * (EPAIRS + 1) + j + 1) * WIDE + 2, ROWS), :] = v
                    acc = acc + v * v
        else:
            for m in (2, 0, 1):
                for j in range(PAIRS):
                    h = base[inner(H1 + m if m < 2 else H3, j), :]
                    q = base[inner(Q1 + m, j), :]
                    if m == 2:
                        new_mu = scale * dmu[inner(0, j), :]
                        v_lam = scale * dl[inner(2, j), :]
                        if not first:
                            new_mu = mu[inner(0, j), :] + new_mu
                            v_lam = lam[inner(0, j), :] + v_lam
                        mu[inner(0, j), :] = new_mu
                        lam[inner(0, j), :] = v_lam
                        p = h - h * jnp.tanh(2.0 * h * (v_lam - new_mu))
                        t3 = new_mu + tb[inner(0, j), :]
                        v = (h - h * jnp.tanh(2.0 * h * t3)) - p
                        dmu[inner(0, j), :] = v
                    else:
                        p = p_x[ext_inner(m, j), :]
                        v_lam = lam_x[ext_inner(m, j), :]
                        v = dmu_x[ext_inner(m, j), :]
                    acc = acc + v * v
                    n = q + q * jnp.tanh(2.0 * q * v_lam)
                    pn[inner(m, j), :] = p - n - bias[m : m + 1]
                image = conv(m, m)
                for j in range(PAIRS):
                    v = pn[inner(m, j), :] - image[j * ROWS : (j + 1) * ROWS]
                    dl[inner(m, j), :] = v
                    d_w[pl.ds((m * (EPAIRS + 1) + j + 1) * WIDE + 2, ROWS), :] = v
                    acc = acc + v * v
        sum_start(i, jnp.sum(acc, axis=0, keepdims=True), value_prev)

        copies = []
        if i < ITERS - 1:
            bufs = tuple(ref.at[i] for ref in (rows_s, cols_s, diag_s, rows_r, cols_r, diag_r))
            copies = halo_start(1 + i, dl, DEPTH, 2, bufs)
            sends += copies
        value_prev = value_row(i)
        if i == ITERS - 1:
            sum_start(ITERS, jnp.zeros((1, 128), F32), value_prev)
        sum_middle(i)
        if i < ITERS - 1:
            for copy in copies:
                copy.wait_recv()
            halo_place(d_w, DEPTH, 2, WIDE, 2, EPAIRS + 1, bufs)
            windows_wide()
            for m in range(DEPTH):
                conv_wide(m)
        else:
            sum_middle(ITERS)
        both = sum_end(i)
        squares = jnp.sum(jnp.where(low_half, both, 0.0), axis=1, keepdims=True)
        scale = steps[i] / jnp.sqrt(squares / (2 * DEPTH * total_cells) + EPS)
        scale = jnp.broadcast_to(scale, (1, 128))
        totals.append(both)

    def finish(j, carry):
        lanes = pl.ds(pl.multiple_of(j * 128, 128), 128)
        for m in range(2):
            lam_out[m, :, lanes] = lam_x[ext_inner(m, j), :] + scale * dl[inner(m, j), :]
            mu_out[m, :, lanes] = mu_x[ext_inner(m, j), :] + scale * dmu_x[ext_inner(m, j), :]
        lam_out[2, :, lanes] = lam[inner(0, j), :] + scale * dl[inner(2, j), :]
        mu_out[2, :, lanes] = mu[inner(0, j), :] + scale * dmu[inner(0, j), :]
        return carry
    lax.fori_loop(0, PAIRS, finish, 0)
    totals.append(sum_end(ITERS))
    for i in range(ITERS):
        mean = jnp.sum(jnp.where(low_half, 0.0, totals[i + 1]), axis=1, keepdims=True) / total_cells
        bounds_ref[i : i + 1, :] = jnp.broadcast_to(mean, (1, 128))

    for copy in sends:
        copy.wait_send()
    for n in range(ITERS + 1):
        for stage in range(2):
            whole(n, stage).wait_send()


def store(bounds_v, lam_v, mu_v, bounds_out, lam_out, mu_out, sem):
    copies = [pltpu.make_async_copy(lam_v, lam_out, sem.at[0]), pltpu.make_async_copy(mu_v, mu_out, sem.at[1])]
    for copy in copies:
        copy.start()
    for i in range(ITERS):
        bounds_out[i] = bounds_v[i, 0]
    for copy in copies:
        copy.wait()


def solution(mesh):
    n_row, n_col = mesh.shape["row"], mesh.shape["col"]
    n_plane = (n_row // PLANES) * n_col
    total_cells = n_row * n_col * ROWS * PAIRS * 128

    def vm(*shape, dtype=F32):
        return pltpu.VMEM(shape, dtype)

    inner_rows = PAIRS * ROWS
    ext_rows = EPAIRS * EXT
    lanes = PAIRS * 128
    hbm_spec = pl.BlockSpec(memory_space=pltpu.HBM)
    vmem_spec = pl.BlockSpec(memory_space=pltpu.VMEM)

    def kernel(*refs):
        body(float(total_cells), n_row, n_col, *refs)

    def shards(*args):
        call = pl.pallas_call(
            kernel,
            out_shape=(pltpu.VMEM((8, 128), F32),
                       pltpu.VMEM((DEPTH, ROWS, lanes), F32),
                       pltpu.VMEM((DEPTH, ROWS, lanes), F32)),
            in_specs=[hbm_spec] * 7 + [pl.BlockSpec(memory_space=pltpu.SMEM)],
            out_specs=(pl.BlockSpec(memory_space=pltpu.VMEM),
                       pl.BlockSpec(memory_space=pltpu.VMEM), pl.BlockSpec(memory_space=pltpu.VMEM)),
            scratch_shapes=[
                vm(ROWS, lanes), vm(ROWS, lanes, dtype=BF16), vm(ROWS, lanes, dtype=BF16),
                vm(DEPTH, ROWS, lanes, dtype=BF16), vm(DEPTH, ROWS, lanes, dtype=BF16),
                vm(LAYERS, 3, 3, CH, CH), vm(LAYERS, CH),
                vm(9 * inner_rows, 128), vm(5 * ext_rows, 128),
                vm(inner_rows, 128), vm(inner_rows, 128),
                vm(2 * ext_rows, 128), vm(2 * ext_rows, 128),
                vm(3 * inner_rows, 128), vm(inner_rows, 128), vm(2 * ext_rows, 128),
                vm(3 * ext_rows, 128), vm(3 * ext_rows, 128),
                vm(2 * ext_rows, 128),
                vm(3 * inner_rows, 128), vm(inner_rows, 128),
                vm(3 * (EPAIRS + 1) * WIDE, 128),
                [vm(EXT, 128)] * 12, [vm(WIDE, 128)] * 9,
                vm(4, 2, 3, inner_rows + 2 * ROWS, 128, dtype=BF16), vm(3, 2, ext_rows, 768, dtype=BF16),
                vm(7, 768, 256, dtype=BF16),
                vm(2, 5, 1, PAIRS, 128), vm(2, 5, ROWS, 128), vm(4, 5, 1, 128),
                vm(2, 5, 1, PAIRS, 128), vm(2, 5, ROWS, 128), vm(4, 5, 1, 128),
                vm(2, 2, 3, 2, PAIRS, 128), vm(2, 2, 3, ROWS, 128), vm(2, 4, 3, 2, 128),
                vm(2, 2, 3, 2, PAIRS, 128), vm(2, 2, 3, ROWS, 128), vm(2, 4, 3, 2, 128),
                vm(ITERS + 1, 2, 1, 128), vm(n_plane, 1, 128), vm(PLANES, 1, 128),
                vm(ITERS, 2, 1, 128), vm(ITERS, n_row * n_col // 2, 1, 128),
                pltpu.SemaphoreType.DMA((7,)),
                pltpu.SemaphoreType.DMA((3, 8)), pltpu.SemaphoreType.DMA((3, 8)),
                pltpu.SemaphoreType.DMA((ITERS + 1, 2)), pltpu.SemaphoreType.DMA((ITERS + 1, 2)),
            ],
            compiler_params=pltpu.CompilerParams(
                collective_id=0, has_side_effects=True, vmem_limit_bytes=56 * 1024 * 1024),
            name="ascent",
        )
        results = call(*args)
        return pl.pallas_call(
            store,
            out_shape=(jax.ShapeDtypeStruct((ITERS,), F32),
                       jax.ShapeDtypeStruct((DEPTH, ROWS, lanes), F32),
                       jax.ShapeDtypeStruct((DEPTH, ROWS, lanes), F32)),
            in_specs=[vmem_spec] * 3,
            out_specs=(pl.BlockSpec(memory_space=pltpu.SMEM), hbm_spec, hbm_spec),
            scratch_shapes=[pltpu.SemaphoreType.DMA((2,))],
            compiler_params=pltpu.CompilerParams(vmem_limit_bytes=1024 * 1024),
            name="store",
        )(*results)

    placed = (P("row", "col"), P("row", "col"), P("row", "col"), P(None, "row", "col"), P(None, "row", "col"),
              P(), P(), P())
    return jax.shard_map(
        shards, mesh=mesh, in_specs=placed,
        out_specs=(P(), P(None, "row", "col"), P(None, "row", "col")), check_vma=False)
```

```python
import jax
import jax.numpy as jnp
from jax import lax
from jax.experimental import pallas as pl
from jax.experimental.pallas import tpu as pltpu
from jax.sharding import PartitionSpec as P

CH = 64
LAYERS = 4
ITERS = 3
DEPTH = LAYERS - 1
EPS = 1e-06
MESH = pl.DeviceIdType.MESH
F32 = jnp.float32
BF16 = jnp.bfloat16

ROWS = 16
PAIRS = 16
EXT = 24
EPAIRS = 18
WIDE = 32
TOP = 8
PLANES = 8
MID, HALF, H1, H2, OBJ, H3, Q1, Q2, Q3 = range(9)
UP, DOWN, LEFT, RIGHT = range(4)
SIDES = ((-1, 0), (1, 0), (0, -1), (0, 1), (-1, -1), (-1, 1), (1, -1), (1, 1))


def at(start, size):
    return pl.ds(pl.multiple_of(start, 8), size)


def inner(which, pair):
    return at((which * PAIRS + pair) * ROWS, ROWS)


def slope(which, pair):
    return at((which * (EPAIRS + 1) + pair + 1) * WIDE + TOP, ROWS)


def ext(which, pair):
    return at((which * EPAIRS + pair) * EXT, EXT)


def ext_inner(which, pair):
    return pl.ds((which * EPAIRS + pair + 1) * EXT + 1, ROWS)


def split(v):
    hi = v.astype(BF16)
    return hi, (v - hi.astype(F32)).astype(BF16)


def body(total_cells, n_row, n_col, obj_h, cen_h, rad_h, low_h, upp_h, ker_h, bia_h, steps,
         bounds_ref, lam_out, mu_out,
         obj_v, cen_v, rad_v, low_v, upp_v, ker_v, bia_v,
         base, wide_in, lam, mu, lam_x, mu_x, dl, dmu, dmu_x, trans, upd, p_x, pn, tb,
         d_w, y_s, y_w, lhs_i, lhs_x, wts,
         rows_s0, cols_s0, diag_s0, rows_r0, cols_r0, diag_r0,
         rows_s, cols_s, diag_s, rows_r, cols_r, diag_r,
         pay, buf_plane, buf_line, buf_pair, buf_chip,
         load_sem, halo_send, halo_recv, sum_send, sum_recv):
    row = lax.axis_index("row")
    col = lax.axis_index("col")
    x_hi = row // PLANES
    z = row % PLANES
    place = x_hi * n_col + col

    ring = [[place_ for place_ in (at_, (at_ + 1) % size, (at_ + size - 1) % size)]
            for at_, size in ((row, n_row), (col, n_col))]

    def side_device(side):
        return (ring[0][side[0]], ring[1][side[1]])

    loads = []
    sends = []
    for n, (src, dst) in enumerate(((cen_h, cen_v), (rad_h, rad_v), (upp_h, upp_v), (obj_h, obj_v),
                                    (ker_h, ker_v), (low_h, low_v), (bia_h, bia_v))):
        copy = pltpu.make_async_copy(src, dst, load_sem.at[n])
        copy.start()
        loads.append(copy)

    barrier = pltpu.get_barrier_semaphore()
    greeted = 0
    for side in SIDES:
        if side[0] != 0:
            pl.semaphore_signal(barrier, inc=1, device_id=side_device(side), device_id_type=MESH)
            greeted += 1
    for a in range(0, n_row, PLANES):
        for b in range(n_col):
            if a or b:
                pl.semaphore_signal(barrier, inc=1, device_id=(row ^ a if a else row, col ^ b if b else col),
                                    device_id_type=MESH)
                greeted += 1
    for a in range(1, PLANES):
        pl.semaphore_signal(barrier, inc=1, device_id=(row ^ a, col), device_id_type=MESH)
        greeted += 1

    zero_tile = jnp.zeros((8, 128), F32)

    def halo_start(n, src_ref, start, step, tall, maps, deep, bufs):
        rows_src, cols_src, diag_src, rows_dst, cols_dst, diag_dst = bufs
        for m in range(maps):
            first = start + m * step
            last = first + (PAIRS - 1) * tall
            for r in range(deep):
                rows_src[UP, m, r] = src_ref[pl.ds(first + r, PAIRS, stride=tall), :]
                rows_src[DOWN, m, r] = src_ref[pl.ds(first + ROWS - deep + r, PAIRS, stride=tall), :]
            for side, at_ in ((0, first), (1, last)):
                cols_src[side, m] = src_ref[at_ : at_ + ROWS, :]
                diag_src[side, m] = src_ref[at_ : at_ + deep, :]
                diag_src[side + 2, m] = src_ref[at_ + ROWS - deep : at_ + ROWS, :]
        copies = []
        for s in (4, 5, 6, 7, 0, 1, 2, 3):
            if s < 2:
                src, dst = rows_src.at[s], rows_dst.at[s]
            elif s < 4:
                src, dst = cols_src.at[s - 2], cols_dst.at[s - 2]
            else:
                src, dst = diag_src.at[s - 4], diag_dst.at[s - 4]
            copy = pltpu.make_async_remote_copy(
                src_ref=src, dst_ref=dst, send_sem=halo_send.at[n, s], recv_sem=halo_recv.at[n, s],
                device_id=side_device(SIDES[s]), device_id_type=MESH)
            copy.start()
            copies.append(copy)
        return copies

    no_above = row == 0
    no_below = row == n_row - 1
    no_left = col == 0
    no_right = col == n_col - 1

    def halo_place(dst_ref, maps, deep, tall, top, pairs, bufs):
        _, _, _, rows_dst, cols_dst, diag_dst = bufs

        def cut(gone, v):
            return jnp.where(gone, 0.0, v)

        for m in range(maps):
            first = m * pairs * tall
            last = first + (EPAIRS - 1) * tall
            for r in range(deep):
                dst_ref[pl.ds(first + tall + top + ROWS + r, PAIRS, stride=tall), :] = cut(
                    no_below, rows_dst[0, m, r])
                dst_ref[pl.ds(first + tall + top - deep + r, PAIRS, stride=tall), :] = cut(
                    no_above, rows_dst[1, m, r])
            dst_ref[last + top : last + top + ROWS, :] = cut(no_right, cols_dst[0, m])
            dst_ref[first + top : first + top + ROWS, :] = cut(no_left, cols_dst[1, m])
            dst_ref[last + top + ROWS : last + top + ROWS + deep, :] = cut(
                jnp.logical_or(no_below, no_right), diag_dst[0, m])
            dst_ref[first + top + ROWS : first + top + ROWS + deep, :] = cut(
                jnp.logical_or(no_below, no_left), diag_dst[1, m])
            dst_ref[last + top - deep : last + top, :] = cut(
                jnp.logical_or(no_above, no_right), diag_dst[2, m])
            dst_ref[first + top - deep : first + top, :] = cut(
                jnp.logical_or(no_above, no_left), diag_dst[3, m])

    def far(d):
        lines, across = d
        z_, y_ = lines % PLANES, across // 4
        return -(min(z_, PLANES - z_) + 2 * (lines // PLANES) + min(y_, 4 - y_) + (across % 4) // 2)

    def order(row_steps, col_steps):
        steps = [(a, b) for a in row_steps for b in col_steps if a or b]
        return sorted(steps, key=far)

    pair_steps = order((0,), (0, 1))
    chip_steps = order(range(n_row), range(0, n_col, 2))
    plane_steps = order(range(0, n_row, PLANES), range(n_col))
    line_steps = order(range(PLANES), (0,))
    chip = row * (n_col // 2) + col // 2

    def stages(n):
        if n == 0:
            return ((plane_steps, buf_plane, place), (line_steps, buf_line, z))
        return ((pair_steps, buf_pair.at[n - 1], col % 2), (chip_steps, buf_chip.at[n - 1], chip))

    def exchange(n, stage, part):
        steps, buf, slot = stages(n)[stage]
        pay[n, stage] = part
        buf[slot] = part
        for a, b in steps:
            pltpu.make_async_remote_copy(
                src_ref=pay.at[n, stage], dst_ref=buf.at[slot],
                send_sem=sum_send.at[n, stage], recv_sem=sum_recv.at[n, stage],
                device_id=(row ^ a if a else row, col ^ b if b else col), device_id_type=MESH).start()

    def whole(n, stage):
        steps, buf, _ = stages(n)[stage]
        part = buf.at[0 : len(steps)]
        return pltpu.make_async_remote_copy(
            src_ref=part, dst_ref=part, send_sem=sum_send.at[n, stage], recv_sem=sum_recv.at[n, stage],
            device_id=side_device((0, 1)), device_id_type=MESH)

    def collect(n, stage):
        whole(n, stage).wait_recv()
        return jnp.sum(stages(n)[stage][1][...], axis=0)

    low_half = lax.broadcasted_iota(jnp.int32, (1, 128), 1) < CH

    def fold(v):
        return v + pltpu.roll(v, CH, 1)

    def sum_start(n, first_row, second_row):
        exchange(n, 0, jnp.where(low_half, fold(first_row), fold(second_row)))

    def sum_middle(n):
        exchange(n, 1, collect(n, 0))

    def sum_end(n):
        return collect(n, 1)

    lane = lax.broadcasted_iota(jnp.int32, (EXT, 128), 1) < CH
    lane_w = lax.broadcasted_iota(jnp.int32, (WIDE, 128), 1) < CH

    def turn(x):
        return pltpu.roll(x, CH, 1)

    def window(k, u, e, before, now):
        y = y_s[u * LAYERS + k]
        y[...] = jnp.where(lane, before, now)
        for dh in range(3):
            hi, lo = split(y[dh : dh + ROWS, :])
            rows = pl.ds(pl.multiple_of(e * ROWS, ROWS), ROWS)
            lhs_i[k, 0, dh, rows, :] = hi
            lhs_i[k, 1, dh, rows, :] = lo

    def conv(slot, weight):
        size = PAIRS * ROWS
        halves = []
        for part in range(2):
            tiles = []
            for dh in range(3):
                tiles.append(lhs_i[slot, part, dh, ROWS : size + ROWS, :])
                tiles.append(lhs_i[slot, part, dh, 2 * ROWS : size + 2 * ROWS, :])
            halves.append(jnp.concatenate(tiles, axis=1))
        return product(halves[0], halves[1], weight)

    def product(hi, lo, weight):
        high = jnp.dot(hi, wts[weight], preferred_element_type=F32)
        low = jnp.dot(lo, wts[weight, :, 0:128], preferred_element_type=F32)
        return (low + high[:, 128:]) + high[:, :128]

    def rim(which, weight, scratch):
        lane_r = lane[0:ROWS]
        none = jnp.zeros((ROWS, 128), F32)
        start = which * EPAIRS * EXT
        sides = []
        for s in (0, ROWS + 1):
            x = [turn(wide_in[pl.ds(start + k * EXT + s, PAIRS, stride=EXT), :]) for k in range(3)]
            sides.append([jnp.where(lane_r, x[0], x[1]), jnp.where(lane_r, x[1], x[2])])
        left = jnp.where(lane_r, turn(wide_in[pl.ds(start + 1, ROWS), :]), none)
        right = jnp.where(lane_r, none, turn(wide_in[pl.ds(start + (EPAIRS - 1) * EXT + 1, ROWS), :]))
        for y, v in zip(scratch, (left, right)):
            y[0:8, :] = zero_tile
            y[16:24, :] = zero_tile
            y[1 : ROWS + 1, :] = v
        blocks = [sides[0] + [none] * 4, [none] * 4 + sides[1], [], []]
        for dh in range(3):
            blocks[2] += [scratch[0][dh : dh + ROWS, :], none]
            blocks[3] += [none, scratch[1][dh : dh + ROWS, :]]
        parts = [split(jnp.concatenate([b[k] for b in blocks], axis=0)) for k in range(6)]
        return product(jnp.concatenate([p[0] for p in parts], axis=1),
                       jnp.concatenate([p[1] for p in parts], axis=1), weight)

    def add_rim(dst, first, v):
        for at_, stride, k in ((0, ROWS, 0), (ROWS - 1, ROWS, 1)):
            rows = pl.ds(first + at_, PAIRS, stride=stride)
            dst[rows, :] = dst[rows, :] + v[k * ROWS : (k + 1) * ROWS]
        for pair, k in ((0, 2), (PAIRS - 1, 3)):
            rows = pl.ds(first + pair * ROWS, ROWS)
            dst[rows, :] = dst[rows, :] + v[k * ROWS : (k + 1) * ROWS]

    def windows_wide():
        def wide(m, p):
            return turn(d_w[at((m * (EPAIRS + 1) + p) * WIDE, WIDE), :])

        none = jnp.zeros((WIDE, 128), F32)
        start = []
        for m in range(DEPTH):
            r = wide(m, 0)
            start += [r, jnp.where(lane_w, none, r)]

        def step(t, carry):
            out = []
            for m in range(DEPTH):
                r0, ya = carry[2 * m], carry[2 * m + 1]
                r1, r2 = wide(m, 2 * t + 1), wide(m, 2 * t + 2)
                yb = jnp.where(lane_w, r0, r1)
                yc = jnp.where(lane_w, r1, r2)
                for i, y in enumerate((ya, yb, yc)):
                    y_w[m * 3 + i][...] = y
                for dh in range(3):
                    ys = [y_w[m * 3 + i][dh + TOP - 2 : dh + TOP - 2 + EXT, :] for i in range(3)]
                    for half in range(2):
                        hi, lo = split(jnp.concatenate([ys[half], ys[half + 1]], axis=0))
                        rows = pl.ds(pl.multiple_of(t * 2 * EXT, 16), 2 * EXT)
                        lhs_x[m, 0, rows, (dh * 2 + half) * 128 : (dh * 2 + half + 1) * 128] = hi
                        lhs_x[m, 1, rows, (dh * 2 + half) * 128 : (dh * 2 + half + 1) * 128] = lo
                out += [r2, yc]
            return tuple(out)
        lax.fori_loop(0, EPAIRS // 2, step, tuple(start))

    def conv_wide(m):
        size = EPAIRS * EXT
        high = jnp.dot(lhs_x[m, 0], wts[3 + m], preferred_element_type=F32)
        low = jnp.dot(lhs_x[m, 1], wts[3 + m, :, 0:128], preferred_element_type=F32)
        upd[at(m * size, size), :] = (low + high[:, 128:]) + high[:, :128]

    for n in range(4):
        loads[n].wait()

    def fill(j, carry):
        lanes = pl.ds(pl.multiple_of(j * 128, 128), 128)
        c = cen_v[:, lanes].astype(F32)
        r = rad_v[:, lanes].astype(F32)
        lo, hi = c - r, c + r
        vals = {MID: 0.5 * (hi + lo), HALF: 0.5 * (hi - lo), OBJ: obj_v[:, lanes]}
        for m, name in enumerate((H1, H2, H3)):
            vals[name] = 0.5 * upp_v[m, :, lanes].astype(F32)
        for name, v in vals.items():
            base[inner(name, j), :] = v
            if name <= OBJ:
                wide_in[at((name * EPAIRS + j + 1) * EXT, 8), :] = zero_tile
                wide_in[at((name * EPAIRS + j + 1) * EXT + 16, 8), :] = zero_tile
                wide_in[ext_inner(name, j), :] = v
        return carry
    lax.fori_loop(0, PAIRS, fill, 0)
    for m in range(5):
        for e in (0, EPAIRS - 1):
            wide_in[ext(m, e), :] = jnp.zeros((EXT, 128), F32)

    pl.semaphore_wait(barrier, greeted)
    bufs0 = (rows_s0, cols_s0, diag_s0, rows_r0, cols_r0, diag_r0)
    first_copies = halo_start(0, base, 0, PAIRS * ROWS, ROWS, 5, 1, bufs0)
    sends += first_copies

    for n in range(4, 7):
        loads[n].wait()

    def fill_low(j, carry):
        lanes = pl.ds(pl.multiple_of(j * 128, 128), 128)
        for m, name in enumerate((Q1, Q2, Q3)):
            base[inner(name, j), :] = 0.5 * low_v[m, :, lanes].astype(F32)
        return carry
    lax.fori_loop(0, PAIRS, fill_low, 0)

    bias = jnp.concatenate([bia_v[...], bia_v[...]], axis=1)
    none64 = jnp.zeros((CH, CH), F32)

    def put_weight(slot, dh, block):
        hi, lo = split(block)
        wts[slot, dh * 256 : (dh + 1) * 256, 0:128] = hi
        wts[slot, dh * 256 : (dh + 1) * 256, 128:256] = lo

    def build(k, carry):
        for dh in range(3):
            taps = [ker_v[k, 2 - dh, dw] for dw in range(3)]
            one = jnp.concatenate([jnp.concatenate([taps[2], taps[1]], axis=1),
                                   jnp.concatenate([none64, taps[2]], axis=1)], axis=0)
            two = jnp.concatenate([jnp.concatenate([taps[0], none64], axis=1),
                                   jnp.concatenate([taps[1], taps[0]], axis=1)], axis=0)
            put_weight(3 + k, dh, jnp.concatenate([one.T, two.T], axis=0))
        return carry
    lax.fori_loop(0, LAYERS, build, 0)

    def build_forward(k, carry):
        for dh in range(3):
            taps = [ker_v[k, dh, dw] for dw in range(3)]
            put_weight(k, dh, jnp.concatenate(
                [jnp.concatenate(taps + [none64], axis=0), jnp.concatenate([none64] + taps, axis=0)], axis=1))
        return carry
    lax.fori_loop(0, DEPTH, build_forward, 0)

    def clear(t, carry):
        d_w[at(t * WIDE, WIDE), :] = jnp.zeros((WIDE, 128), F32)
        return carry
    lax.fori_loop(0, DEPTH * (EPAIRS + 1), clear, 0)

    def value_terms(i, j):
        total = base[inner(OBJ, j), :] * bias[DEPTH : DEPTH + 1]
        hs = [base[inner(n, j), :] for n in (H1, H2, H3)]
        t3 = tb[inner(0, j), :]
        args = []
        if i == 0:
            args.append(-4.0 * hs[2] * t3)
        else:
            mid, half = base[inner(MID, j), :], base[inner(HALF, j), :]
            qs = [base[inner(n, j), :] for n in (Q1, Q2, Q3)]
            g0 = -trans[ext_inner(0, j), :]
            total += g0 * (mid - half)
            args.append(-4.0 * half * g0)
            lams = [lam_x[ext_inner(0, j), :], lam_x[ext_inner(1, j), :], lam[inner(0, j), :]]
            mus = [mu_x[ext_inner(0, j), :], mu_x[ext_inner(1, j), :], mu[inner(0, j), :]]
            for m in range(DEPTH):
                g = mus[m] - trans[ext_inner(m + 1, j), :] if m < 2 else mus[2] + t3
                h4 = -4.0 * hs[m]
                args += [h4 * g, h4 * (lams[m] - mus[m]), 4.0 * qs[m] * lams[m]]
                total -= lams[m] * bias[m : m + 1]
        product = 1.0 + jnp.exp(-jnp.abs(args[0]))
        positive = jnp.maximum(args[0], 0.0)
        for arg in args[1:]:
            product = product * (1.0 + jnp.exp(-jnp.abs(arg)))
            positive = positive + jnp.maximum(arg, 0.0)
        return total - 0.5 * (positive + jnp.log(product))

    def value_row(i):
        def step(j, acc):
            return acc + value_terms(i, j)
        acc = lax.fori_loop(0, PAIRS, step, jnp.zeros((ROWS, 128), F32))
        out = jnp.sum(acc, axis=0, keepdims=True)
        if i == 0:
            out = out - (0.5 * 0.6931471805599453 * 9 * ROWS * PAIRS)
        return out

    scale = None
    value_prev = jnp.zeros((1, 128), F32)
    totals = []
    for i in range(ITERS):
        first = i == 1

        def start_x(g, carry):
            before = list(carry)
            for u in range(3):
                e = 3 * g + u
                xs = [wide_in[ext(n, e), :] for n in (MID, H1, H2)]
                for m in range(2):
                    p_x[ext(m, e), :] = xs[m + 1]
                    dmu_x[ext(m, e), :] = xs[m + 1] - p_x[ext(m, e), :]
                xs.append(wide_in[ext(OBJ, e), :])
                for k, x in enumerate(xs):
                    now = turn(x)
                    window(k, u, e, before[k], now)
                    before[k] = now
            return tuple(before)

        def step_x(k):
            before = jnp.zeros((EXT, 128), F32)
            for e in range(EPAIRS):
                half = wide_in[ext((HALF, H1, H2)[k], e), :]
                mid = wide_in[ext(MID, e), :] if k == 0 else half
                t = scale * upd[ext(k, e), :]
                if not first:
                    t = trans[ext(k, e), :] + t
                trans[ext(k, e), :] = t
                coef = -t
                if k > 0:
                    m = k - 1
                    new_mu = scale * dmu_x[ext(m, e), :]
                    new_lam = scale * d_w[pl.ds((m * (EPAIRS + 1) + e) * WIDE + TOP - 1, EXT), :]
                    if not first:
                        new_mu = mu_x[ext(m, e), :] + new_mu
                        new_lam = lam_x[ext(m, e), :] + new_lam
                    mu_x[ext(m, e), :] = new_mu
                    lam_x[ext(m, e), :] = new_lam
                    coef = new_mu - t
                x = mid - half * jnp.tanh(2.0 * half * coef)
                if k > 0:
                    p = half - half * jnp.tanh(2.0 * half * (new_lam - new_mu))
                    p_x[ext(m, e), :] = p
                    dmu_x[ext(m, e), :] = x - p
                now = turn(x)
                window(k, e % 3, e, before, now)
                before = now

        if i == 0:
            lax.fori_loop(0, EPAIRS // 3, start_x, tuple(jnp.zeros((EXT, 128), F32) for _ in range(LAYERS)))
        else:
            step_x(0)
            step_x(1)

        acc = jnp.zeros((ROWS, 128), F32)
        if i == 0:
            for m in range(DEPTH):
                image = conv(m, m)
                for j in range(PAIRS):
                    dl[inner(m, j), :] = image[j * ROWS : (j + 1) * ROWS]
            image = conv(DEPTH, 3 + DEPTH)
            for j in range(PAIRS):
                tb[inner(0, j), :] = image[j * ROWS : (j + 1) * ROWS]
            for copy in first_copies:
                copy.wait_recv()
            halo_place(wide_in, 5, 1, EXT, 1, EPAIRS, bufs0)
            add_rim(tb, 0, rim(OBJ, 3 + DEPTH, y_s[0:2]))
            for m in range(DEPTH):
                add_rim(dl, m * PAIRS * ROWS, rim((MID, H1, H2)[m], m, y_s[2 * m + 2 : 2 * m + 4]))
            for j in range(PAIRS):
                for m in range(DEPTH):
                    h = base[inner(H1 + m if m < 2 else H3, j), :]
                    p = h if m == 2 else p_x[ext_inner(m, j), :]
                    if m == 2:
                        v = (h - h * jnp.tanh(2.0 * h * tb[inner(0, j), :])) - p
                        dmu[inner(0, j), :] = v
                    else:
                        v = dmu_x[ext_inner(m, j), :]
                    acc = acc + v * v
                    v = (p - base[inner(Q1 + m, j), :] - bias[m : m + 1]) - dl[inner(m, j), :]
                    d_w[slope(m, j), :] = v
                    acc = acc + v * v
        else:
            for m in range(DEPTH):
                rest = []
                for j in range(PAIRS):
                    h = base[inner(H1 + m if m < 2 else H3, j), :]
                    q = base[inner(Q1 + m, j), :]
                    if m == 2:
                        new_mu = scale * dmu[inner(0, j), :]
                        v_lam = scale * d_w[slope(2, j), :]
                        if not first:
                            new_mu = mu[inner(0, j), :] + new_mu
                            v_lam = lam[inner(0, j), :] + v_lam
                        mu[inner(0, j), :] = new_mu
                        lam[inner(0, j), :] = v_lam
                        p = h - h * jnp.tanh(2.0 * h * (v_lam - new_mu))
                        t3 = new_mu + tb[inner(0, j), :]
                        v = (h - h * jnp.tanh(2.0 * h * t3)) - p
                        dmu[inner(0, j), :] = v
                    else:
                        p = p_x[ext_inner(m, j), :]
                        v_lam = lam_x[ext_inner(m, j), :]
                        v = dmu_x[ext_inner(m, j), :]
                    acc = acc + v * v
                    n = q + q * jnp.tanh(2.0 * q * v_lam)
                    rest.append(p - n - bias[m : m + 1])
                image = conv(m, m)
                for j in range(PAIRS):
                    v = rest[j] - image[j * ROWS : (j + 1) * ROWS]
                    d_w[slope(m, j), :] = v
                    acc = acc + v * v
                if m == 0:
                    step_x(2)
        sum_start(i, jnp.sum(acc, axis=0, keepdims=True), value_prev)

        copies = []
        if i < ITERS - 1:
            bufs = tuple(ref.at[i] for ref in (rows_s, cols_s, diag_s, rows_r, cols_r, diag_r))
            copies = halo_start(1 + i, d_w, WIDE + TOP, (EPAIRS + 1) * WIDE, WIDE, DEPTH, 2, bufs)
            sends += copies
        value_prev = value_row(i)
        if i == ITERS - 1:
            sum_start(ITERS, jnp.zeros((1, 128), F32), value_prev)
        sum_middle(i)
        if i < ITERS - 1:
            for copy in copies:
                copy.wait_recv()
            halo_place(d_w, DEPTH, 2, WIDE, TOP, EPAIRS + 1, bufs)
            windows_wide()
            for m in range(DEPTH):
                conv_wide(m)
        else:
            sum_middle(ITERS)
        both = sum_end(i)
        squares = jnp.sum(jnp.where(low_half, both, 0.0), axis=1, keepdims=True)
        scale = steps[i] / jnp.sqrt(squares / (2 * DEPTH * total_cells) + EPS)
        scale = jnp.broadcast_to(scale, (1, 128))
        totals.append(both)

    def finish(j, carry):
        lanes = pl.ds(pl.multiple_of(j * 128, 128), 128)
        for m in range(2):
            lam_out[m, :, lanes] = lam_x[ext_inner(m, j), :] + scale * d_w[slope(m, j), :]
            mu_out[m, :, lanes] = mu_x[ext_inner(m, j), :] + scale * dmu_x[ext_inner(m, j), :]
        lam_out[2, :, lanes] = lam[inner(0, j), :] + scale * d_w[slope(2, j), :]
        mu_out[2, :, lanes] = mu[inner(0, j), :] + scale * dmu[inner(0, j), :]
        return carry
    lax.fori_loop(0, PAIRS, finish, 0)
    for copy in sends:
        copy.wait_send()
    for n in range(ITERS + 1):
        for stage in range(2):
            whole(n, stage).wait_send()
    for i in range(ITERS):
        if i == ITERS - 1:
            totals.append(sum_end(ITERS))
        mean = jnp.sum(jnp.where(low_half, 0.0, totals[i + 1]), axis=1, keepdims=True) / total_cells
        bounds_ref[i : i + 1, :] = jnp.broadcast_to(mean, (1, 128))


def store(bounds_v, lam_v, mu_v, bounds_out, lam_out, mu_out, sem):
    copies = [pltpu.make_async_copy(lam_v, lam_out, sem.at[0]), pltpu.make_async_copy(mu_v, mu_out, sem.at[1])]
    for copy in copies:
        copy.start()
    for i in range(ITERS):
        bounds_out[i] = bounds_v[i, 0]
    for copy in copies:
        copy.wait()


def solution(mesh):
    n_row, n_col = mesh.shape["row"], mesh.shape["col"]
    n_plane = (n_row // PLANES) * n_col
    total_cells = n_row * n_col * ROWS * PAIRS * 128

    def vm(*shape, dtype=F32):
        return pltpu.VMEM(shape, dtype)

    inner_rows = PAIRS * ROWS
    ext_rows = EPAIRS * EXT
    lanes = PAIRS * 128
    hbm_spec = pl.BlockSpec(memory_space=pltpu.HBM)
    vmem_spec = pl.BlockSpec(memory_space=pltpu.VMEM)

    def kernel(*refs):
        body(float(total_cells), n_row, n_col, *refs)

    def shards(*args):
        call = pl.pallas_call(
            kernel,
            out_shape=(pltpu.VMEM((8, 128), F32),
                       pltpu.VMEM((DEPTH, ROWS, lanes), F32),
                       pltpu.VMEM((DEPTH, ROWS, lanes), F32)),
            in_specs=[hbm_spec] * 7 + [pl.BlockSpec(memory_space=pltpu.SMEM)],
            out_specs=(pl.BlockSpec(memory_space=pltpu.VMEM),
                       pl.BlockSpec(memory_space=pltpu.VMEM), pl.BlockSpec(memory_space=pltpu.VMEM)),
            scratch_shapes=[
                vm(ROWS, lanes), vm(ROWS, lanes, dtype=BF16), vm(ROWS, lanes, dtype=BF16),
                vm(DEPTH, ROWS, lanes, dtype=BF16), vm(DEPTH, ROWS, lanes, dtype=BF16),
                vm(LAYERS, 3, 3, CH, CH), vm(LAYERS, CH),
                vm(9 * inner_rows, 128), vm(5 * ext_rows, 128),
                vm(inner_rows, 128), vm(inner_rows, 128),
                vm(2 * ext_rows, 128), vm(2 * ext_rows, 128),
                vm(3 * inner_rows, 128), vm(inner_rows, 128), vm(2 * ext_rows, 128),
                vm(3 * ext_rows, 128), vm(3 * ext_rows, 128),
                vm(2 * ext_rows, 128),
                vm(3 * inner_rows, 128), vm(inner_rows, 128),
                vm(3 * (EPAIRS + 1) * WIDE, 128),
                [vm(EXT, 128)] * 12, [vm(WIDE, 128)] * 9,
                vm(4, 2, 3, inner_rows + 2 * ROWS, 128, dtype=BF16), vm(3, 2, ext_rows, 768, dtype=BF16),
                vm(7, 768, 256, dtype=BF16),
                vm(2, 5, 1, PAIRS, 128), vm(2, 5, ROWS, 128), vm(4, 5, 1, 128),
                vm(2, 5, 1, PAIRS, 128), vm(2, 5, ROWS, 128), vm(4, 5, 1, 128),
                vm(2, 2, 3, 2, PAIRS, 128), vm(2, 2, 3, ROWS, 128), vm(2, 4, 3, 2, 128),
                vm(2, 2, 3, 2, PAIRS, 128), vm(2, 2, 3, ROWS, 128), vm(2, 4, 3, 2, 128),
                vm(ITERS + 1, 2, 1, 128), vm(n_plane, 1, 128), vm(PLANES, 1, 128),
                vm(ITERS, 2, 1, 128), vm(ITERS, n_row * n_col // 2, 1, 128),
                pltpu.SemaphoreType.DMA((7,)),
                pltpu.SemaphoreType.DMA((3, 8)), pltpu.SemaphoreType.DMA((3, 8)),
                pltpu.SemaphoreType.DMA((ITERS + 1, 2)), pltpu.SemaphoreType.DMA((ITERS + 1, 2)),
            ],
            compiler_params=pltpu.CompilerParams(
                collective_id=0, has_side_effects=True, vmem_limit_bytes=56 * 1024 * 1024),
            name="ascent",
        )
        results = call(*args)
        return pl.pallas_call(
            store,
            out_shape=(jax.ShapeDtypeStruct((ITERS,), F32),
                       jax.ShapeDtypeStruct((DEPTH, ROWS, lanes), F32),
                       jax.ShapeDtypeStruct((DEPTH, ROWS, lanes), F32)),
            in_specs=[vmem_spec] * 3,
            out_specs=(pl.BlockSpec(memory_space=pltpu.SMEM), hbm_spec, hbm_spec),
            scratch_shapes=[pltpu.SemaphoreType.DMA((2,))],
            compiler_params=pltpu.CompilerParams(vmem_limit_bytes=1024 * 1024),
            name="store",
        )(*results)

    placed = (P("row", "col"), P("row", "col"), P("row", "col"), P(None, "row", "col"), P(None, "row", "col"),
              P(), P(), P())
    return jax.shard_map(
        shards, mesh=mesh, in_specs=placed,
        out_specs=(P(), P(None, "row", "col"), P(None, "row", "col")), check_vma=False)
```

```python
import jax
import jax.numpy as jnp
from jax import lax
from jax.experimental import pallas as pl
from jax.experimental.pallas import tpu as pltpu
from jax.sharding import PartitionSpec as P

CH = 64
LAYERS = 4
ITERS = 3
DEPTH = LAYERS - 1
EPS = 1e-06
MESH = pl.DeviceIdType.MESH
F32 = jnp.float32
BF16 = jnp.bfloat16

ROWS = 16
PAIRS = 16
EXT = 24
EPAIRS = 18
WIDE = 32
TOP = 8
PLANES = 8
MID, HALF, H1, H2, OBJ, H3, Q1, Q2, Q3 = range(9)
UP, DOWN, LEFT, RIGHT = range(4)
SIDES = ((-1, 0), (1, 0), (0, -1), (0, 1), (-1, -1), (-1, 1), (1, -1), (1, 1))


def at(start, size):
    return pl.ds(pl.multiple_of(start, 8), size)


def inner(which, pair):
    return at((which * PAIRS + pair) * ROWS, ROWS)


def slope(which, pair):
    return at((which * (EPAIRS + 1) + pair + 1) * WIDE + TOP, ROWS)


def ext(which, pair):
    return at((which * EPAIRS + pair) * EXT, EXT)


def ext_inner(which, pair):
    return pl.ds((which * EPAIRS + pair + 1) * EXT + 1, ROWS)


def softplus_sum(args):
    product = 1.0 + jnp.exp(-jnp.abs(args[0]))
    positive = jnp.maximum(args[0], 0.0)
    for arg in args[1:]:
        product = product * (1.0 + jnp.exp(-jnp.abs(arg)))
        positive = positive + jnp.maximum(arg, 0.0)
    return positive + jnp.log(product)


def split(v):
    hi = v.astype(BF16)
    return hi, (v - hi.astype(F32)).astype(BF16)


def body(total_cells, n_row, n_col, obj_h, cen_h, rad_h, low_h, upp_h, ker_h, bia_h, steps,
         bounds_ref, lam_out, mu_out,
         obj_v, cen_v, rad_v, low_v, upp_v, ker_v, bia_v,
         base, wide_in, lam, mu, lam_x, mu_x, dl, dmu, dmu_x, trans, upd, p_x, pn, tb,
         d_w, y_s, y_w, lhs_i, lhs_x, wts,
         rows_s0, cols_s0, diag_s0, rows_r0, cols_r0, diag_r0,
         rows_s, cols_s, diag_s, rows_r, cols_r, diag_r,
         pay, buf_plane, buf_line, buf_pair, buf_chip,
         load_sem, halo_send, halo_recv, sum_send, sum_recv):
    row = lax.axis_index("row")
    col = lax.axis_index("col")
    x_hi = row // PLANES
    z = row % PLANES
    place = x_hi * n_col + col

    ring = [[place_ for place_ in (at_, (at_ + 1) % size, (at_ + size - 1) % size)]
            for at_, size in ((row, n_row), (col, n_col))]

    def side_device(side):
        return (ring[0][side[0]], ring[1][side[1]])

    loads = []
    sends = []
    for n, (src, dst) in enumerate(((cen_h, cen_v), (rad_h, rad_v), (upp_h, upp_v), (obj_h, obj_v),
                                    (ker_h, ker_v), (low_h, low_v), (bia_h, bia_v))):
        copy = pltpu.make_async_copy(src, dst, load_sem.at[n])
        copy.start()
        loads.append(copy)

    barrier = pltpu.get_barrier_semaphore()
    greeted = 0
    for side in SIDES:
        if side[0] != 0:
            pl.semaphore_signal(barrier, inc=1, device_id=side_device(side), device_id_type=MESH)
            greeted += 1
    for a in range(0, n_row, PLANES):
        for b in range(n_col):
            if a or b:
                pl.semaphore_signal(barrier, inc=1, device_id=(row ^ a if a else row, col ^ b if b else col),
                                    device_id_type=MESH)
                greeted += 1
    for a in range(1, PLANES):
        pl.semaphore_signal(barrier, inc=1, device_id=(row ^ a, col), device_id_type=MESH)
        greeted += 1

    zero_tile = jnp.zeros((8, 128), F32)

    def halo_start(n, src_ref, start, step, tall, maps, deep, bufs):
        rows_src, cols_src, diag_src, rows_dst, cols_dst, diag_dst = bufs
        for m in range(maps):
            first = start + m * step
            last = first + (PAIRS - 1) * tall
            for r in range(deep):
                rows_src[UP, m, r] = src_ref[pl.ds(first + r, PAIRS, stride=tall), :]
                rows_src[DOWN, m, r] = src_ref[pl.ds(first + ROWS - deep + r, PAIRS, stride=tall), :]
            for side, at_ in ((0, first), (1, last)):
                cols_src[side, m] = src_ref[at_ : at_ + ROWS, :]
                diag_src[side, m] = src_ref[at_ : at_ + deep, :]
                diag_src[side + 2, m] = src_ref[at_ + ROWS - deep : at_ + ROWS, :]
        copies = []
        for s in (4, 5, 6, 7, 0, 1, 2, 3):
            if s < 2:
                src, dst = rows_src.at[s], rows_dst.at[s]
            elif s < 4:
                src, dst = cols_src.at[s - 2], cols_dst.at[s - 2]
            else:
                src, dst = diag_src.at[s - 4], diag_dst.at[s - 4]
            copy = pltpu.make_async_remote_copy(
                src_ref=src, dst_ref=dst, send_sem=halo_send.at[n, s], recv_sem=halo_recv.at[n, s],
                device_id=side_device(SIDES[s]), device_id_type=MESH)
            copy.start()
            copies.append(copy)
        return copies

    no_above = row == 0
    no_below = row == n_row - 1
    no_left = col == 0
    no_right = col == n_col - 1

    def halo_place(dst_ref, maps, deep, tall, top, pairs, bufs):
        _, _, _, rows_dst, cols_dst, diag_dst = bufs

        def cut(gone, v):
            return jnp.where(gone, 0.0, v)

        for m in range(maps):
            first = m * pairs * tall
            last = first + (EPAIRS - 1) * tall
            for r in range(deep):
                dst_ref[pl.ds(first + tall + top + ROWS + r, PAIRS, stride=tall), :] = cut(
                    no_below, rows_dst[0, m, r])
                dst_ref[pl.ds(first + tall + top - deep + r, PAIRS, stride=tall), :] = cut(
                    no_above, rows_dst[1, m, r])
            dst_ref[last + top : last + top + ROWS, :] = cut(no_right, cols_dst[0, m])
            dst_ref[first + top : first + top + ROWS, :] = cut(no_left, cols_dst[1, m])
            dst_ref[last + top + ROWS : last + top + ROWS + deep, :] = cut(
                jnp.logical_or(no_below, no_right), diag_dst[0, m])
            dst_ref[first + top + ROWS : first + top + ROWS + deep, :] = cut(
                jnp.logical_or(no_below, no_left), diag_dst[1, m])
            dst_ref[last + top - deep : last + top, :] = cut(
                jnp.logical_or(no_above, no_right), diag_dst[2, m])
            dst_ref[first + top - deep : first + top, :] = cut(
                jnp.logical_or(no_above, no_left), diag_dst[3, m])

    def far(d):
        lines, across = d
        z_, y_ = lines % PLANES, across // 4
        return -(min(z_, PLANES - z_) + 2 * (lines // PLANES) + min(y_, 4 - y_) + (across % 4) // 2)

    def order(row_steps, col_steps):
        steps = [(a, b) for a in row_steps for b in col_steps if a or b]
        return sorted(steps, key=far)

    pair_steps = order((0,), (0, 1))
    chip_steps = order(range(n_row), range(0, n_col, 2))
    plane_steps = order(range(0, n_row, PLANES), range(n_col))
    line_steps = order(range(PLANES), (0,))
    chip = row * (n_col // 2) + col // 2

    def stages(n):
        if n == 0:
            return ((plane_steps, buf_plane, place), (line_steps, buf_line, z))
        return ((pair_steps, buf_pair.at[n - 1], col % 2), (chip_steps, buf_chip.at[n - 1], chip))

    def exchange(n, stage, part):
        steps, buf, slot = stages(n)[stage]
        pay[n, stage] = part
        buf[slot] = part
        for a, b in steps:
            pltpu.make_async_remote_copy(
                src_ref=pay.at[n, stage], dst_ref=buf.at[slot],
                send_sem=sum_send.at[n, stage], recv_sem=sum_recv.at[n, stage],
                device_id=(row ^ a if a else row, col ^ b if b else col), device_id_type=MESH).start()

    def whole(n, stage):
        steps, buf, _ = stages(n)[stage]
        part = buf.at[0 : len(steps)]
        return pltpu.make_async_remote_copy(
            src_ref=part, dst_ref=part, send_sem=sum_send.at[n, stage], recv_sem=sum_recv.at[n, stage],
            device_id=side_device((0, 1)), device_id_type=MESH)

    def collect(n, stage):
        whole(n, stage).wait_recv()
        return jnp.sum(stages(n)[stage][1][...], axis=0)

    lane_1 = lax.broadcasted_iota(jnp.int32, (1, 128), 1)
    holds = (lane_1 < 32, jnp.logical_and(lane_1 >= 32, lane_1 < CH), lane_1 >= CH)

    def fold_to(v, width):
        step = CH
        while step >= width:
            v = v + pltpu.roll(v, step, 1)
            step //= 2
        return v

    def sum_start(n, first_row, second_row, third_row):
        exchange(n, 0, jnp.where(holds[0], fold_to(first_row, 32),
                                 jnp.where(holds[1], fold_to(second_row, 32), fold_to(third_row, CH))))

    def sum_middle(n):
        exchange(n, 1, collect(n, 0))

    def sum_end(n):
        return collect(n, 1)

    lane = lax.broadcasted_iota(jnp.int32, (EXT, 128), 1) < CH
    lane_w = lax.broadcasted_iota(jnp.int32, (WIDE, 128), 1) < CH

    def turn(x):
        return pltpu.roll(x, CH, 1)

    def window(k, u, e, before, now):
        y = y_s[u * LAYERS + k]
        y[...] = jnp.where(lane, before, now)
        for dh in range(3):
            hi, lo = split(y[dh : dh + ROWS, :])
            rows = pl.ds(pl.multiple_of(e * ROWS, ROWS), ROWS)
            lhs_i[k, 0, dh, rows, :] = hi
            lhs_i[k, 1, dh, rows, :] = lo

    def conv(slot, weight):
        size = PAIRS * ROWS
        halves = []
        for part in range(2):
            tiles = []
            for dh in range(3):
                tiles.append(lhs_i[slot, part, dh, ROWS : size + ROWS, :])
                tiles.append(lhs_i[slot, part, dh, 2 * ROWS : size + 2 * ROWS, :])
            halves.append(jnp.concatenate(tiles, axis=1))
        return product(halves[0], halves[1], weight)

    def product(hi, lo, weight):
        high = jnp.dot(hi, wts[weight], preferred_element_type=F32)
        low = jnp.dot(lo, wts[weight, :, 0:128], preferred_element_type=F32)
        return (low + high[:, 128:]) + high[:, :128]

    def rim(which, weight, scratch):
        lane_r = lane[0:ROWS]
        none = jnp.zeros((ROWS, 128), F32)
        start = which * EPAIRS * EXT
        sides = []
        for s in (0, ROWS + 1):
            x = [turn(wide_in[pl.ds(start + k * EXT + s, PAIRS, stride=EXT), :]) for k in range(3)]
            sides.append([jnp.where(lane_r, x[0], x[1]), jnp.where(lane_r, x[1], x[2])])
        left = jnp.where(lane_r, turn(wide_in[pl.ds(start + 1, ROWS), :]), none)
        right = jnp.where(lane_r, none, turn(wide_in[pl.ds(start + (EPAIRS - 1) * EXT + 1, ROWS), :]))
        for y, v in zip(scratch, (left, right)):
            y[0:8, :] = zero_tile
            y[16:24, :] = zero_tile
            y[1 : ROWS + 1, :] = v
        blocks = [sides[0] + [none] * 4, [none] * 4 + sides[1], [], []]
        for dh in range(3):
            blocks[2] += [scratch[0][dh : dh + ROWS, :], none]
            blocks[3] += [none, scratch[1][dh : dh + ROWS, :]]
        parts = [split(jnp.concatenate([b[k] for b in blocks], axis=0)) for k in range(6)]
        return product(jnp.concatenate([p[0] for p in parts], axis=1),
                       jnp.concatenate([p[1] for p in parts], axis=1), weight)

    def add_rim(dst, first, v):
        for at_, stride, k in ((0, ROWS, 0), (ROWS - 1, ROWS, 1)):
            rows = pl.ds(first + at_, PAIRS, stride=stride)
            dst[rows, :] = dst[rows, :] + v[k * ROWS : (k + 1) * ROWS]
        for pair, k in ((0, 2), (PAIRS - 1, 3)):
            rows = pl.ds(first + pair * ROWS, ROWS)
            dst[rows, :] = dst[rows, :] + v[k * ROWS : (k + 1) * ROWS]

    def windows_wide():
        def wide(m, p):
            return turn(d_w[at((m * (EPAIRS + 1) + p) * WIDE, WIDE), :])

        none = jnp.zeros((WIDE, 128), F32)
        start = []
        for m in range(DEPTH):
            r = wide(m, 0)
            start += [r, jnp.where(lane_w, none, r)]

        def step(t, carry):
            out = []
            for m in range(DEPTH):
                r0, ya = carry[2 * m], carry[2 * m + 1]
                r1, r2 = wide(m, 2 * t + 1), wide(m, 2 * t + 2)
                yb = jnp.where(lane_w, r0, r1)
                yc = jnp.where(lane_w, r1, r2)
                for i, y in enumerate((ya, yb, yc)):
                    y_w[m * 3 + i][...] = y
                for dh in range(3):
                    ys = [y_w[m * 3 + i][dh + TOP - 2 : dh + TOP - 2 + EXT, :] for i in range(3)]
                    for half in range(2):
                        hi, lo = split(jnp.concatenate([ys[half], ys[half + 1]], axis=0))
                        rows = pl.ds(pl.multiple_of(t * 2 * EXT, 16), 2 * EXT)
                        lhs_x[m, 0, rows, (dh * 2 + half) * 128 : (dh * 2 + half + 1) * 128] = hi
                        lhs_x[m, 1, rows, (dh * 2 + half) * 128 : (dh * 2 + half + 1) * 128] = lo
                out += [r2, yc]
            return tuple(out)
        lax.fori_loop(0, EPAIRS // 2, step, tuple(start))

    def conv_wide(m):
        size = EPAIRS * EXT
        high = jnp.dot(lhs_x[m, 0], wts[3 + m], preferred_element_type=F32)
        low = jnp.dot(lhs_x[m, 1], wts[3 + m, :, 0:128], preferred_element_type=F32)
        upd[at(m * size, size), :] = (low + high[:, 128:]) + high[:, :128]

    for n in range(4):
        loads[n].wait()

    def fill(j, carry):
        lanes = pl.ds(pl.multiple_of(j * 128, 128), 128)
        c = cen_v[:, lanes].astype(F32)
        r = rad_v[:, lanes].astype(F32)
        lo, hi = c - r, c + r
        vals = {MID: 0.5 * (hi + lo), HALF: 0.5 * (hi - lo), OBJ: obj_v[:, lanes]}
        for m, name in enumerate((H1, H2, H3)):
            vals[name] = 0.5 * upp_v[m, :, lanes].astype(F32)
        for name, v in vals.items():
            base[inner(name, j), :] = v
            if name <= OBJ:
                wide_in[at((name * EPAIRS + j + 1) * EXT, 8), :] = zero_tile
                wide_in[at((name * EPAIRS + j + 1) * EXT + 16, 8), :] = zero_tile
                wide_in[ext_inner(name, j), :] = v
        return carry
    lax.fori_loop(0, PAIRS, fill, 0, unroll=4)
    for m in range(5):
        for e in (0, EPAIRS - 1):
            wide_in[ext(m, e), :] = jnp.zeros((EXT, 128), F32)

    pl.semaphore_wait(barrier, greeted)
    bufs0 = (rows_s0, cols_s0, diag_s0, rows_r0, cols_r0, diag_r0)
    first_copies = halo_start(0, base, 0, PAIRS * ROWS, ROWS, 5, 1, bufs0)
    sends += first_copies

    for n in range(4, 7):
        loads[n].wait()

    def fill_low(j, carry):
        lanes = pl.ds(pl.multiple_of(j * 128, 128), 128)
        for m, name in enumerate((Q1, Q2, Q3)):
            base[inner(name, j), :] = 0.5 * low_v[m, :, lanes].astype(F32)
        return carry
    lax.fori_loop(0, PAIRS, fill_low, 0)

    bias = jnp.concatenate([bia_v[...], bia_v[...]], axis=1)
    none64 = jnp.zeros((CH, CH), F32)

    def put_weight(slot, dh, block):
        hi, lo = split(block)
        wts[slot, dh * 256 : (dh + 1) * 256, 0:128] = hi
        wts[slot, dh * 256 : (dh + 1) * 256, 128:256] = lo

    def build(k, carry):
        for dh in range(3):
            taps = [ker_v[k, 2 - dh, dw] for dw in range(3)]
            one = jnp.concatenate([jnp.concatenate([taps[2], taps[1]], axis=1),
                                   jnp.concatenate([none64, taps[2]], axis=1)], axis=0)
            two = jnp.concatenate([jnp.concatenate([taps[0], none64], axis=1),
                                   jnp.concatenate([taps[1], taps[0]], axis=1)], axis=0)
            put_weight(3 + k, dh, jnp.concatenate([one.T, two.T], axis=0))
        return carry
    lax.fori_loop(0, LAYERS, build, 0)

    def build_forward(k, carry):
        for dh in range(3):
            taps = [ker_v[k, dh, dw] for dw in range(3)]
            put_weight(k, dh, jnp.concatenate(
                [jnp.concatenate(taps + [none64], axis=0), jnp.concatenate([none64] + taps, axis=0)], axis=1))
        return carry
    lax.fori_loop(0, DEPTH, build_forward, 0)

    def clear(t, carry):
        d_w[at(t * WIDE, WIDE), :] = jnp.zeros((WIDE, 128), F32)
        return carry
    lax.fori_loop(0, DEPTH * (EPAIRS + 1), clear, 0)

    def value_terms(i, j):
        total = base[inner(OBJ, j), :] * bias[DEPTH : DEPTH + 1]
        hs = [base[inner(n, j), :] for n in (H1, H2, H3)]
        t3 = tb[inner(0, j), :]
        args = []
        if i == 0:
            args.append(-4.0 * hs[2] * t3)
        else:
            mid, half = base[inner(MID, j), :], base[inner(HALF, j), :]
            qs = [base[inner(n, j), :] for n in (Q1, Q2, Q3)]
            g0 = -trans[ext_inner(0, j), :]
            total += g0 * (mid - half)
            args.append(-4.0 * half * g0)
            lams = [lam_x[ext_inner(0, j), :], lam_x[ext_inner(1, j), :], lam[inner(0, j), :]]
            mus = [mu_x[ext_inner(0, j), :], mu_x[ext_inner(1, j), :], mu[inner(0, j), :]]
            for m in range(DEPTH):
                g = mus[m] - trans[ext_inner(m + 1, j), :] if m < 2 else mus[2] + t3
                h4 = -4.0 * hs[m]
                args += [h4 * g, h4 * (lams[m] - mus[m]), 4.0 * qs[m] * lams[m]]
                total -= lams[m] * bias[m : m + 1]
        return total - 0.5 * softplus_sum(args)

    def value_row(i):
        def step(j, acc):
            return acc + value_terms(i, j)
        acc = lax.fori_loop(0, PAIRS, step, jnp.zeros((ROWS, 128), F32))
        out = jnp.sum(acc, axis=0, keepdims=True)
        if i == 0:
            out = out - (0.5 * 0.6931471805599453 * 9 * ROWS * PAIRS)
        return out

    scale = None
    value_prev = jnp.zeros((1, 128), F32)
    totals = []
    for i in range(ITERS):
        first = i == 1

        def start_x(g, carry):
            before = list(carry)
            for u in range(3):
                e = 3 * g + u
                xs = [wide_in[ext(n, e), :] for n in (MID, H1, H2)]
                for m in range(2):
                    p_x[ext(m, e), :] = xs[m + 1]
                    dmu_x[ext(m, e), :] = xs[m + 1] - p_x[ext(m, e), :]
                xs.append(wide_in[ext(OBJ, e), :])
                for k, x in enumerate(xs):
                    now = turn(x)
                    window(k, u, e, before[k], now)
                    before[k] = now
            return tuple(before)

        def step_x(k):
            before = jnp.zeros((EXT, 128), F32)
            for e in range(EPAIRS):
                half = wide_in[ext((HALF, H1, H2)[k], e), :]
                mid = wide_in[ext(MID, e), :] if k == 0 else half
                t = scale * upd[ext(k, e), :]
                if not first:
                    t = trans[ext(k, e), :] + t
                trans[ext(k, e), :] = t
                coef = -t
                if k > 0:
                    m = k - 1
                    new_mu = scale * dmu_x[ext(m, e), :]
                    new_lam = scale * d_w[pl.ds((m * (EPAIRS + 1) + e) * WIDE + TOP - 1, EXT), :]
                    if not first:
                        new_mu = mu_x[ext(m, e), :] + new_mu
                        new_lam = lam_x[ext(m, e), :] + new_lam
                    mu_x[ext(m, e), :] = new_mu
                    lam_x[ext(m, e), :] = new_lam
                    coef = new_mu - t
                x = mid - half * jnp.tanh(2.0 * half * coef)
                if k > 0:
                    p = half - half * jnp.tanh(2.0 * half * (new_lam - new_mu))
                    p_x[ext(m, e), :] = p
                    dmu_x[ext(m, e), :] = x - p
                now = turn(x)
                window(k, e % 3, e, before, now)
                before = now

        if i == 0:
            lax.fori_loop(0, EPAIRS // 3, start_x, tuple(jnp.zeros((EXT, 128), F32) for _ in range(LAYERS)))
        else:
            step_x(0)
            step_x(1)
            if i == ITERS - 1:
                step_x(2)

        acc = jnp.zeros((ROWS, 128), F32)
        value_last = jnp.zeros((ROWS, 128), F32)
        if i == 0:
            for m in range(DEPTH):
                image = conv(m, m)
                for j in range(PAIRS):
                    dl[inner(m, j), :] = image[j * ROWS : (j + 1) * ROWS]
            image = conv(DEPTH, 3 + DEPTH)
            for j in range(PAIRS):
                tb[inner(0, j), :] = image[j * ROWS : (j + 1) * ROWS]
            for copy in first_copies:
                copy.wait_recv()
            halo_place(wide_in, 5, 1, EXT, 1, EPAIRS, bufs0)
            add_rim(tb, 0, rim(OBJ, 3 + DEPTH, y_s[0:2]))
            for m in range(DEPTH):
                add_rim(dl, m * PAIRS * ROWS, rim((MID, H1, H2)[m], m, y_s[2 * m + 2 : 2 * m + 4]))
            for j in range(PAIRS):
                for m in range(DEPTH):
                    h = base[inner(H1 + m if m < 2 else H3, j), :]
                    p = h if m == 2 else p_x[ext_inner(m, j), :]
                    if m == 2:
                        v = (h - h * jnp.tanh(2.0 * h * tb[inner(0, j), :])) - p
                        dmu[inner(0, j), :] = v
                    else:
                        v = dmu_x[ext_inner(m, j), :]
                    acc = acc + v * v
                    v = (p - base[inner(Q1 + m, j), :] - bias[m : m + 1]) - dl[inner(m, j), :]
                    d_w[slope(m, j), :] = v
                    acc = acc + v * v
        else:
            for m in range(DEPTH):
                rest = []
                for j in range(PAIRS):
                    h = base[inner(H1 + m if m < 2 else H3, j), :]
                    q = base[inner(Q1 + m, j), :]
                    if m == 2:
                        new_mu = scale * dmu[inner(0, j), :]
                        v_lam = scale * d_w[slope(2, j), :]
                        if not first:
                            new_mu = mu[inner(0, j), :] + new_mu
                            v_lam = lam[inner(0, j), :] + v_lam
                        mu[inner(0, j), :] = new_mu
                        lam[inner(0, j), :] = v_lam
                        p = h - h * jnp.tanh(2.0 * h * (v_lam - new_mu))
                        t3 = new_mu + tb[inner(0, j), :]
                        v = (h - h * jnp.tanh(2.0 * h * t3)) - p
                        dmu[inner(0, j), :] = v
                    else:
                        p = p_x[ext_inner(m, j), :]
                        v_lam = lam_x[ext_inner(m, j), :]
                        v = dmu_x[ext_inner(m, j), :]
                    acc = acc + v * v
                    if i == ITERS - 1:
                        if m == 2:
                            v_mu, coef = new_mu, t3
                        else:
                            v_mu = mu_x[ext_inner(m, j), :]
                            coef = v_mu - trans[ext_inner(m + 1, j), :]
                        args = [-4.0 * h * coef, -4.0 * h * (v_lam - v_mu), 4.0 * q * v_lam]
                        part = -v_lam * bias[m : m + 1]
                        if m == 0:
                            half = base[inner(HALF, j), :]
                            coef = -trans[ext_inner(0, j), :]
                            args.append(-4.0 * half * coef)
                            part += coef * (base[inner(MID, j), :] - half)
                            part += base[inner(OBJ, j), :] * bias[DEPTH : DEPTH + 1]
                        value_last = value_last + (part - 0.5 * softplus_sum(args))
                    n = q + q * jnp.tanh(2.0 * q * v_lam)
                    rest.append(p - n - bias[m : m + 1])
                image = conv(m, m)
                for j in range(PAIRS):
                    v = rest[j] - image[j * ROWS : (j + 1) * ROWS]
                    d_w[slope(m, j), :] = v
                    acc = acc + v * v
                if m == 0 and i < ITERS - 1:
                    step_x(2)
        sum_start(i, *[jnp.sum(v, axis=0, keepdims=True) for v in (acc, value_last)], value_prev)

        copies = []
        if i < ITERS - 1:
            bufs = tuple(ref.at[i] for ref in (rows_s, cols_s, diag_s, rows_r, cols_r, diag_r))
            copies = halo_start(1 + i, d_w, WIDE + TOP, (EPAIRS + 1) * WIDE, WIDE, DEPTH, 2, bufs)
            sends += copies
        if i < ITERS - 1:
            value_prev = value_row(i)
        sum_middle(i)
        if i < ITERS - 1:
            for copy in copies:
                copy.wait_recv()
            halo_place(d_w, DEPTH, 2, WIDE, TOP, EPAIRS + 1, bufs)
            windows_wide()
            for m in range(DEPTH):
                conv_wide(m)
        if i == ITERS - 1:
            for copy in sends:
                copy.wait_send()
            for n in range(ITERS):
                for stage in range(2):
                    whole(n, stage).wait_send()
        both = sum_end(i)
        squares = jnp.sum(jnp.where(holds[0], both, 0.0), axis=1, keepdims=True)
        scale = steps[i] / jnp.sqrt(squares / (2 * DEPTH * total_cells) + EPS)
        scale = jnp.broadcast_to(scale, (1, 128))
        totals.append(both)

    for j in range(PAIRS):
        lanes = pl.ds(j * 128, 128)
        for m in range(2):
            lam_out[m, :, lanes] = lam_x[ext_inner(m, j), :] + scale * d_w[slope(m, j), :]
            mu_out[m, :, lanes] = mu_x[ext_inner(m, j), :] + scale * dmu_x[ext_inner(m, j), :]
        lam_out[2, :, lanes] = lam[inner(0, j), :] + scale * d_w[slope(2, j), :]
        mu_out[2, :, lanes] = mu[inner(0, j), :] + scale * dmu[inner(0, j), :]
    for i in range(ITERS):
        last = i == ITERS - 1
        mean = jnp.sum(jnp.where(holds[1 if last else 2], totals[i if last else i + 1], 0.0), axis=1, keepdims=True)
        bounds_ref[i : i + 1, :] = jnp.broadcast_to(mean / total_cells, (1, 128))


def store(bounds_v, lam_v, mu_v, bounds_out, lam_out, mu_out, sem):
    copies = [pltpu.make_async_copy(lam_v, lam_out, sem.at[0]), pltpu.make_async_copy(mu_v, mu_out, sem.at[1])]
    for copy in copies:
        copy.start()
    for i in range(ITERS):
        bounds_out[i] = bounds_v[i, 0]
    for copy in copies:
        copy.wait()


def solution(mesh):
    n_row, n_col = mesh.shape["row"], mesh.shape["col"]
    n_plane = (n_row // PLANES) * n_col
    total_cells = n_row * n_col * ROWS * PAIRS * 128

    def vm(*shape, dtype=F32):
        return pltpu.VMEM(shape, dtype)

    inner_rows = PAIRS * ROWS
    ext_rows = EPAIRS * EXT
    lanes = PAIRS * 128
    hbm_spec = pl.BlockSpec(memory_space=pltpu.HBM)
    vmem_spec = pl.BlockSpec(memory_space=pltpu.VMEM)

    def kernel(*refs):
        body(float(total_cells), n_row, n_col, *refs)

    def shards(*args):
        call = pl.pallas_call(
            kernel,
            out_shape=(pltpu.VMEM((8, 128), F32),
                       pltpu.VMEM((DEPTH, ROWS, lanes), F32),
                       pltpu.VMEM((DEPTH, ROWS, lanes), F32)),
            in_specs=[hbm_spec] * 7 + [pl.BlockSpec(memory_space=pltpu.SMEM)],
            out_specs=(pl.BlockSpec(memory_space=pltpu.VMEM),
                       pl.BlockSpec(memory_space=pltpu.VMEM), pl.BlockSpec(memory_space=pltpu.VMEM)),
            scratch_shapes=[
                vm(ROWS, lanes), vm(ROWS, lanes, dtype=BF16), vm(ROWS, lanes, dtype=BF16),
                vm(DEPTH, ROWS, lanes, dtype=BF16), vm(DEPTH, ROWS, lanes, dtype=BF16),
                vm(LAYERS, 3, 3, CH, CH), vm(LAYERS, CH),
                vm(9 * inner_rows, 128), vm(5 * ext_rows, 128),
                vm(inner_rows, 128), vm(inner_rows, 128),
                vm(2 * ext_rows, 128), vm(2 * ext_rows, 128),
                vm(3 * inner_rows, 128), vm(inner_rows, 128), vm(2 * ext_rows, 128),
                vm(3 * ext_rows, 128), vm(3 * ext_rows, 128),
                vm(2 * ext_rows, 128),
                vm(3 * inner_rows, 128), vm(inner_rows, 128),
                vm(3 * (EPAIRS + 1) * WIDE, 128),
                [vm(EXT, 128)] * 12, [vm(WIDE, 128)] * 9,
                vm(4, 2, 3, inner_rows + 2 * ROWS, 128, dtype=BF16), vm(3, 2, ext_rows, 768, dtype=BF16),
                vm(7, 768, 256, dtype=BF16),
                vm(2, 5, 1, PAIRS, 128), vm(2, 5, ROWS, 128), vm(4, 5, 1, 128),
                vm(2, 5, 1, PAIRS, 128), vm(2, 5, ROWS, 128), vm(4, 5, 1, 128),
                vm(2, 2, 3, 2, PAIRS, 128), vm(2, 2, 3, ROWS, 128), vm(2, 4, 3, 2, 128),
                vm(2, 2, 3, 2, PAIRS, 128), vm(2, 2, 3, ROWS, 128), vm(2, 4, 3, 2, 128),
                vm(ITERS, 2, 1, 128), vm(n_plane, 1, 128), vm(PLANES, 1, 128),
                vm(ITERS - 1, 2, 1, 128), vm(ITERS - 1, n_row * n_col // 2, 1, 128),
                pltpu.SemaphoreType.DMA((7,)),
                pltpu.SemaphoreType.DMA((3, 8)), pltpu.SemaphoreType.DMA((3, 8)),
                pltpu.SemaphoreType.DMA((ITERS, 2)), pltpu.SemaphoreType.DMA((ITERS, 2)),
            ],
            compiler_params=pltpu.CompilerParams(
                collective_id=0, has_side_effects=True, vmem_limit_bytes=56 * 1024 * 1024),
            name="ascent",
        )
        results = call(*args)
        return pl.pallas_call(
            store,
            out_shape=(jax.ShapeDtypeStruct((ITERS,), F32),
                       jax.ShapeDtypeStruct((DEPTH, ROWS, lanes), F32),
                       jax.ShapeDtypeStruct((DEPTH, ROWS, lanes), F32)),
            in_specs=[vmem_spec] * 3,
            out_specs=(pl.BlockSpec(memory_space=pltpu.SMEM), hbm_spec, hbm_spec),
            scratch_shapes=[pltpu.SemaphoreType.DMA((2,))],
            compiler_params=pltpu.CompilerParams(vmem_limit_bytes=1024 * 1024),
            name="store",
        )(*results)

    placed = (P("row", "col"), P("row", "col"), P("row", "col"), P(None, "row", "col"), P(None, "row", "col"),
              P(), P(), P())
    return jax.shard_map(
        shards, mesh=mesh, in_specs=placed,
        out_specs=(P(), P(None, "row", "col"), P(None, "row", "col")), check_vma=False)
```

```python
import jax
import jax.numpy as jnp
from jax import lax
from jax.experimental import pallas as pl
from jax.experimental.pallas import tpu as pltpu
from jax.sharding import PartitionSpec as P

CH = 64
LAYERS = 4
ITERS = 3
DEPTH = LAYERS - 1
EPS = 1e-06
MESH = pl.DeviceIdType.MESH
F32 = jnp.float32
BF16 = jnp.bfloat16

ROWS = 16
PAIRS = 16
EXT = 24
EPAIRS = 18
WIDE = 32
TOP = 8
PLANES = 8
MID, HALF, H1, H2, OBJ, H3, Q1, Q2, Q3 = range(9)
UP, DOWN, LEFT, RIGHT = range(4)
SIDES = ((-1, 0), (1, 0), (0, -1), (0, 1), (-1, -1), (-1, 1), (1, -1), (1, 1))


def at(start, size):
    return pl.ds(pl.multiple_of(start, 8), size)


def inner(which, pair):
    return at((which * PAIRS + pair) * ROWS, ROWS)


def slope(which, pair):
    return at((which * (EPAIRS + 1) + pair + 1) * WIDE + TOP, ROWS)


def ext(which, pair):
    return at((which * EPAIRS + pair) * EXT, EXT)


def ext_inner(which, pair):
    return pl.ds((which * EPAIRS + pair + 1) * EXT + 1, ROWS)


def softplus_sum(args):
    product = 1.0 + jnp.exp(-jnp.abs(args[0]))
    positive = jnp.maximum(args[0], 0.0)
    for arg in args[1:]:
        product = product * (1.0 + jnp.exp(-jnp.abs(arg)))
        positive = positive + jnp.maximum(arg, 0.0)
    return positive + jnp.log(product)


def split(v):
    hi = v.astype(BF16)
    return hi, (v - hi.astype(F32)).astype(BF16)


def body(total_cells, n_row, n_col, obj_h, cen_h, rad_h, low_h, upp_h, ker_h, bia_h, steps,
         bounds_ref, lam_out, mu_out,
         obj_v, cen_v, rad_v, low_v, upp_v, ker_v, bia_v,
         base, wide_in, lam, mu, lam_x, mu_x, dl, dmu, dmu_x, trans, upd, p_x, pn, tb,
         d_w, y_s, y_w, lhs_i, lhs_x, wts,
         rows_s0, cols_s0, diag_s0, rows_r0, cols_r0, diag_r0,
         rows_s, cols_s, diag_s, rows_r, cols_r, diag_r,
         pay, buf_plane, buf_line, buf_pair, buf_chip,
         load_sem, halo_send, halo_recv, sum_send, sum_recv):
    row = lax.axis_index("row")
    col = lax.axis_index("col")
    x_hi = row // PLANES
    z = row % PLANES
    place = x_hi * n_col + col

    ring = [[place_ for place_ in (at_, (at_ + 1) % size, (at_ + size - 1) % size)]
            for at_, size in ((row, n_row), (col, n_col))]

    def side_device(side):
        return (ring[0][side[0]], ring[1][side[1]])

    loads = []
    sends = []
    for n, (src, dst) in enumerate(((cen_h, cen_v), (rad_h, rad_v), (upp_h, upp_v), (obj_h, obj_v),
                                    (ker_h, ker_v), (low_h, low_v), (bia_h, bia_v))):
        copy = pltpu.make_async_copy(src, dst, load_sem.at[n])
        copy.start()
        loads.append(copy)

    barrier = pltpu.get_barrier_semaphore()
    greeted = 0
    for side in SIDES:
        if side[0] != 0:
            pl.semaphore_signal(barrier, inc=1, device_id=side_device(side), device_id_type=MESH)
            greeted += 1
    for a in range(0, n_row, PLANES):
        for b in range(n_col):
            if a or b:
                pl.semaphore_signal(barrier, inc=1, device_id=(row ^ a if a else row, col ^ b if b else col),
                                    device_id_type=MESH)
                greeted += 1
    for a in range(1, PLANES):
        pl.semaphore_signal(barrier, inc=1, device_id=(row ^ a, col), device_id_type=MESH)
        greeted += 1

    zero_tile = jnp.zeros((8, 128), F32)

    def halo_start(n, src_ref, start, step, tall, maps, deep, bufs):
        rows_src, cols_src, diag_src, rows_dst, cols_dst, diag_dst = bufs
        for m in range(maps):
            first = start + m * step
            last = first + (PAIRS - 1) * tall
            for r in range(deep):
                rows_src[UP, m, r] = src_ref[pl.ds(first + r, PAIRS, stride=tall), :]
                rows_src[DOWN, m, r] = src_ref[pl.ds(first + ROWS - deep + r, PAIRS, stride=tall), :]
            for side, at_ in ((0, first), (1, last)):
                cols_src[side, m] = src_ref[at_ : at_ + ROWS, :]
                diag_src[side, m] = src_ref[at_ : at_ + deep, :]
                diag_src[side + 2, m] = src_ref[at_ + ROWS - deep : at_ + ROWS, :]
        copies = []
        for s in (4, 5, 6, 7, 0, 1, 2, 3):
            if s < 2:
                src, dst = rows_src.at[s], rows_dst.at[s]
            elif s < 4:
                src, dst = cols_src.at[s - 2], cols_dst.at[s - 2]
            else:
                src, dst = diag_src.at[s - 4], diag_dst.at[s - 4]
            copy = pltpu.make_async_remote_copy(
                src_ref=src, dst_ref=dst, send_sem=halo_send.at[n, s], recv_sem=halo_recv.at[n, s],
                device_id=side_device(SIDES[s]), device_id_type=MESH)
            copy.start()
            copies.append(copy)
        return copies

    no_above = row == 0
    no_below = row == n_row - 1
    no_left = col == 0
    no_right = col == n_col - 1

    def halo_place(dst_ref, maps, deep, tall, top, pairs, bufs):
        _, _, _, rows_dst, cols_dst, diag_dst = bufs

        def cut(gone, v):
            return jnp.where(gone, 0.0, v)

        for m in range(maps):
            first = m * pairs * tall
            last = first + (EPAIRS - 1) * tall
            for r in range(deep):
                dst_ref[pl.ds(first + tall + top + ROWS + r, PAIRS, stride=tall), :] = cut(
                    no_below, rows_dst[0, m, r])
                dst_ref[pl.ds(first + tall + top - deep + r, PAIRS, stride=tall), :] = cut(
                    no_above, rows_dst[1, m, r])
            dst_ref[last + top : last + top + ROWS, :] = cut(no_right, cols_dst[0, m])
            dst_ref[first + top : first + top + ROWS, :] = cut(no_left, cols_dst[1, m])
            dst_ref[last + top + ROWS : last + top + ROWS + deep, :] = cut(
                jnp.logical_or(no_below, no_right), diag_dst[0, m])
            dst_ref[first + top + ROWS : first + top + ROWS + deep, :] = cut(
                jnp.logical_or(no_below, no_left), diag_dst[1, m])
            dst_ref[last + top - deep : last + top, :] = cut(
                jnp.logical_or(no_above, no_right), diag_dst[2, m])
            dst_ref[first + top - deep : first + top, :] = cut(
                jnp.logical_or(no_above, no_left), diag_dst[3, m])

    def far(d):
        lines, across = d
        z_, y_ = lines % PLANES, across // 4
        return -(min(z_, PLANES - z_) + 2 * (lines // PLANES) + min(y_, 4 - y_) + (across % 4) // 2)

    def order(row_steps, col_steps):
        steps = [(a, b) for a in row_steps for b in col_steps if a or b]
        return sorted(steps, key=far)

    pair_steps = order((0,), (0, 1))
    chip_steps = order(range(n_row), range(0, n_col, 2))
    plane_steps = order(range(0, n_row, PLANES), range(n_col))
    line_steps = order(range(PLANES), (0,))
    chip = row * (n_col // 2) + col // 2

    def stages(n):
        if n == 0:
            return ((plane_steps, buf_plane, place), (line_steps, buf_line, z))
        return ((pair_steps, buf_pair.at[n - 1], col % 2), (chip_steps, buf_chip.at[n - 1], chip))

    def exchange(n, stage, part):
        steps, buf, slot = stages(n)[stage]
        pay[n, stage] = part
        buf[slot] = part
        for a, b in steps:
            pltpu.make_async_remote_copy(
                src_ref=pay.at[n, stage], dst_ref=buf.at[slot],
                send_sem=sum_send.at[n, stage], recv_sem=sum_recv.at[n, stage],
                device_id=(row ^ a if a else row, col ^ b if b else col), device_id_type=MESH).start()

    def whole(n, stage):
        steps, buf, _ = stages(n)[stage]
        part = buf.at[0 : len(steps)]
        return pltpu.make_async_remote_copy(
            src_ref=part, dst_ref=part, send_sem=sum_send.at[n, stage], recv_sem=sum_recv.at[n, stage],
            device_id=side_device((0, 1)), device_id_type=MESH)

    def collect(n, stage):
        whole(n, stage).wait_recv()
        return jnp.sum(stages(n)[stage][1][...], axis=0)

    lane_1 = lax.broadcasted_iota(jnp.int32, (1, 128), 1)
    holds = (lane_1 < 32, jnp.logical_and(lane_1 >= 32, lane_1 < CH), lane_1 >= CH)

    def fold_to(v, width):
        step = CH
        while step >= width:
            v = v + pltpu.roll(v, step, 1)
            step //= 2
        return v

    def sum_start(n, first_row, second_row, third_row):
        exchange(n, 0, jnp.where(holds[0], fold_to(first_row, 32),
                                 jnp.where(holds[1], fold_to(second_row, 32), fold_to(third_row, CH))))

    def sum_middle(n):
        exchange(n, 1, collect(n, 0))

    def sum_end(n):
        return collect(n, 1)

    lane = lax.broadcasted_iota(jnp.int32, (EXT, 128), 1) < CH
    lane_w = lax.broadcasted_iota(jnp.int32, (WIDE, 128), 1) < CH

    def turn(x):
        return pltpu.roll(x, CH, 1)

    def window(k, u, e, before, now):
        y = y_s[u * LAYERS + k]
        y[...] = jnp.where(lane, before, now)
        for dh in range(3):
            hi, lo = split(y[dh : dh + ROWS, :])
            rows = pl.ds(pl.multiple_of(e * ROWS, ROWS), ROWS)
            lhs_i[k, 0, dh, rows, :] = hi
            lhs_i[k, 1, dh, rows, :] = lo

    def conv(slot, weight):
        size = PAIRS * ROWS
        halves = []
        for part in range(2):
            tiles = []
            for dh in range(3):
                tiles.append(lhs_i[slot, part, dh, ROWS : size + ROWS, :])
                tiles.append(lhs_i[slot, part, dh, 2 * ROWS : size + 2 * ROWS, :])
            halves.append(jnp.concatenate(tiles, axis=1))
        return product(halves[0], halves[1], weight)

    def product(hi, lo, weight):
        high = jnp.dot(hi, wts[weight], preferred_element_type=F32)
        low = jnp.dot(lo, wts[weight, :, 0:128], preferred_element_type=F32)
        return (low + high[:, 128:]) + high[:, :128]

    def rim(which, weight, scratch):
        lane_r = lane[0:ROWS]
        none = jnp.zeros((ROWS, 128), F32)
        start = which * EPAIRS * EXT
        sides = []
        for s in (0, ROWS + 1):
            x = [turn(wide_in[pl.ds(start + k * EXT + s, PAIRS, stride=EXT), :]) for k in range(3)]
            sides.append([jnp.where(lane_r, x[0], x[1]), jnp.where(lane_r, x[1], x[2])])
        left = jnp.where(lane_r, turn(wide_in[pl.ds(start + 1, ROWS), :]), none)
        right = jnp.where(lane_r, none, turn(wide_in[pl.ds(start + (EPAIRS - 1) * EXT + 1, ROWS), :]))
        for y, v in zip(scratch, (left, right)):
            y[0:8, :] = zero_tile
            y[16:24, :] = zero_tile
            y[1 : ROWS + 1, :] = v
        blocks = [sides[0] + [none] * 4, [none] * 4 + sides[1], [], []]
        for dh in range(3):
            blocks[2] += [scratch[0][dh : dh + ROWS, :], none]
            blocks[3] += [none, scratch[1][dh : dh + ROWS, :]]
        parts = [split(jnp.concatenate([b[k] for b in blocks], axis=0)) for k in range(6)]
        return product(jnp.concatenate([p[0] for p in parts], axis=1),
                       jnp.concatenate([p[1] for p in parts], axis=1), weight)

    def add_rim(dst, first, v):
        for at_, stride, k in ((0, ROWS, 0), (ROWS - 1, ROWS, 1)):
            rows = pl.ds(first + at_, PAIRS, stride=stride)
            dst[rows, :] = dst[rows, :] + v[k * ROWS : (k + 1) * ROWS]
        for pair, k in ((0, 2), (PAIRS - 1, 3)):
            rows = pl.ds(first + pair * ROWS, ROWS)
            dst[rows, :] = dst[rows, :] + v[k * ROWS : (k + 1) * ROWS]

    def windows_wide():
        def wide(m, p):
            return turn(d_w[at((m * (EPAIRS + 1) + p) * WIDE, WIDE), :])

        none = jnp.zeros((WIDE, 128), F32)
        start = []
        for m in range(DEPTH):
            r = wide(m, 0)
            start += [r, jnp.where(lane_w, none, r)]

        def step(t, carry):
            out = []
            for m in range(DEPTH):
                r0, ya = carry[2 * m], carry[2 * m + 1]
                r1, r2 = wide(m, 2 * t + 1), wide(m, 2 * t + 2)
                yb = jnp.where(lane_w, r0, r1)
                yc = jnp.where(lane_w, r1, r2)
                for i, y in enumerate((ya, yb, yc)):
                    y_w[m * 3 + i][...] = y
                for dh in range(3):
                    ys = [y_w[m * 3 + i][dh + TOP - 2 : dh + TOP - 2 + EXT, :] for i in range(3)]
                    for half in range(2):
                        hi, lo = split(jnp.concatenate([ys[half], ys[half + 1]], axis=0))
                        rows = pl.ds(pl.multiple_of(t * 2 * EXT, 16), 2 * EXT)
                        lhs_x[m, 0, rows, (dh * 2 + half) * 128 : (dh * 2 + half + 1) * 128] = hi
                        lhs_x[m, 1, rows, (dh * 2 + half) * 128 : (dh * 2 + half + 1) * 128] = lo
                out += [r2, yc]
            return tuple(out)
        lax.fori_loop(0, EPAIRS // 2, step, tuple(start))

    def conv_wide(m):
        size = EPAIRS * EXT
        high = jnp.dot(lhs_x[m, 0], wts[3 + m], preferred_element_type=F32)
        low = jnp.dot(lhs_x[m, 1], wts[3 + m, :, 0:128], preferred_element_type=F32)
        upd[at(m * size, size), :] = (low + high[:, 128:]) + high[:, :128]

    for n in range(4):
        loads[n].wait()

    def fill(j, carry):
        lanes = pl.ds(pl.multiple_of(j * 128, 128), 128)
        c = cen_v[:, lanes].astype(F32)
        r = rad_v[:, lanes].astype(F32)
        lo, hi = c - r, c + r
        vals = {MID: 0.5 * (hi + lo), HALF: 0.5 * (hi - lo), OBJ: obj_v[:, lanes]}
        for m, name in enumerate((H1, H2, H3)):
            vals[name] = 0.5 * upp_v[m, :, lanes].astype(F32)
        for name, v in vals.items():
            base[inner(name, j), :] = v
            if name <= OBJ:
                wide_in[at((name * EPAIRS + j + 1) * EXT, 8), :] = zero_tile
                wide_in[at((name * EPAIRS + j + 1) * EXT + 16, 8), :] = zero_tile
                wide_in[ext_inner(name, j), :] = v
        return carry
    lax.fori_loop(0, PAIRS, fill, 0, unroll=4)
    for m in range(5):
        for e in (0, EPAIRS - 1):
            wide_in[ext(m, e), :] = jnp.zeros((EXT, 128), F32)

    pl.semaphore_wait(barrier, greeted)
    bufs0 = (rows_s0, cols_s0, diag_s0, rows_r0, cols_r0, diag_r0)
    first_copies = halo_start(0, base, 0, PAIRS * ROWS, ROWS, 5, 1, bufs0)
    sends += first_copies

    for n in range(4, 7):
        loads[n].wait()

    def fill_low(j, carry):
        lanes = pl.ds(pl.multiple_of(j * 128, 128), 128)
        for m, name in enumerate((Q1, Q2, Q3)):
            base[inner(name, j), :] = 0.5 * low_v[m, :, lanes].astype(F32)
        return carry
    lax.fori_loop(0, PAIRS, fill_low, 0)

    bias = jnp.concatenate([bia_v[...], bia_v[...]], axis=1)
    none64 = jnp.zeros((CH, CH), F32)

    def put_weight(slot, dh, block):
        hi, lo = split(block)
        wts[slot, dh * 256 : (dh + 1) * 256, 0:128] = hi
        wts[slot, dh * 256 : (dh + 1) * 256, 128:256] = lo

    def build(k, carry):
        for dh in range(3):
            taps = [ker_v[k, 2 - dh, dw] for dw in range(3)]
            one = jnp.concatenate([jnp.concatenate([taps[2], taps[1]], axis=1),
                                   jnp.concatenate([none64, taps[2]], axis=1)], axis=0)
            two = jnp.concatenate([jnp.concatenate([taps[0], none64], axis=1),
                                   jnp.concatenate([taps[1], taps[0]], axis=1)], axis=0)
            put_weight(3 + k, dh, jnp.concatenate([one.T, two.T], axis=0))
        return carry
    lax.fori_loop(0, LAYERS, build, 0)

    def build_forward(k, carry):
        for dh in range(3):
            taps = [ker_v[k, dh, dw] for dw in range(3)]
            put_weight(k, dh, jnp.concatenate(
                [jnp.concatenate(taps + [none64], axis=0), jnp.concatenate([none64] + taps, axis=0)], axis=1))
        return carry
    lax.fori_loop(0, DEPTH, build_forward, 0)

    def clear(t, carry):
        d_w[at(t * WIDE, WIDE), :] = jnp.zeros((WIDE, 128), F32)
        return carry
    lax.fori_loop(0, DEPTH * (EPAIRS + 1), clear, 0)

    def value_terms(i, j):
        total = base[inner(OBJ, j), :] * bias[DEPTH : DEPTH + 1]
        hs = [base[inner(n, j), :] for n in (H1, H2, H3)]
        t3 = tb[inner(0, j), :]
        args = []
        if i == 0:
            args.append(-4.0 * hs[2] * t3)
        else:
            mid, half = base[inner(MID, j), :], base[inner(HALF, j), :]
            qs = [base[inner(n, j), :] for n in (Q1, Q2, Q3)]
            g0 = -trans[ext_inner(0, j), :]
            total += g0 * (mid - half)
            args.append(-4.0 * half * g0)
            lams = [lam_x[ext_inner(0, j), :], lam_x[ext_inner(1, j), :], lam[inner(0, j), :]]
            mus = [mu_x[ext_inner(0, j), :], mu_x[ext_inner(1, j), :], mu[inner(0, j), :]]
            for m in range(DEPTH):
                g = mus[m] - trans[ext_inner(m + 1, j), :] if m < 2 else mus[2] + t3
                h4 = -4.0 * hs[m]
                args += [h4 * g, h4 * (lams[m] - mus[m]), 4.0 * qs[m] * lams[m]]
                total -= lams[m] * bias[m : m + 1]
        return total - 0.5 * softplus_sum(args)

    def value_row(i):
        def step(j, acc):
            return acc + value_terms(i, j)
        acc = lax.fori_loop(0, PAIRS, step, jnp.zeros((ROWS, 128), F32))
        out = jnp.sum(acc, axis=0, keepdims=True)
        if i == 0:
            out = out - (0.5 * 0.6931471805599453 * 9 * ROWS * PAIRS)
        return out

    scale = None
    value_prev = jnp.zeros((1, 128), F32)
    totals = []
    for i in range(ITERS):
        first = i == 1

        def start_x(g, carry):
            before = list(carry)
            for u in range(3):
                e = 3 * g + u
                xs = [wide_in[ext(n, e), :] for n in (MID, H1, H2)]
                for m in range(2):
                    p_x[ext(m, e), :] = xs[m + 1]
                    dmu_x[ext(m, e), :] = xs[m + 1] - p_x[ext(m, e), :]
                xs.append(wide_in[ext(OBJ, e), :])
                for k, x in enumerate(xs):
                    now = turn(x)
                    window(k, u, e, before[k], now)
                    before[k] = now
            return tuple(before)

        def step_x(k):
            before = jnp.zeros((EXT, 128), F32)
            for e in range(EPAIRS):
                half = wide_in[ext((HALF, H1, H2)[k], e), :]
                mid = wide_in[ext(MID, e), :] if k == 0 else half
                t = scale * upd[ext(k, e), :]
                if not first:
                    t = trans[ext(k, e), :] + t
                trans[ext(k, e), :] = t
                coef = -t
                if k > 0:
                    m = k - 1
                    new_mu = scale * dmu_x[ext(m, e), :]
                    new_lam = scale * d_w[pl.ds((m * (EPAIRS + 1) + e) * WIDE + TOP - 1, EXT), :]
                    if not first:
                        new_mu = mu_x[ext(m, e), :] + new_mu
                        new_lam = lam_x[ext(m, e), :] + new_lam
                    mu_x[ext(m, e), :] = new_mu
                    lam_x[ext(m, e), :] = new_lam
                    coef = new_mu - t
                x = mid - half * jnp.tanh(2.0 * half * coef)
                if k > 0:
                    p = half - half * jnp.tanh(2.0 * half * (new_lam - new_mu))
                    p_x[ext(m, e), :] = p
                    dmu_x[ext(m, e), :] = x - p
                now = turn(x)
                window(k, e % 3, e, before, now)
                before = now

        if i == 0:
            lax.fori_loop(0, EPAIRS // 3, start_x, tuple(jnp.zeros((EXT, 128), F32) for _ in range(LAYERS)))
        else:
            step_x(0)
            step_x(1)
            if i == ITERS - 1:
                step_x(2)

        acc = jnp.zeros((ROWS, 128), F32)
        value_last = jnp.zeros((ROWS, 128), F32)
        if i == 0:
            for m in range(DEPTH):
                image = conv(m, m)
                for j in range(PAIRS):
                    dl[inner(m, j), :] = image[j * ROWS : (j + 1) * ROWS]
            image = conv(DEPTH, 3 + DEPTH)
            for j in range(PAIRS):
                tb[inner(0, j), :] = image[j * ROWS : (j + 1) * ROWS]
            for copy in first_copies:
                copy.wait_recv()
            halo_place(wide_in, 5, 1, EXT, 1, EPAIRS, bufs0)
            add_rim(tb, 0, rim(OBJ, 3 + DEPTH, y_s[0:2]))
            for m in range(DEPTH):
                add_rim(dl, m * PAIRS * ROWS, rim((MID, H1, H2)[m], m, y_s[2 * m + 2 : 2 * m + 4]))
            for j in range(PAIRS):
                for m in range(DEPTH):
                    h = base[inner(H1 + m if m < 2 else H3, j), :]
                    p = h if m == 2 else p_x[ext_inner(m, j), :]
                    if m == 2:
                        v = (h - h * jnp.tanh(2.0 * h * tb[inner(0, j), :])) - p
                        dmu[inner(0, j), :] = v
                    else:
                        v = dmu_x[ext_inner(m, j), :]
                    acc = acc + v * v
                    v = (p - base[inner(Q1 + m, j), :] - bias[m : m + 1]) - dl[inner(m, j), :]
                    d_w[slope(m, j), :] = v
                    acc = acc + v * v
        else:
            for m in range(DEPTH):
                rest = []
                for j in range(PAIRS):
                    h = base[inner(H1 + m if m < 2 else H3, j), :]
                    q = base[inner(Q1 + m, j), :]
                    if m == 2:
                        new_mu = scale * dmu[inner(0, j), :]
                        v_lam = scale * d_w[slope(2, j), :]
                        if not first:
                            new_mu = mu[inner(0, j), :] + new_mu
                            v_lam = lam[inner(0, j), :] + v_lam
                        mu[inner(0, j), :] = new_mu
                        lam[inner(0, j), :] = v_lam
                        p = h - h * jnp.tanh(2.0 * h * (v_lam - new_mu))
                        t3 = new_mu + tb[inner(0, j), :]
                        v = (h - h * jnp.tanh(2.0 * h * t3)) - p
                        dmu[inner(0, j), :] = v
                    else:
                        p = p_x[ext_inner(m, j), :]
                        v_lam = lam_x[ext_inner(m, j), :]
                        v = dmu_x[ext_inner(m, j), :]
                    acc = acc + v * v
                    if i == ITERS - 1:
                        if m == 2:
                            v_mu, coef = new_mu, t3
                        else:
                            v_mu = mu_x[ext_inner(m, j), :]
                            coef = v_mu - trans[ext_inner(m + 1, j), :]
                        args = [-4.0 * h * coef, -4.0 * h * (v_lam - v_mu), 4.0 * q * v_lam]
                        part = -v_lam * bias[m : m + 1]
                        if m == 0:
                            half = base[inner(HALF, j), :]
                            coef = -trans[ext_inner(0, j), :]
                            args.append(-4.0 * half * coef)
                            part += coef * (base[inner(MID, j), :] - half)
                            part += base[inner(OBJ, j), :] * bias[DEPTH : DEPTH + 1]
                        value_last = value_last + (part - 0.5 * softplus_sum(args))
                    n = q + q * jnp.tanh(2.0 * q * v_lam)
                    rest.append(p - n - bias[m : m + 1])
                image = conv(m, m)
                for j in range(PAIRS):
                    v = rest[j] - image[j * ROWS : (j + 1) * ROWS]
                    d_w[slope(m, j), :] = v
                    acc = acc + v * v
                if m == 0 and i < ITERS - 1:
                    step_x(2)
        sum_start(i, *[jnp.sum(v, axis=0, keepdims=True) for v in (acc, value_last)], value_prev)

        copies = []
        if i < ITERS - 1:
            bufs = tuple(ref.at[i] for ref in (rows_s, cols_s, diag_s, rows_r, cols_r, diag_r))
            copies = halo_start(1 + i, d_w, WIDE + TOP, (EPAIRS + 1) * WIDE, WIDE, DEPTH, 2, bufs)
            sends += copies
        if i == 0:
            value_prev = value_row(i)
        sum_middle(i)
        if 0 < i < ITERS - 1:
            value_prev = value_row(i)
        if i < ITERS - 1:
            for copy in copies:
                copy.wait_recv()
            halo_place(d_w, DEPTH, 2, WIDE, TOP, EPAIRS + 1, bufs)
            windows_wide()
            for m in range(DEPTH):
                conv_wide(m)
        if i == ITERS - 1:
            for copy in sends:
                copy.wait_send()
            for n in range(ITERS):
                for stage in range(2):
                    whole(n, stage).wait_send()
        both = sum_end(i)
        squares = jnp.sum(jnp.where(holds[0], both, 0.0), axis=1, keepdims=True)
        scale = steps[i] / jnp.sqrt(squares / (2 * DEPTH * total_cells) + EPS)
        scale = jnp.broadcast_to(scale, (1, 128))
        totals.append(both)

    for j in range(PAIRS):
        lanes = pl.ds(j * 128, 128)
        for m in range(2):
            lam_out[m, :, lanes] = lam_x[ext_inner(m, j), :] + scale * d_w[slope(m, j), :]
            mu_out[m, :, lanes] = mu_x[ext_inner(m, j), :] + scale * dmu_x[ext_inner(m, j), :]
        lam_out[2, :, lanes] = lam[inner(0, j), :] + scale * d_w[slope(2, j), :]
        mu_out[2, :, lanes] = mu[inner(0, j), :] + scale * dmu[inner(0, j), :]
    for i in range(ITERS):
        last = i == ITERS - 1
        mean = jnp.sum(jnp.where(holds[1 if last else 2], totals[i if last else i + 1], 0.0), axis=1, keepdims=True)
        bounds_ref[i : i + 1, :] = jnp.broadcast_to(mean / total_cells, (1, 128))


def store(bounds_v, lam_v, mu_v, bounds_out, lam_out, mu_out, sem):
    copies = [pltpu.make_async_copy(lam_v, lam_out, sem.at[0]), pltpu.make_async_copy(mu_v, mu_out, sem.at[1])]
    for copy in copies:
        copy.start()
    for i in range(ITERS):
        bounds_out[i] = bounds_v[i, 0]
    for copy in copies:
        copy.wait()


def solution(mesh):
    n_row, n_col = mesh.shape["row"], mesh.shape["col"]
    n_plane = (n_row // PLANES) * n_col
    total_cells = n_row * n_col * ROWS * PAIRS * 128

    def vm(*shape, dtype=F32):
        return pltpu.VMEM(shape, dtype)

    inner_rows = PAIRS * ROWS
    ext_rows = EPAIRS * EXT
    lanes = PAIRS * 128
    hbm_spec = pl.BlockSpec(memory_space=pltpu.HBM)
    vmem_spec = pl.BlockSpec(memory_space=pltpu.VMEM)

    def kernel(*refs):
        body(float(total_cells), n_row, n_col, *refs)

    def shards(*args):
        call = pl.pallas_call(
            kernel,
            out_shape=(pltpu.VMEM((8, 128), F32),
                       pltpu.VMEM((DEPTH, ROWS, lanes), F32),
                       pltpu.VMEM((DEPTH, ROWS, lanes), F32)),
            in_specs=[hbm_spec] * 7 + [pl.BlockSpec(memory_space=pltpu.SMEM)],
            out_specs=(pl.BlockSpec(memory_space=pltpu.VMEM),
                       pl.BlockSpec(memory_space=pltpu.VMEM), pl.BlockSpec(memory_space=pltpu.VMEM)),
            scratch_shapes=[
                vm(ROWS, lanes), vm(ROWS, lanes, dtype=BF16), vm(ROWS, lanes, dtype=BF16),
                vm(DEPTH, ROWS, lanes, dtype=BF16), vm(DEPTH, ROWS, lanes, dtype=BF16),
                vm(LAYERS, 3, 3, CH, CH), vm(LAYERS, CH),
                vm(9 * inner_rows, 128), vm(5 * ext_rows, 128),
                vm(inner_rows, 128), vm(inner_rows, 128),
                vm(2 * ext_rows, 128), vm(2 * ext_rows, 128),
                vm(3 * inner_rows, 128), vm(inner_rows, 128), vm(2 * ext_rows, 128),
                vm(3 * ext_rows, 128), vm(3 * ext_rows, 128),
                vm(2 * ext_rows, 128),
                vm(3 * inner_rows, 128), vm(inner_rows, 128),
                vm(3 * (EPAIRS + 1) * WIDE, 128),
                [vm(EXT, 128)] * 12, [vm(WIDE, 128)] * 9,
                vm(4, 2, 3, inner_rows + 2 * ROWS, 128, dtype=BF16), vm(3, 2, ext_rows, 768, dtype=BF16),
                vm(7, 768, 256, dtype=BF16),
                vm(2, 5, 1, PAIRS, 128), vm(2, 5, ROWS, 128), vm(4, 5, 1, 128),
                vm(2, 5, 1, PAIRS, 128), vm(2, 5, ROWS, 128), vm(4, 5, 1, 128),
                vm(2, 2, 3, 2, PAIRS, 128), vm(2, 2, 3, ROWS, 128), vm(2, 4, 3, 2, 128),
                vm(2, 2, 3, 2, PAIRS, 128), vm(2, 2, 3, ROWS, 128), vm(2, 4, 3, 2, 128),
                vm(ITERS, 2, 1, 128), vm(n_plane, 1, 128), vm(PLANES, 1, 128),
                vm(ITERS - 1, 2, 1, 128), vm(ITERS - 1, n_row * n_col // 2, 1, 128),
                pltpu.SemaphoreType.DMA((7,)),
                pltpu.SemaphoreType.DMA((3, 8)), pltpu.SemaphoreType.DMA((3, 8)),
                pltpu.SemaphoreType.DMA((ITERS, 2)), pltpu.SemaphoreType.DMA((ITERS, 2)),
            ],
            compiler_params=pltpu.CompilerParams(
                collective_id=0, has_side_effects=True, vmem_limit_bytes=56 * 1024 * 1024),
            name="ascent",
        )
        results = call(*args)
        return pl.pallas_call(
            store,
            out_shape=(jax.ShapeDtypeStruct((ITERS,), F32),
                       jax.ShapeDtypeStruct((DEPTH, ROWS, lanes), F32),
                       jax.ShapeDtypeStruct((DEPTH, ROWS, lanes), F32)),
            in_specs=[vmem_spec] * 3,
            out_specs=(pl.BlockSpec(memory_space=pltpu.SMEM), hbm_spec, hbm_spec),
            scratch_shapes=[pltpu.SemaphoreType.DMA((2,))],
            compiler_params=pltpu.CompilerParams(vmem_limit_bytes=1024 * 1024),
            name="store",
        )(*results)

    placed = (P("row", "col"), P("row", "col"), P("row", "col"), P(None, "row", "col"), P(None, "row", "col"),
              P(), P(), P())
    return jax.shard_map(
        shards, mesh=mesh, in_specs=placed,
        out_specs=(P(), P(None, "row", "col"), P(None, "row", "col")), check_vma=False)
```
